32 devices in a mesh: ctx: 8 (over z, y), fsdp: 4 (over x, core).
Axes of the slice: x: 2, y: 2, z: 4, core: 2. Of those that a mesh axis runs over, the one named last changes fastest.
Arguments:
- tokens: bfloat16 [3, 4, 2048, 1024], P(None, 'fsdp', 'ctx'), may hold values from -6 to 6
- w_router: float32 [1024], replicated, may hold values from -0.1875 to 0.1875
- gain_attn: float32 [1024], replicated, may hold values from 0.1 to 1.9
- w_qkv: bfloat16 [1024, 3072], P('fsdp'), may hold values from -0.1875 to 0.1875
- w_out: bfloat16 [1024, 1024], P('fsdp'), may hold values from -1 to 1
- gain_mlp: float32 [1024], replicated, may hold values from 0.1 to 1.9
- w_up: bfloat16 [1024, 4096], P('fsdp'), may hold values from -0.1875 to 0.1875
- w_down: bfloat16 [4096, 1024], P('fsdp'), may hold values from -0.09375 to 0.09375
- routed: int32 [3, 4, 256], P(None, 'fsdp', 'ctx'), may hold values from 0 to 2047, as said below
- deal: int32 [16], replicated, may hold values from 0 to 15, as said below
- cotangent: bfloat16 [3, 4, 2048, 1024], P(None, 'fsdp', 'ctx'), may hold values from -6 to 6
Outputs:
- output: bfloat16 [3, 4, 2048, 1024], P(None, 'fsdp', 'ctx')
- input_grad: bfloat16 [3, 4, 2048, 1024], P(None, 'fsdp', 'ctx')
- grad_router: float32 [1024], P(('ctx', 'fsdp'))
- grad_gain_attn: float32 [1024], P(('ctx', 'fsdp'))
- grad_qkv: float32 [1024, 3072], P(('ctx', 'fsdp'))
- grad_out: float32 [1024, 1024], P(('ctx', 'fsdp'))
- grad_gain_mlp: float32 [1024], P(('ctx', 'fsdp'))
- grad_up: float32 [1024, 4096], P(('ctx', 'fsdp'))
- grad_down: float32 [4096, 1024], P(('ctx', 'fsdp'))
The draws below stay inside these ranges and needn't reach their ends.
Inputs may be any that keep to these rules, and one draw needn't show every extreme that they name: `routed`: for each micro-batch and sequence the indices rise; entries j * 32 to (j + 1) * 32 - 1 are distinct stored rows among j * 256 to (j + 1) * 256 - 1, and include j * 256 and (j + 1) * 256 - 1. `deal`: each initial span appears once; stored spans 2 j and 2 j + 1 hold initial spans c and 15 - c.
All inputs are finite; a program needn't handle non-finite values.
Results may differ from the reference program's by a relative error of at most 0.012.
Values may be sent and summed in bfloat16 or wider, within the bound.
No kernel may reach another device: no remote copies, remote signals or barrier semaphores. Data moves between devices by JAX's collectives and lax.ppermute only.
A program may use at most 256 MiB of HBM per device.

```python
import math
import jax
import jax.numpy as jnp
from jax import lax

D = 1024
HEADS = 16
HEAD_DIM = 64
FF = 4096
TOK_DEV = 256
MICRO = 3
BLOCK = 256
R_DEV = 32
NCHUNK = 16
LENGTH = 2048
R_TOT = 256
SEQS = 4


def draw_routed(key, part):
    devices = R_TOT // R_DEV
    scores = jax.random.randint(key, (MICRO, SEQS, devices, TOK_DEV), 0, 2 ** 31 // TOK_DEV, dtype=jnp.int32)
    positions = jnp.arange(TOK_DEV, dtype=jnp.int32)
    scores = scores * TOK_DEV + positions
    ends = (positions == 0) | (positions == TOK_DEV - 1)
    scores = jnp.where(ends, positions // TOK_DEV - 2 + (positions == TOK_DEV - 1).astype(jnp.int32), scores)
    ranking = jnp.argsort(scores, axis=-1)[..., :R_DEV].astype(jnp.int32)
    picked = jnp.sort(ranking, axis=-1) + (jnp.arange(devices, dtype=jnp.int32) * TOK_DEV)[:, None]
    return picked.reshape(MICRO, SEQS, R_TOT).astype(jnp.int32)


def draw_deal(key, part):
    pairs = NCHUNK // 2
    first = jax.random.permutation(key, pairs).astype(jnp.int32)
    second = NCHUNK - 1 - first
    return jnp.stack([first, second], axis=1).reshape(NCHUNK).astype(jnp.int32)


def level_of(stream_key, shape, shards, least, high):
    level, own = 1.0, jax.random.fold_in(stream_key, 6)
    for position, shards_of in shards:
        heights = jnp.exp(jax.random.uniform(jax.random.fold_in(own, position), (shards_of,), jnp.float32, least / len(shards), high / len(shards)))
        level = level * jnp.repeat(heights, shape[position] // shards_of).reshape([-1 if axis == position else 1 for axis in range(len(shape))])
    return level


def bell_draw(own_key, extent, deviation, bound, split=(), kind=jnp.bfloat16):
    drawn = deviation * jax.random.normal(own_key, extent, jnp.float32)
    if split:
        drawn = drawn * level_of(own_key, extent, split, -0.22, 0.18)
    return jnp.clip(drawn, -bound, bound).astype(kind)


def setup_inputs(seed: int = 0) -> dict:
    key_list = jax.random.split(jax.random.key(seed), 12)
    return {
        "tokens": bell_draw(key_list[0], (MICRO, SEQS, LENGTH, D), 1.0, 6.0, ((1, 4), (2, 8))),
        "w_router": bell_draw(key_list[1], (D,), D ** -0.5, 0.1875, (), jnp.float32),
        "gain_attn": jnp.clip(1.0 + 0.18 * jax.random.normal(key_list[2], (D,), jnp.float32), 0.1, 1.9),
        "w_qkv": bell_draw(key_list[3], (D, 3 * D), D ** -0.5, 0.1875, ((0, 4),)),
        "w_out": bell_draw(key_list[4], (D, D), (max(1, D * 8 // R_TOT)) ** -0.5, 1.0, ((0, 4),)),
        "gain_mlp": jnp.clip(1.0 + 0.18 * jax.random.normal(key_list[5], (D,), jnp.float32), 0.1, 1.9),
        "w_up": bell_draw(key_list[6], (D, FF), D ** -0.5, 0.1875, ((0, 4),)),
        "w_down": bell_draw(key_list[7], (FF, D), FF ** -0.5, 0.09375, ((0, 4),)),
        "routed": draw_routed(jax.random.fold_in(key_list[11], 71), 0),
        "deal": draw_deal(jax.random.fold_in(key_list[11], 71), 0),
        "cotangent": bell_draw(key_list[10], (MICRO, SEQS, LENGTH, D), 1.0, 6.0, ((1, 4), (2, 8))),
    }


EPSILON = 1e-06
MASKED = -1e+30
HIGHEST = lax.Precision.HIGHEST

@jax.custom_vjp
def low(v):
    return lax.optimization_barrier(v.astype(jnp.bfloat16)).astype(jnp.float32)

@jax.custom_vjp
def low_back(v):
    return v

def low_keep(v):
    return (low(v), None)

def low_pass(kept, grad):
    return (grad,)

def back_keep(v):
    return (v, None)

def back_low(kept, grad):
    return (low(grad),)
low.defvjp(low_keep, low_pass)
low_back.defvjp(back_keep, back_low)

def dense(left, right):
    return jnp.dot(left, right, precision=HIGHEST)

def rms_norm(values, gain):
    factor = lax.rsqrt(lax.optimization_barrier(jnp.mean(values * values, axis=-1, keepdims=True)) + EPSILON)
    return values * factor * gain

def attend_block(query_block, query_places, keys, values, key_places):
    scores = jnp.einsum('qhd,khd->hqk', query_block, keys, precision=HIGHEST) * HEAD_DIM ** (-0.5)
    scores = jnp.where(key_places[None, None, :] <= query_places[None, :, None], scores, MASKED)
    scores = low_back(scores)
    probs = low(jax.nn.softmax(scores, axis=-1))
    return jnp.einsum('hqk,khd->qhd', probs, values, precision=HIGHEST)

def layer(sequence, places, index, w_router, gain_attn, w_qkv, w_out, gain_mlp, w_up, w_down):
    rows = sequence[index]
    count = rows.shape[0]
    gate = jax.nn.sigmoid(dense(rows, w_router))
    norm1 = low(rms_norm(rows, gain_attn))
    qkv = low(low_back(dense(norm1, w_qkv)))
    queries = qkv[:, :D].reshape(count, HEADS, HEAD_DIM)
    keys = qkv[:, D:2 * D].reshape(count, HEADS, HEAD_DIM)
    values = qkv[:, 2 * D:].reshape(count, HEADS, HEAD_DIM)
    size = math.gcd(512, count)
    query_blocks = queries.reshape(count // size, size, HEADS, HEAD_DIM)
    place_blocks = places.reshape(count // size, size)

    def one_block(pair):
        return attend_block(pair[0], pair[1], keys, values, places)
    attended = lax.map(jax.checkpoint(one_block), (query_blocks, place_blocks)).reshape(count, D)
    attended = low(low_back(attended))
    attn = low_back(dense(attended, w_out))
    mid = rows + attn
    norm2 = low(rms_norm(mid, gain_mlp))
    hidden = low_back(dense(norm2, w_up))
    act = low(jax.nn.gelu(hidden, approximate=False))
    mlp = low_back(dense(act, w_down))
    result = rows + gate[:, None] * (attn + mlp)
    return sequence.at[index].set(result)

def reference(tokens, w_router, gain_attn, w_qkv, w_out, gain_mlp, w_up, w_down, routed, deal, cotangent):
    total = MICRO * SEQS
    flat_tokens = tokens.reshape(total, LENGTH, D)
    flat_cot = cotangent.reshape(total, LENGTH, D)
    flat_index = routed.reshape(total, R_TOT).astype(jnp.int32)
    span = LENGTH // NCHUNK
    anchor = deal[flat_index // span].astype(jnp.int32) * span + flat_index % span
    flat_places = (anchor // BLOCK).astype(jnp.int32)
    weights = (w_router.astype(jnp.float32), gain_attn.astype(jnp.float32), w_qkv.astype(jnp.float32), w_out.astype(jnp.float32), gain_mlp.astype(jnp.float32), w_up.astype(jnp.float32), w_down.astype(jnp.float32))

    def one_sequence(totals, inputs):
        seq_tokens, seq_cot, index, places = inputs

        def layer_of(sequence, *params):
            return layer(sequence, places, index, *params)
        result, pullback = jax.vjp(layer_of, seq_tokens.astype(jnp.float32), *weights)
        grads = pullback(seq_cot.astype(jnp.float32))
        totals = tuple((acc + grad for acc, grad in zip(totals, grads[1:])))
        return (totals, (result.astype(jnp.bfloat16), grads[0].astype(jnp.bfloat16)))
    start = tuple((jnp.zeros_like(weight) for weight in weights))
    totals, stacked = lax.scan(one_sequence, start, (flat_tokens, flat_cot, flat_index, flat_places))
    output = stacked[0].reshape(MICRO, SEQS, LENGTH, D)
    input_grad = stacked[1].reshape(MICRO, SEQS, LENGTH, D)
    return (output, input_grad, totals[0], totals[1], totals[2], totals[3], totals[4], totals[5], totals[6])
```

```python
import math

import jax
import jax.numpy as jnp
from jax import lax
from jax.experimental import pallas as pl
from jax.experimental.pallas import tpu as pltpu
from jax.sharding import PartitionSpec as P

HEADS = 16
HEAD_DIM = 64
BLOCK = 256


EPSILON = 1e-06
MASKED = -1e30
HIGHEST = lax.Precision.HIGHEST
BF16, F32 = jnp.bfloat16, jnp.float32
VMEM_LIMIT = 56 * 2**20


def rms_norm(values, gain):
    factor = lax.rsqrt(jnp.mean(values * values, axis=-1, keepdims=True) + EPSILON)
    return values * factor * gain


def exact_gelu(values):
    return jax.nn.gelu(values, approximate=False)


def fetch(w_qkv, w_out, w_up, w_down):
    return (
        lax.all_gather(w_qkv, "fsdp", axis=0, tiled=True),
        lax.all_gather(w_out, "fsdp", axis=0, tiled=True),
        lax.all_gather(w_up, "fsdp", axis=0, tiled=True),
        lax.all_gather(w_down, "fsdp", axis=0, tiled=True),
    )


def lookup(table, index):
    hits = index[..., None] == jnp.arange(table.shape[0], dtype=jnp.int32)
    return jnp.sum(jnp.where(hits, table, 0), axis=-1)


def outer_sum(left, right):
    return lax.dot_general(
        left, right, (((0,), (0,)), ((), ())), preferred_element_type=jnp.float32
    )


def gather_rows(pieces, column):
    return jnp.concatenate([piece[column] for piece in pieces], axis=0)


def shards(
    tokens, w_router, gain_attn, w_qkv, w_out, gain_mlp, w_up, w_down, routed, deal, cotangent
):
    micros, tok_dev, width = (tokens.shape[0], tokens.shape[2], tokens.shape[3])
    span = tok_dev // 2
    rank = lax.axis_index("ctx")
    storage = routed[:, 0, :]
    local_rows = storage - rank * tok_dev
    anchor = lookup(deal, storage // span) * span + storage % span
    own_blocks = anchor // BLOCK
    all_blocks = lax.all_gather(own_blocks, "ctx", axis=1, tiled=True)
    factor = HEAD_DIM ** (-0.5)
    outputs, in_grads, kept = ([], [], [])
    sum_router = jnp.zeros((width,), jnp.float32)
    sum_gain_attn = jnp.zeros((width,), jnp.float32)
    sum_gain_mlp = jnp.zeros((width,), jnp.float32)
    for micro in range(micros):
        full_qkv, full_out, full_up, full_down = fetch(w_qkv, w_out, w_up, w_down)
        resid = tokens[micro, 0].astype(jnp.float32)
        grad_in = cotangent[micro, 0].astype(jnp.float32)
        rows_index = local_rows[micro]
        rows = jnp.take(resid, rows_index, axis=0)
        count = rows.shape[0]
        gate = jax.nn.sigmoid(jnp.dot(rows, w_router, precision=HIGHEST))
        norm1, norm1_back = jax.vjp(rms_norm, rows, gain_attn)
        norm1_low = norm1.astype(jnp.bfloat16)
        qkv = jnp.dot(norm1_low, full_qkv, preferred_element_type=jnp.float32).astype(jnp.bfloat16)
        queries = qkv[:, :width]
        keys_local = qkv[:, width : 2 * width]
        values_local = qkv[:, 2 * width :]
        keys_all, values_all = (
            lax.all_gather(keys_local, "ctx", axis=0, tiled=True),
            lax.all_gather(values_local, "ctx", axis=0, tiled=True),
        )
        total = keys_all.shape[0]
        query_heads = queries.reshape(count, HEADS, HEAD_DIM)
        key_heads = keys_all.reshape(total, HEADS, HEAD_DIM)
        value_heads = values_all.reshape(total, HEADS, HEAD_DIM)
        visible = all_blocks[micro][None, :] <= own_blocks[micro][:, None]
        scores = (
            jnp.einsum("qhd,khd->hqk", query_heads, key_heads, preferred_element_type=jnp.float32)
            * factor
        )
        scores = jnp.where(visible[None], scores, MASKED)
        probs = jax.nn.softmax(scores, axis=-1)
        probs_low = probs.astype(jnp.bfloat16)
        attended = jnp.einsum(
            "hqk,khd->qhd", probs_low, value_heads, preferred_element_type=jnp.float32
        )
        attended_low = attended.reshape(count, width).astype(jnp.bfloat16)
        attn = jnp.dot(attended_low, full_out, preferred_element_type=jnp.float32)
        mid = rows + attn
        norm2, norm2_back = jax.vjp(rms_norm, mid, gain_mlp)
        norm2_low = norm2.astype(jnp.bfloat16)
        hidden = jnp.dot(norm2_low, full_up, preferred_element_type=jnp.float32)
        act, gelu_back = jax.vjp(exact_gelu, hidden)
        act_low = act.astype(jnp.bfloat16)
        mlp = jnp.dot(act_low, full_down, preferred_element_type=jnp.float32)
        branch = attn + mlp
        outputs.append(resid.at[rows_index].set(rows + gate[:, None] * branch).astype(jnp.bfloat16))
        cot_rows = jnp.take(grad_in, rows_index, axis=0)
        d_branch = gate[:, None] * cot_rows
        d_mlp = d_branch.astype(jnp.bfloat16)
        d_logit = jnp.sum(cot_rows * branch, axis=-1) * gate * (1.0 - gate)
        d_act = jnp.dot(d_mlp, full_down.T, preferred_element_type=jnp.float32)
        d_hidden = gelu_back(d_act)[0].astype(jnp.bfloat16)
        d_norm2 = jnp.dot(d_hidden, full_up.T, preferred_element_type=jnp.float32)
        d_mid, d_gain2 = norm2_back(d_norm2)
        d_attn = (d_branch + d_mid).astype(jnp.bfloat16)
        d_attended = jnp.dot(d_attn, full_out.T, preferred_element_type=jnp.float32).astype(
            jnp.bfloat16
        )
        d_heads = d_attended.reshape(count, HEADS, HEAD_DIM)
        d_probs = jnp.einsum(
            "qhd,khd->hqk", d_heads, value_heads, preferred_element_type=jnp.float32
        )
        weighted = jnp.sum(probs * d_probs, axis=-1, keepdims=True)
        d_scores = (probs * (d_probs - weighted)).astype(jnp.bfloat16)
        d_query = (
            jnp.einsum("hqk,khd->qhd", d_scores, key_heads, preferred_element_type=jnp.float32)
            * factor
        )
        d_key_part = (
            jnp.einsum("hqk,qhd->khd", d_scores, query_heads, preferred_element_type=jnp.float32)
            * factor
        )
        d_value_part = jnp.einsum(
            "hqk,qhd->khd", probs_low, d_heads, preferred_element_type=jnp.float32
        )
        d_keys, d_values = (
            lax.psum_scatter(
                d_key_part.reshape(total, width), "ctx", scatter_dimension=0, tiled=True
            ),
            lax.psum_scatter(
                d_value_part.reshape(total, width), "ctx", scatter_dimension=0, tiled=True
            ),
        )
        d_qkv = jnp.concatenate([d_query.reshape(count, width), d_keys, d_values], axis=1).astype(
            jnp.bfloat16
        )
        d_norm1 = jnp.dot(d_qkv, full_qkv.T, preferred_element_type=jnp.float32)
        d_rows_norm, d_gain1 = norm1_back(d_norm1)
        d_rows = cot_rows + d_mid + d_rows_norm + d_logit[:, None] * w_router
        in_grads.append(grad_in.at[rows_index].set(d_rows).astype(jnp.bfloat16))
        sum_router = sum_router + jnp.dot(d_logit, rows, precision=HIGHEST)
        sum_gain_attn = sum_gain_attn + d_gain1
        sum_gain_mlp = sum_gain_mlp + d_gain2
        kept.append((norm1_low, d_qkv, attended_low, d_attn, norm2_low, d_hidden, act_low, d_mlp))
    stacked_rows = tuple((gather_rows(kept, column) for column in range(8)))
    grad_qkv = outer_sum(stacked_rows[0], stacked_rows[1])
    grad_out = outer_sum(stacked_rows[2], stacked_rows[3])
    grad_up = outer_sum(stacked_rows[4], stacked_rows[5])
    grad_down = outer_sum(stacked_rows[6], stacked_rows[7])
    summed = (
        lax.psum_scatter(sum_router, ("ctx", "fsdp"), scatter_dimension=0, tiled=True),
        lax.psum_scatter(sum_gain_attn, ("ctx", "fsdp"), scatter_dimension=0, tiled=True),
        lax.psum_scatter(grad_qkv, ("ctx", "fsdp"), scatter_dimension=0, tiled=True),
        lax.psum_scatter(grad_out, ("ctx", "fsdp"), scatter_dimension=0, tiled=True),
        lax.psum_scatter(sum_gain_mlp, ("ctx", "fsdp"), scatter_dimension=0, tiled=True),
        lax.psum_scatter(grad_up, ("ctx", "fsdp"), scatter_dimension=0, tiled=True),
        lax.psum_scatter(grad_down, ("ctx", "fsdp"), scatter_dimension=0, tiled=True),
    )
    output = jnp.stack(outputs)[:, None]
    input_grad = jnp.stack(in_grads)[:, None]
    return (
        output,
        input_grad,
        summed[0],
        summed[1],
        summed[2],
        summed[3],
        summed[4],
        summed[5],
        summed[6],
    )


def vmem_call(kernel, outs, smem, args, scratch=(), flops=0, name=None):
    total = sum(a.size * a.dtype.itemsize for a in (*args, *outs))
    return pl.pallas_call(
        kernel,
        out_shape=tuple(outs),
        in_specs=[pl.BlockSpec(memory_space=pltpu.SMEM)] * len(smem)
        + [pl.BlockSpec(memory_space=pltpu.VMEM)] * len(args),
        out_specs=tuple(pl.BlockSpec(memory_space=pltpu.VMEM) for _ in outs),
        scratch_shapes=list(scratch),
        compiler_params=pltpu.CompilerParams(vmem_limit_bytes=VMEM_LIMIT),
        cost_estimate=pl.CostEstimate(flops=flops, bytes_accessed=total, transcendentals=0),
        name=name,
    )(*smem, *args)


def sds(shape, dtype):
    return jax.ShapeDtypeStruct(shape, dtype)


def mm(left, right):
    return jnp.dot(left, right, preferred_element_type=F32)


def mm_t(left, right):
    return lax.dot_general(left, right, (((1,), (1,)), ((), ())), preferred_element_type=F32)


def t_mm(left, right):
    return lax.dot_general(left, right, (((0,), (0,)), ((), ())), preferred_element_type=F32)


def exchange(x, axis, size, mask):
    return lax.ppermute(x, axis, [(i, i ^ mask) for i in range(size)])


def gather_kernel(deal, storage, base, tokens, cot, w_router, rowsx, cots, d_mlp, gate_out):
    micros, tok_dev, width = tokens.shape
    count = cots.shape[0]
    per = count // micros
    span = tok_dev // 2
    index = storage[...]
    local = index - base[0]
    lanes = lax.broadcasted_iota(jnp.int32, (tok_dev, index.shape[1]), 1)
    hit = lax.broadcasted_iota(jnp.int32, (tok_dev, index.shape[1]), 0) == local
    rows = jnp.zeros((index.shape[1], width), F32)
    cot_rows = jnp.zeros((index.shape[1], width), F32)
    for micro in range(micros):
        mine = (lanes >= micro * per) & (lanes < (micro + 1) * per)
        pick = jnp.where(hit & mine, 1.0, 0.0).astype(BF16)
        rows = rows + t_mm(pick, tokens[micro])
        cot_rows = cot_rows + t_mm(pick, cot[micro])
    rows, cot_rows = rows[:count], cot_rows[:count]
    chunk = index // span
    anchor = jnp.zeros_like(index)
    for entry in range(deal.shape[0]):
        anchor = jnp.where(chunk == entry, deal[entry], anchor)
    place = (anchor * span + index % span) // BLOCK
    rowsx[:count] = rows.astype(BF16)
    rowsx[count:] = jnp.zeros((rowsx.shape[0] - count, width), BF16)
    rowsx[count : count + 8, : index.shape[1]] = jnp.broadcast_to(
        place.astype(F32), (8, index.shape[1])
    ).astype(BF16)
    cots[...] = cot_rows.astype(BF16)
    gate = jax.nn.sigmoid(jnp.sum(rows * w_router[...], axis=1, keepdims=True))
    d_mlp[...] = (gate * cot_rows).astype(BF16)
    gate_out[...] = gate


def slice_qkv_kernel(ids, w_qkv, *outs):
    width = w_qkv.shape[1] // 3
    part = width // 4
    for k, out in enumerate(outs):
        peer = ids[1] ^ k
        for j in range(2):
            for b in range(3):
                start = pl.multiple_of(peer * part + (b * width + j * 128), 128)
                out[:, (3 * j + b) * 128 : (3 * j + b + 1) * 128] = w_qkv[:, pl.ds(start, 128)]


def slice_up_kernel(ids, w_up, *outs):
    part = w_up.shape[1] // 4
    for k, out in enumerate(outs):
        out[...] = w_up[:, pl.ds(pl.multiple_of((ids[1] ^ k) * part, part), part)]


def rms_factor(values):
    return lax.rsqrt(jnp.mean(values * values, axis=-1, keepdims=True) + EPSILON)


def qkv_kernel(ids, gain, r0, r1, r2, r3, w0, w1, w2, w3, *rest):
    outs, (w_full, norm1, raw) = rest[:8], rest[8:]
    c, f = ids[0], ids[1]
    part = w0.shape[0]
    count = norm1.shape[1]
    for k, w in enumerate((w0, w1, w2, w3)):
        w_full[pl.ds(pl.multiple_of((f ^ k) * part, part), part), :] = w[...]
    for k, r in enumerate((r0, r1, r2, r3)):
        rows = r[:count].astype(F32)
        norm1[f ^ k] = (rows * rms_factor(rows) * gain[...]).astype(BF16)
    for s in range(4):
        raw[s] = mm(norm1[s], w_full[...]).astype(BF16)
    places = (r0, r1, r2, r3)
    for k in range(8):
        target = c ^ k
        s, j = target & 3, target >> 2
        outs[k][:count] = raw[s, :, pl.ds(pl.multiple_of(j * 384, 128), 384)]
        outs[k][count:, 128:] = jnp.zeros((8, 256), BF16)
        for q in range(4):
            @pl.when(s == (f ^ q))
            def _():
                outs[k][count:, :128] = places[q][count:, :128]


def head_masks():
    lanes = lax.broadcasted_iota(jnp.int32, (1, 128), 1)
    low = jnp.where(lanes < 64, 1.0, 0.0)
    return low, 1.0 - low


def attend_kernel(*refs):
    blocks, outs, (stack, probs, place_col) = refs[:8], refs[8:16], refs[16:]
    count = outs[0].shape[0]
    micros = stack.shape[0]
    per = count // micros
    total = stack.shape[1]
    eye = lax.broadcasted_iota(jnp.int32, (count, 128), 0) == lax.broadcasted_iota(
        jnp.int32, (count, 128), 1
    )
    for k, block in enumerate(blocks):
        row = block[count : count + 8, :128].astype(F32)[0:1]
        col = jnp.sum(jnp.where(eye, row, 0.0), axis=1, keepdims=True)
        for m in range(micros):
            stack[m, k * per : (k + 1) * per, :] = block[m * per : (m + 1) * per, :]
            place_col[m, k * per : (k + 1) * per, :] = jnp.broadcast_to(
                col[m * per : (m + 1) * per], (per, 128)
            )
    big_eye = lax.broadcasted_iota(jnp.int32, (total, total), 0) == lax.broadcasted_iota(
        jnp.int32, (total, total), 1
    )
    masks = head_masks()
    for m in range(micros):
        q, k, v = stack[m, :, :128], stack[m, :, 128:256], stack[m, :, 256:384]
        mine = place_col[m, :, 0:1]
        theirs = jnp.sum(jnp.where(big_eye, mine, 0.0), axis=0, keepdims=True)
        visible = theirs <= mine
        attended = jnp.zeros((total, 128), F32)
        for h in range(2):
            scores = mm_t(q * masks[h].astype(BF16), k) * (HEAD_DIM**-0.5)
            scores = jnp.where(visible, scores, MASKED)
            top = jnp.max(scores, axis=1, keepdims=True)
            grown = jnp.exp(scores - top)
            weight = grown / jnp.sum(grown, axis=1, keepdims=True)
            probs[2 * m + h] = weight
            attended = attended + mm(weight.astype(BF16), v) * masks[h]
        low = attended.astype(BF16)
        for k in range(8):
            outs[k][m * per : (m + 1) * per, :] = low[k * per : (k + 1) * per]


def split_sum(ids, full, send, keep):
    f = ids[1]
    send[0] = full[f ^ 1].astype(BF16)
    send[1] = full[f ^ 3].astype(BF16)
    keep[0] = full[f]
    keep[1] = full[f ^ 2]


def out_kernel(ids, w_out, b0, b1, b2, b3, b4, b5, b6, b7, attended, send, keep, full):
    c = ids[0]
    for k, block in enumerate((b0, b1, b2, b3, b4, b5, b6, b7)):
        target = c ^ k
        s, j = target & 3, target >> 2
        attended[s, :, pl.ds(pl.multiple_of(j * 128, 128), 128)] = block[...]
    for s in range(4):
        full[s] = mm(attended[s], w_out[...])
    split_sum(ids, full, send, keep)


def add_kernel(keep, received, send2, keep2):
    send2[...] = (keep[1] + received[1].astype(F32)).astype(BF16)
    keep2[...] = keep[0] + received[0].astype(F32)


def mid_kernel(keep, received, rowsx, gain, attn, norm2):
    count = keep.shape[0]
    value = keep[...] + received[...].astype(F32)
    attn[...] = value
    mid = rowsx[:count].astype(F32) + value
    norm2[...] = (mid * rms_factor(mid) * gain[...]).astype(BF16)


def mlp_kernel(
    ids, n0, n1, n2, n3, m0, m1, m2, m3, u0, u1, u2, u3, w_down,
    norm2, d_mlp, act, d_hidden, send, keep, w_up,
):
    f = ids[1]
    part = u0.shape[0]
    count = n0.shape[0]
    for k, u in enumerate((u0, u1, u2, u3)):
        w_up[pl.ds(pl.multiple_of((f ^ k) * part, part), part), :] = u[...]
    for k, (n, m) in enumerate(((n0, m0), (n1, m1), (n2, m2), (n3, m3))):
        rows = slice(k * count, (k + 1) * count)
        norm2[rows] = n[...]
        d_mlp[rows] = m[...]
        hidden = mm(n[...], w_up[...])
        d_act = mm_t(m[...], w_down[...])
        phi = 0.5 * (1.0 + lax.erf(hidden * (0.5**0.5)))
        act[rows] = (hidden * phi).astype(BF16)
        slope = phi + hidden * jnp.exp(-0.5 * hidden * hidden) * ((2.0 * math.pi) ** -0.5)
        low = (d_act * slope).astype(BF16)
        d_hidden[rows] = low
        d_norm2 = mm_t(low, w_up[...])
        if k % 2:
            send[k // 2] = d_norm2.astype(BF16)
        else:
            keep[k // 2] = d_norm2


def mlp_out_kernel(act, w_down, send, keep):
    count = send.shape[1]
    for k in range(4):
        part = mm(act[k * count : (k + 1) * count], w_down[...])
        if k % 2:
            send[k // 2] = part.astype(BF16)
        else:
            keep[k // 2] = part


def store_block(k, send, keep, where, value):
    if k % 2:
        send[(k // 2, *where)] = value.astype(BF16)
    else:
        keep[(k // 2, *where)] = value


def grad_mlp_kernel(ids, norm2, d_hidden, act, d_mlp, send, keep):
    c, f = ids[0], ids[1]
    for k in range(8):
        start = pl.multiple_of((c ^ k) * 128, 128)
        up = t_mm(norm2[:, pl.ds(start, 128)], d_hidden[...])
        for q in range(4):
            rows = pl.ds(pl.multiple_of((f ^ q) * 32, 32), 32)
            store_block(k, send, keep, (rows, slice(None)), up[q * 32 : (q + 1) * 32])
        down = t_mm(act[:, pl.ds(start, 128)], d_mlp[...])
        store_block(k, send, keep, (slice(128, 256), slice(None)), down)


def d_attn_kernel(keep, received, attn, rowsx, cots, gate, gain, d_mid_out, d_attn, grad_gain):
    count = keep.shape[0]
    mid = rowsx[:count].astype(F32) + attn[...]
    r2 = rms_factor(mid)
    d_norm2 = keep[...] + received[...].astype(F32)
    t2 = d_norm2 * gain[...]
    d_mid = r2 * t2 - mid * (r2 * r2 * r2) * jnp.mean(t2 * mid, axis=1, keepdims=True)
    d_mid_out[...] = d_mid
    d_attn[...] = (gate[...] * cots[...].astype(F32) + d_mid).astype(BF16)
    grad_gain[...] = jnp.sum(d_norm2 * mid * r2, axis=0, keepdims=True)


def d_attended_kernel(ids, w_out, d0, d1, d2, d3, *rest):
    outs, (d_attn, d_att) = rest[:8], rest[8:]
    c, f = ids[0], ids[1]
    for k, d in enumerate((d0, d1, d2, d3)):
        d_attn[f ^ k] = d[...]
        d_att[f ^ k] = mm_t(d[...], w_out[...]).astype(BF16)
    for k in range(8):
        target = c ^ k
        s, j = target & 3, target >> 2
        outs[k][...] = d_att[s, :, pl.ds(pl.multiple_of(j * 128, 128), 128)]


def attend_back_kernel(*refs):
    blocks, (stack, probs), outs, (d_stack,) = refs[:8], refs[8:10], refs[10:18], refs[18:]
    micros = stack.shape[0]
    count = outs[0].shape[0]
    per = count // micros
    total = stack.shape[1]
    masks = head_masks()
    for m in range(micros):
        for k, block in enumerate(blocks):
            d_stack[k * per : (k + 1) * per, :] = block[m * per : (m + 1) * per, :]
        q, k, v = stack[m, :, :128], stack[m, :, 128:256], stack[m, :, 256:384]
        d_out = d_stack[...]
        d_q = jnp.zeros((total, 128), F32)
        d_k = jnp.zeros((total, 128), F32)
        d_v = jnp.zeros((total, 128), F32)
        for h in range(2):
            weight = probs[2 * m + h]
            d_probs = mm_t(d_out * masks[h].astype(BF16), v)
            inner = jnp.sum(weight * d_probs, axis=1, keepdims=True)
            d_scores = (weight * (d_probs - inner)).astype(BF16)
            d_q = d_q + mm(d_scores, k) * masks[h]
            d_k = d_k + t_mm(d_scores, q) * masks[h]
            d_v = d_v + t_mm(weight.astype(BF16), d_out) * masks[h]
        d_q = (d_q * (HEAD_DIM**-0.5)).astype(BF16)
        d_k = (d_k * (HEAD_DIM**-0.5)).astype(BF16)
        d_v = d_v.astype(BF16)
        for t in range(8):
            rows, source = slice(m * per, (m + 1) * per), slice(t * per, (t + 1) * per)
            outs[t][rows, :128] = d_q[source]
            outs[t][rows, 128:256] = d_k[source]
            outs[t][rows, 256:384] = d_v[source]


def d_norm1_kernel(
    ids, w_full, r0, r1, r2, r3, b0, b1, b2, b3, b4, b5, b6, b7,
    d_qkv, send, keep, grad_gain, full,
):
    c, f = ids[0], ids[1]
    count = d_qkv.shape[1]
    for k, block in enumerate((b0, b1, b2, b3, b4, b5, b6, b7)):
        target = c ^ k
        s, j = target & 3, target >> 2
        d_qkv[s, :, pl.ds(pl.multiple_of(j * 384, 128), 384)] = block[...]
    for s in range(4):
        full[s] = mm_t(d_qkv[s], w_full[...])
    split_sum(ids, full, send, keep)
    total = jnp.zeros((1, w_full.shape[0]), F32)
    for k, r in enumerate((r0, r1, r2, r3)):
        rows = r[:count].astype(F32)
        total = total + jnp.sum(full[f ^ k] * (rows * rms_factor(rows)), axis=0, keepdims=True)
    grad_gain[...] = total


def grad_out_kernel(ids, attended, d_attn, send, keep, full):
    c = ids[0]
    total = jnp.zeros(full.shape, F32)
    for s in range(4):
        total = total + t_mm(attended[s], d_attn[s])
    full[...] = total
    for k in range(8):
        rows = full[pl.ds(pl.multiple_of((c ^ k) * 32, 32), 32), :]
        if k % 2:
            send[k // 2] = rows.astype(BF16)
        else:
            keep[k // 2] = rows


def grad_qkv_kernel(ids, norm1, d_qkv, gains, send, keep):
    c, f = ids[0], ids[1]
    for k in range(8):
        start = pl.multiple_of((c ^ k) * 128, 128)
        part = t_mm(norm1[:, pl.ds(start, 128)], d_qkv[...])
        for q in range(4):
            rows = pl.ds(pl.multiple_of((f ^ q) * 32, 32), 32)
            store_block(k, send, keep, (rows, slice(None)), part[q * 32 : (q + 1) * 32])
        for v in range(3):
            row = jnp.broadcast_to(gains[v : v + 1, pl.ds(start, 128)], (16, 128))
            store_block(k, send, keep, (slice(128, 144), slice(v * 128, v * 128 + 128)), row)
            store_block(
                k, send, keep, (slice(128, 144), slice(384 + v * 128, 512 + v * 128)),
                jnp.zeros((16, 128), F32),
            )


def place_rows(storage, base, micro, per, source, rows, out):
    tok_dev = source.shape[0]
    index = storage[...] - base[0]
    lanes = lax.broadcasted_iota(jnp.int32, (tok_dev, index.shape[1]), 1)
    hit = lax.broadcasted_iota(jnp.int32, (tok_dev, index.shape[1]), 0) == index
    mine = (lanes >= micro * per) & (lanes < (micro + 1) * per)
    pick = jnp.where(hit & mine, 1.0, 0.0)
    routed = jnp.sum(pick, axis=1, keepdims=True) > 0.5
    placed = mm(pick.astype(BF16), rows)
    out[...] = jnp.where(routed, placed, source[...].astype(F32)).astype(BF16)


def output_kernel(
    base, storage, keep, received, attn, rowsx, cots, gate, tokens,
    output, d_logit_out, grad_router, padded,
):
    count = keep.shape[0]
    micros = tokens.shape[0]
    branch = attn[...] + keep[...] + received[...].astype(F32)
    rows = rowsx[:count].astype(F32)
    d_logit = (
        jnp.sum(cots[...].astype(F32) * branch, axis=1, keepdims=True)
        * gate[...]
        * (1.0 - gate[...])
    )
    d_logit_out[...] = d_logit
    grad_router[...] = jnp.sum(rows * d_logit, axis=0, keepdims=True)
    padded[...] = jnp.zeros(padded.shape, BF16)
    padded[:count] = (rows + gate[...] * branch).astype(BF16)
    for micro in range(micros):
        place_rows(
            storage, base, micro, count // micros, tokens.at[micro], padded[...], output.at[micro]
        )


def input_grad_kernel(
    base, storage, keep, received, d_mid, rowsx, cots, d_logit, w_router, gain, cot,
    input_grad, padded,
):
    count = keep.shape[0]
    micros = cot.shape[0]
    rows = rowsx[:count].astype(F32)
    r1 = rms_factor(rows)
    t1 = (keep[...] + received[...].astype(F32)) * gain[...]
    d_rows = (
        cots[...].astype(F32)
        + d_mid[...]
        + r1 * t1
        - rows * (r1 * r1 * r1) * jnp.mean(t1 * rows, axis=1, keepdims=True)
        + d_logit[...] * w_router[...]
    )
    padded[...] = jnp.zeros(padded.shape, BF16)
    padded[:count] = d_rows.astype(BF16)
    for micro in range(micros):
        place_rows(
            storage, base, micro, count // micros, cot.at[micro], padded[...], input_grad.at[micro]
        )


def join_up_kernel(ids, p0, p1, p2, p3, out):
    part = p0.shape[1]
    for k, piece in enumerate((p0, p1, p2, p3)):
        out[:, pl.ds(pl.multiple_of((ids[1] ^ k) * part, part), part)] = piece[...]


def join_qkv_kernel(ids, p0, p1, p2, p3, v0, v1, v2, v3, out, vectors):
    width = out.shape[1] // 3
    part = width // 4
    for k, piece in enumerate((p0, p1, p2, p3)):
        for j in range(2):
            for b in range(3):
                start = pl.multiple_of((ids[1] ^ k) * part + (b * width + j * 128), 128)
                out[:, pl.ds(start, 128)] = piece[:, (3 * j + b) * 128 : (3 * j + b + 1) * 128]
    vectors[...] = v0[...] + v1[...] + v2[...] + v3[...]


def scatter_sum(send, keep):
    first = keep + exchange(send, "ctx", 8, 1).astype(F32)
    second = first[:2] + exchange(first[2:].astype(BF16), "ctx", 8, 4).astype(F32)
    return second[0] + exchange(second[1].astype(BF16), "ctx", 8, 2).astype(F32)


def row_sum(send, keep):
    received = exchange(send, "fsdp", 4, 1)
    count, width = keep.shape[1:]
    send2, keep2 = vmem_call(
        add_kernel, (sds((count, width), BF16), sds((count, width), F32)), (), (keep, received),
        name="add_rows",
    )
    return keep2, exchange(send2, "fsdp", 4, 2)


def row_gather(mine):
    across = exchange(mine, "fsdp", 4, 2)
    beside = exchange(mine, "fsdp", 4, 1)
    return mine, beside, across, exchange(across, "fsdp", 4, 1)


def swap_blocks(blocks):
    return (blocks[0], *(exchange(b, "ctx", 8, k) for k, b in enumerate(blocks) if k))


def shards_8x4(
    tokens, w_router, gain_attn, w_qkv, w_out, gain_mlp, w_up, w_down, routed, deal, cotangent
):
    micros, tok_dev, width = tokens.shape[0], tokens.shape[2], tokens.shape[3]
    per = routed.shape[2]
    count = micros * per
    total = 8 * per
    part = width // 4
    hidden = w_down.shape[0]
    c, f = lax.axis_index("ctx"), lax.axis_index("fsdp")
    ids = jnp.stack([c, f]).astype(jnp.int32)
    base = (c * tok_dev).astype(jnp.int32).reshape(1)
    storage = jnp.pad(routed.reshape(1, count), ((0, 0), (0, 128 - count)), constant_values=-1)
    tok, cot = tokens[:, 0], cotangent[:, 0]
    w_router, gain_attn, gain_mlp = (
        w_router.reshape(1, width), gain_attn.reshape(1, width), gain_mlp.reshape(1, width),
    )
    rows_bf, rows_f = sds((count, width), BF16), sds((count, width), F32)
    pair_bf, pair_f = sds((2, count, width), BF16), sds((2, count, width), F32)

    w_parts = vmem_call(slice_qkv_kernel, (sds((part, 768), BF16),) * 4, (ids,), (w_qkv,), name="slice_qkv")
    w_parts = (w_parts[0], *(exchange(w_parts[k], "fsdp", 4, k) for k in (1, 2, 3)))
    rowsx, cots, d_mlp_mine, gate = pl.pallas_call(
        gather_kernel,
        out_shape=(sds((count + 8, width), BF16), rows_bf, rows_bf, sds((count, 1), F32)),
        in_specs=[
            pl.BlockSpec(memory_space=pltpu.SMEM),
            pl.BlockSpec(memory_space=pltpu.VMEM),
            pl.BlockSpec(memory_space=pltpu.SMEM),
        ]
        + [pl.BlockSpec(memory_space=pltpu.VMEM)] * 3,
        out_specs=(pl.BlockSpec(memory_space=pltpu.VMEM),) * 4,
        compiler_params=pltpu.CompilerParams(vmem_limit_bytes=VMEM_LIMIT),
        name="gather_rows",
    )(deal, storage, base, tok, cot, w_router)
    rows_all = row_gather(rowsx)
    *blocks, w_full, norm1 = vmem_call(
        qkv_kernel,
        (sds((count + 8, 384), BF16),) * 8 + (sds((width, 768), BF16), sds((4, count, width), BF16)),
        (ids,), (gain_attn, *rows_all, *w_parts), scratch=[pltpu.VMEM((4, count, 768), BF16)],
        flops=2 * 4 * count * width * 768, name="qkv",
    )
    blocks = swap_blocks(blocks)
    up_parts = vmem_call(slice_up_kernel, (sds((part, hidden), BF16),) * 4, (ids,), (w_up,), name="slice_up")
    up_parts = (up_parts[0], *(exchange(up_parts[k], "fsdp", 4, k) for k in (1, 2, 3)))
    d_mlp_all = row_gather(d_mlp_mine)
    *heads, stack, probs = vmem_call(
        attend_kernel,
        (sds((count, 128), BF16),) * 8
        + (sds((micros, total, 384), BF16), sds((2 * micros, total, total), F32)),
        (), blocks, scratch=[pltpu.VMEM((micros, total, 128), F32)],
        flops=2 * micros * 2 * total * total * 256, name="attend",
    )
    heads = swap_blocks(heads)
    attended, send, keep = vmem_call(
        out_kernel, (sds((4, count, part), BF16), pair_bf, pair_f), (ids,), (w_out, *heads),
        scratch=[pltpu.VMEM((4, count, width), F32)], flops=2 * 4 * count * part * width,
        name="attn_out",
    )
    keep, received = row_sum(send, keep)
    attn, norm2 = vmem_call(
        mid_kernel, (rows_f, rows_bf), (), (keep, received, rowsx, gain_mlp), name="mid"
    )
    norm2_all = row_gather(norm2)
    norm2_full, d_mlp_full, act, d_hidden, send, keep = vmem_call(
        mlp_kernel,
        (sds((4 * count, width), BF16), sds((4 * count, width), BF16))
        + (sds((4 * count, hidden), BF16), sds((4 * count, hidden), BF16), pair_bf, pair_f),
        (ids,), (*norm2_all, *d_mlp_all, *up_parts, w_down),
        scratch=[pltpu.VMEM((width, hidden), BF16)], flops=3 * 2 * 4 * count * width * hidden,
        name="mlp",
    )
    keep, received = row_sum(send, keep)
    send_m, keep_m = vmem_call(
        mlp_out_kernel, (pair_bf, pair_f), (), (act, w_down),
        flops=2 * 4 * count * width * hidden, name="mlp_out",
    )
    send_g, keep_g = vmem_call(
        grad_mlp_kernel, (sds((4, 256, width), BF16), sds((4, 256, width), F32)), (ids,),
        (norm2_full, d_hidden, act, d_mlp_full), flops=2 * 2 * 4 * count * width * hidden,
        name="grad_mlp",
    )
    d_mid, d_attn, grad_gain_mlp = vmem_call(
        d_attn_kernel, (rows_f, rows_bf, sds((1, width), F32)), (),
        (keep, received, attn, rowsx, cots, gate, gain_mlp), name="d_attn",
    )
    d_attn_all = row_gather(d_attn)
    *d_heads, d_attn_full = vmem_call(
        d_attended_kernel, (sds((count, 128), BF16),) * 8 + (sds((4, count, width), BF16),),
        (ids,), (w_out, *d_attn_all), scratch=[pltpu.VMEM((4, count, part), BF16)],
        flops=2 * 4 * count * part * width, name="d_attended",
    )
    d_heads = swap_blocks(d_heads)
    d_blocks = vmem_call(
        attend_back_kernel, (sds((count, 384), BF16),) * 8, (), (*d_heads, stack, probs),
        scratch=[pltpu.VMEM((total, 128), BF16)], flops=2 * micros * 2 * total * total * 512,
        name="attend_back",
    )
    d_blocks = swap_blocks(d_blocks)
    d_qkv, send, keep, grad_gain_attn = vmem_call(
        d_norm1_kernel, (sds((4, count, 768), BF16), pair_bf, pair_f, sds((1, width), F32)),
        (ids,), (w_full, *rows_all, *d_blocks), scratch=[pltpu.VMEM((4, count, width), F32)],
        flops=2 * 4 * count * 768 * width, name="d_norm1",
    )
    keep, received = row_sum(send, keep)

    keep_m, received_m = row_sum(send_m, keep_m)
    output, d_logit, grad_router = pl.pallas_call(
        output_kernel,
        out_shape=(sds(tok.shape, BF16), sds((count, 1), F32), sds((1, width), F32)),
        in_specs=[pl.BlockSpec(memory_space=pltpu.SMEM)]
        + [pl.BlockSpec(memory_space=pltpu.VMEM)] * 8,
        out_specs=(pl.BlockSpec(memory_space=pltpu.VMEM),) * 3,
        scratch_shapes=[pltpu.VMEM((128, width), BF16)],
        compiler_params=pltpu.CompilerParams(vmem_limit_bytes=VMEM_LIMIT),
        name="output",
    )(base, storage, keep_m, received_m, attn, rowsx, cots, gate, tok)
    (input_grad,) = vmem_call(
        input_grad_kernel, (sds(cot.shape, BF16),), (base,),
        (storage, keep, received, d_mid, rowsx, cots, d_logit, w_router, gain_attn, cot),
        scratch=[pltpu.VMEM((128, width), BF16)], name="input_grad",
    )

    sum_mlp = scatter_sum(send_g, keep_g)
    up_chunks = sum_mlp[:128].reshape(4, 32, hidden)
    up_chunks = (up_chunks[0], *(exchange(up_chunks[k], "fsdp", 4, k) for k in (1, 2, 3)))
    (grad_up,) = vmem_call(join_up_kernel, (sds((32, 4 * hidden), F32),), (ids,), up_chunks, name="join_up")
    to_owner = [(4 * a + b, 4 * (2 * b + a // 4) + a % 4) for a in range(8) for b in range(4)]
    grad_down = lax.ppermute(sum_mlp[128:], ("ctx", "fsdp"), to_owner)
    send_o, keep_o = vmem_call(
        grad_out_kernel, (sds((4, 32, width), BF16), sds((4, 32, width), F32)), (ids,),
        (attended, d_attn_full), scratch=[pltpu.VMEM((part, width), F32)],
        flops=2 * 4 * count * part * width, name="grad_out",
    )
    grad_out = lax.ppermute(scatter_sum(send_o, keep_o), ("ctx", "fsdp"), to_owner)
    gains = jnp.concatenate([grad_router, grad_gain_attn, grad_gain_mlp], axis=0)
    send_q, keep_q = vmem_call(
        grad_qkv_kernel, (sds((4, 144, 768), BF16), sds((4, 144, 768), F32)), (ids,),
        (norm1.reshape(4 * count, width), d_qkv.reshape(4 * count, 768), gains),
        flops=2 * 4 * count * width * 768, name="grad_qkv",
    )
    sum_qkv = scatter_sum(send_q, keep_q)
    vector = sum_qkv[128:136]
    pieces = tuple(sum_qkv[32 * k : 32 * k + 32] for k in range(4))
    pieces = tuple(
        p if k == 0 else exchange(jnp.concatenate([p, vector], axis=0), "fsdp", 4, k)
        for k, p in enumerate(pieces)
    )
    grad_qkv, vectors = vmem_call(
        join_qkv_kernel, (sds((32, 3 * width), F32), sds((8, 768), F32)), (ids,),
        (*(p[:32] for p in pieces), vector, *(p[32:] for p in pieces[1:])), name="join_qkv",
    )
    vectors = lax.dynamic_slice_in_dim(vectors[0, :384].reshape(3, 128), f * 32, 32, axis=1)
    return (
        output[:, None], input_grad[:, None], vectors[0], vectors[1], grad_qkv, grad_out,
        vectors[2], grad_up, grad_down,
    )


def solution(mesh):
    placed = (
        P(None, "fsdp", "ctx", None),
        P(),
        P(),
        P("fsdp", None),
        P("fsdp", None),
        P(),
        P("fsdp", None),
        P("fsdp", None),
        P(None, "fsdp", "ctx"),
        P(),
        P(None, "fsdp", "ctx", None),
    )
    fits = mesh.shape["ctx"] == 8 and mesh.shape["fsdp"] == 4
    return jax.shard_map(
        shards_8x4 if fits else shards,
        mesh=mesh,
        in_specs=placed,
        out_specs=(
            P(None, "fsdp", "ctx", None),
            P(None, "fsdp", "ctx", None),
            P(("ctx", "fsdp")),
            P(("ctx", "fsdp")),
            P(("ctx", "fsdp"), None),
            P(("ctx", "fsdp"), None),
            P(("ctx", "fsdp")),
            P(("ctx", "fsdp"), None),
            P(("ctx", "fsdp"), None),
        ),
        check_vma=False,
    )
```

```python
import math

import jax
import jax.numpy as jnp
from jax import lax
from jax.experimental import pallas as pl
from jax.experimental.pallas import tpu as pltpu
from jax.sharding import PartitionSpec as P

HEADS = 16
HEAD_DIM = 64
BLOCK = 256


EPSILON = 1e-06
MASKED = -1e30
HIGHEST = lax.Precision.HIGHEST
BF16, F32 = jnp.bfloat16, jnp.float32
VMEM_LIMIT = 24 * 2**20
UP_ORDER = (1, 2, 4)
WEIGHT = 10**10


def rms_norm(values, gain):
    factor = lax.rsqrt(jnp.mean(values * values, axis=-1, keepdims=True) + EPSILON)
    return values * factor * gain


def exact_gelu(values):
    return jax.nn.gelu(values, approximate=False)


def fetch(w_qkv, w_out, w_up, w_down):
    return (
        lax.all_gather(w_qkv, "fsdp", axis=0, tiled=True),
        lax.all_gather(w_out, "fsdp", axis=0, tiled=True),
        lax.all_gather(w_up, "fsdp", axis=0, tiled=True),
        lax.all_gather(w_down, "fsdp", axis=0, tiled=True),
    )


def lookup(table, index):
    hits = index[..., None] == jnp.arange(table.shape[0], dtype=jnp.int32)
    return jnp.sum(jnp.where(hits, table, 0), axis=-1)


def outer_sum(left, right):
    return lax.dot_general(
        left, right, (((0,), (0,)), ((), ())), preferred_element_type=jnp.float32
    )


def gather_rows(pieces, column):
    return jnp.concatenate([piece[column] for piece in pieces], axis=0)


def shards(
    tokens, w_router, gain_attn, w_qkv, w_out, gain_mlp, w_up, w_down, routed, deal, cotangent
):
    micros, tok_dev, width = (tokens.shape[0], tokens.shape[2], tokens.shape[3])
    span = tok_dev // 2
    rank = lax.axis_index("ctx")
    storage = routed[:, 0, :]
    local_rows = storage - rank * tok_dev
    anchor = lookup(deal, storage // span) * span + storage % span
    own_blocks = anchor // BLOCK
    all_blocks = lax.all_gather(own_blocks, "ctx", axis=1, tiled=True)
    factor = HEAD_DIM ** (-0.5)
    outputs, in_grads, kept = ([], [], [])
    sum_router = jnp.zeros((width,), jnp.float32)
    sum_gain_attn = jnp.zeros((width,), jnp.float32)
    sum_gain_mlp = jnp.zeros((width,), jnp.float32)
    for micro in range(micros):
        full_qkv, full_out, full_up, full_down = fetch(w_qkv, w_out, w_up, w_down)
        resid = tokens[micro, 0].astype(jnp.float32)
        grad_in = cotangent[micro, 0].astype(jnp.float32)
        rows_index = local_rows[micro]
        rows = jnp.take(resid, rows_index, axis=0)
        count = rows.shape[0]
        gate = jax.nn.sigmoid(jnp.dot(rows, w_router, precision=HIGHEST))
        norm1, norm1_back = jax.vjp(rms_norm, rows, gain_attn)
        norm1_low = norm1.astype(jnp.bfloat16)
        qkv = jnp.dot(norm1_low, full_qkv, preferred_element_type=jnp.float32).astype(jnp.bfloat16)
        queries = qkv[:, :width]
        keys_local = qkv[:, width : 2 * width]
        values_local = qkv[:, 2 * width :]
        keys_all, values_all = (
            lax.all_gather(keys_local, "ctx", axis=0, tiled=True),
            lax.all_gather(values_local, "ctx", axis=0, tiled=True),
        )
        total = keys_all.shape[0]
        query_heads = queries.reshape(count, HEADS, HEAD_DIM)
        key_heads = keys_all.reshape(total, HEADS, HEAD_DIM)
        value_heads = values_all.reshape(total, HEADS, HEAD_DIM)
        visible = all_blocks[micro][None, :] <= own_blocks[micro][:, None]
        scores = (
            jnp.einsum("qhd,khd->hqk", query_heads, key_heads, preferred_element_type=jnp.float32)
            * factor
        )
        scores = jnp.where(visible[None], scores, MASKED)
        probs = jax.nn.softmax(scores, axis=-1)
        probs_low = probs.astype(jnp.bfloat16)
        attended = jnp.einsum(
            "hqk,khd->qhd", probs_low, value_heads, preferred_element_type=jnp.float32
        )
        attended_low = attended.reshape(count, width).astype(jnp.bfloat16)
        attn = jnp.dot(attended_low, full_out, preferred_element_type=jnp.float32)
        mid = rows + attn
        norm2, norm2_back = jax.vjp(rms_norm, mid, gain_mlp)
        norm2_low = norm2.astype(jnp.bfloat16)
        hidden = jnp.dot(norm2_low, full_up, preferred_element_type=jnp.float32)
        act, gelu_back = jax.vjp(exact_gelu, hidden)
        act_low = act.astype(jnp.bfloat16)
        mlp = jnp.dot(act_low, full_down, preferred_element_type=jnp.float32)
        branch = attn + mlp
        outputs.append(resid.at[rows_index].set(rows + gate[:, None] * branch).astype(jnp.bfloat16))
        cot_rows = jnp.take(grad_in, rows_index, axis=0)
        d_branch = gate[:, None] * cot_rows
        d_mlp = d_branch.astype(jnp.bfloat16)
        d_logit = jnp.sum(cot_rows * branch, axis=-1) * gate * (1.0 - gate)
        d_act = jnp.dot(d_mlp, full_down.T, preferred_element_type=jnp.float32)
        d_hidden = gelu_back(d_act)[0].astype(jnp.bfloat16)
        d_norm2 = jnp.dot(d_hidden, full_up.T, preferred_element_type=jnp.float32)
        d_mid, d_gain2 = norm2_back(d_norm2)
        d_attn = (d_branch + d_mid).astype(jnp.bfloat16)
        d_attended = jnp.dot(d_attn, full_out.T, preferred_element_type=jnp.float32).astype(
            jnp.bfloat16
        )
        d_heads = d_attended.reshape(count, HEADS, HEAD_DIM)
        d_probs = jnp.einsum(
            "qhd,khd->hqk", d_heads, value_heads, preferred_element_type=jnp.float32
        )
        weighted = jnp.sum(probs * d_probs, axis=-1, keepdims=True)
        d_scores = (probs * (d_probs - weighted)).astype(jnp.bfloat16)
        d_query = (
            jnp.einsum("hqk,khd->qhd", d_scores, key_heads, preferred_element_type=jnp.float32)
            * factor
        )
        d_key_part = (
            jnp.einsum("hqk,qhd->khd", d_scores, query_heads, preferred_element_type=jnp.float32)
            * factor
        )
        d_value_part = jnp.einsum(
            "hqk,qhd->khd", probs_low, d_heads, preferred_element_type=jnp.float32
        )
        d_keys, d_values = (
            lax.psum_scatter(
                d_key_part.reshape(total, width), "ctx", scatter_dimension=0, tiled=True
            ),
            lax.psum_scatter(
                d_value_part.reshape(total, width), "ctx", scatter_dimension=0, tiled=True
            ),
        )
        d_qkv = jnp.concatenate([d_query.reshape(count, width), d_keys, d_values], axis=1).astype(
            jnp.bfloat16
        )
        d_norm1 = jnp.dot(d_qkv, full_qkv.T, preferred_element_type=jnp.float32)
        d_rows_norm, d_gain1 = norm1_back(d_norm1)
        d_rows = cot_rows + d_mid + d_rows_norm + d_logit[:, None] * w_router
        in_grads.append(grad_in.at[rows_index].set(d_rows).astype(jnp.bfloat16))
        sum_router = sum_router + jnp.dot(d_logit, rows, precision=HIGHEST)
        sum_gain_attn = sum_gain_attn + d_gain1
        sum_gain_mlp = sum_gain_mlp + d_gain2
        kept.append((norm1_low, d_qkv, attended_low, d_attn, norm2_low, d_hidden, act_low, d_mlp))
    stacked_rows = tuple((gather_rows(kept, column) for column in range(8)))
    grad_qkv = outer_sum(stacked_rows[0], stacked_rows[1])
    grad_out = outer_sum(stacked_rows[2], stacked_rows[3])
    grad_up = outer_sum(stacked_rows[4], stacked_rows[5])
    grad_down = outer_sum(stacked_rows[6], stacked_rows[7])
    summed = (
        lax.psum_scatter(sum_router, ("ctx", "fsdp"), scatter_dimension=0, tiled=True),
        lax.psum_scatter(sum_gain_attn, ("ctx", "fsdp"), scatter_dimension=0, tiled=True),
        lax.psum_scatter(grad_qkv, ("ctx", "fsdp"), scatter_dimension=0, tiled=True),
        lax.psum_scatter(grad_out, ("ctx", "fsdp"), scatter_dimension=0, tiled=True),
        lax.psum_scatter(sum_gain_mlp, ("ctx", "fsdp"), scatter_dimension=0, tiled=True),
        lax.psum_scatter(grad_up, ("ctx", "fsdp"), scatter_dimension=0, tiled=True),
        lax.psum_scatter(grad_down, ("ctx", "fsdp"), scatter_dimension=0, tiled=True),
    )
    output = jnp.stack(outputs)[:, None]
    input_grad = jnp.stack(in_grads)[:, None]
    return (
        output,
        input_grad,
        summed[0],
        summed[1],
        summed[2],
        summed[3],
        summed[4],
        summed[5],
        summed[6],
    )


ORDER = (0, 2, 1, 3)


def sds(shape, dtype):
    return jax.ShapeDtypeStruct(shape, dtype)


def local(shape, dtype):
    return pltpu.VMEM(shape, dtype)


def near(x):
    return pltpu.with_memory_space_constraint(x, pltpu.VMEM)


class Chain:
    def __init__(self):
        self.last = None

    def __call__(self, kernel, outs, smem, args, scratch=(), name=None, far=(), after=(), weight=WEIGHT):
        count = len(smem) + len(far) + len(args)
        spec = pl.BlockSpec(memory_space=pltpu.VMEM)
        extra = () if self.last is None else (near(self.last),)
        extra = (*extra, *(near(a) for a in after))

        def body(*refs):
            kernel(*refs[:count], *refs[count + len(extra) :])

        results = pl.pallas_call(
            body,
            out_shape=tuple(outs),
            in_specs=[pl.BlockSpec(memory_space=pltpu.SMEM)] * len(smem)
            + [pl.BlockSpec(memory_space=pltpu.HBM)] * len(far)
            + [spec] * (len(args) + len(extra)),
            out_specs=tuple(spec for _ in outs),
            scratch_shapes=list(scratch),
            compiler_params=pltpu.CompilerParams(vmem_limit_bytes=VMEM_LIMIT),
            cost_estimate=pl.CostEstimate(flops=weight, bytes_accessed=weight // 10000, transcendentals=0),
            name=name,
        )(
            *smem, *(pltpu.with_memory_space_constraint(a, pltpu.HBM) for a in far), *(near(a) for a in args), *extra
        )
        if not isinstance(outs[0], jax.ShapeDtypeStruct):
            self.last = results[0]
        return results

    def hold(self, x, *after):
        (x,) = self(hold_kernel, (local(x.shape, x.dtype),), (), (x,), after=after, name="hold")
        return x


def hold_kernel(x, out):
    out[...] = x[...]


def pair_kernel(a, b, out):
    out[0] = a[...]
    out[1] = b[...]


def mm(left, right):
    return jnp.dot(left, right, preferred_element_type=F32)


def mm_t(left, right):
    return lax.dot_general(left, right, (((1,), (1,)), ((), ())), preferred_element_type=F32)


def t_mm(left, right):
    return lax.dot_general(left, right, (((0,), (0,)), ((), ())), preferred_element_type=F32)


def exchange(x, axis, size, mask):
    return lax.ppermute(x, axis, [(i, i ^ mask) for i in range(size)])


def rms_factor(values):
    return lax.rsqrt(jnp.mean(values * values, axis=-1, keepdims=True) + EPSILON)


def aligned(start, unit):
    return pl.multiple_of(start, unit)


def iota(shape, axis):
    return lax.broadcasted_iota(jnp.int32, shape, axis)


def picks(ids, routed, micro, tok_dev):
    index = routed[micro : micro + 1, :] - ids[0] * tok_dev
    shape = (tok_dev, routed.shape[1])
    return jnp.where(iota(shape, 0) == index, 1.0, 0.0)


def share_peers(ids):
    return ids[1], ids[1] ^ 1, ids[1] ^ (2 + (ids[0] & 1))


def share_rows(c, f):
    y = c & 1
    return f, f ^ 1, f ^ (2 + y), f ^ (3 - y)


def cut_qkv(ids, half, w_qkv, pieces, sem, first, by_y=True):
    width = w_qkv.shape[1] // 3
    copies = []
    peers = share_peers(ids) if by_y else tuple(ids[1] ^ k for k in range(4))
    for k, (peer, piece) in enumerate(zip(peers, pieces)):
        for b in range(3):
            start = b * width + peer * (width // 4) + half * 128
            copies.append(
                pltpu.make_async_copy(
                    w_qkv.at[:, pl.ds(aligned(start, 128), 128)],
                    piece.at[:, pl.ds(b * 128, 128)],
                    sem.at[first + 3 * k + b],
                )
            )
    return copies


def front_kernel(ids, deal, tokens, w_qkv, routed, rowsx, p0, p1, p2, near_tokens, sem):
    micros, tok_dev, width = tokens.shape
    per = routed.shape[1]
    count = micros * per
    span = tok_dev // 2
    first = pltpu.make_async_copy(tokens, near_tokens, sem.at[0])
    first.start()
    copies = cut_qkv(ids, ids[0] >> 2, w_qkv, (p0, p1, p2), sem, 1)
    for copy in copies:
        copy.start()
    stored = routed[...]
    chunk = stored // span
    anchor = jnp.zeros_like(stored)
    for entry in range(deal.shape[0]):
        anchor = jnp.where(chunk == entry, deal[entry], anchor)
    place = ((anchor * span + stored % span) // BLOCK).astype(F32)
    rowsx[count:] = jnp.zeros((8, width), BF16)
    for micro in range(micros):
        rowsx[count + micro : count + micro + 1, :per] = place[micro : micro + 1].astype(BF16)
    first.wait()
    for micro in range(micros):
        pick = picks(ids, routed, micro, tok_dev).astype(BF16)
        rowsx[micro * per : (micro + 1) * per] = t_mm(pick, near_tokens[micro]).astype(BF16)
    for copy in copies:
        copy.wait()


def cut_kernel(ids, w_up, w_qkv, p0, p1, p2, v0, v1, v2, v3, sem):
    share = p0.shape[1]
    copies = cut_qkv(ids, 1 - (ids[0] >> 2), w_qkv, (v0, v1, v2, v3), sem, 3, False)
    for k, (peer, piece) in enumerate(zip(share_peers(ids), (p0, p1, p2))):
        copies.append(
            pltpu.make_async_copy(
                w_up.at[:, pl.ds(aligned(peer * share, share), share)], piece, sem.at[k]
            )
        )
    for copy in copies:
        copy.start()
    for copy in copies:
        copy.wait()


def cot_kernel(ids, routed, cot, rowsx, both):
    micros, tok_dev = cot.shape[:2]
    per = routed.shape[1]
    start = rowsx.shape[0]
    both[:start] = rowsx[...]
    for micro in range(micros):
        pick = picks(ids, routed, micro, tok_dev).astype(BF16)
        both[start + micro * per : start + (micro + 1) * per] = t_mm(pick, cot[micro]).astype(BF16)


def rows_of(both):
    return both[: both.shape[0] // 2 - 4].astype(F32)


def cots_of(both):
    return both[both.shape[0] // 2 + 4 :].astype(F32)


def d_mlp_kernel(b0, b1, b2, b3, w_router, d_mlp, gate_out):
    count = gate_out.shape[1]
    for i, both in enumerate((b0, b1, b2, b3)):
        gate = jax.nn.sigmoid(jnp.sum(rows_of(both) * w_router[...], axis=1, keepdims=True))
        d_mlp[i * count : (i + 1) * count] = (gate * cots_of(both)).astype(BF16)
        gate_out[i] = gate


def head_masks():
    lanes = iota((1, 128), 1)
    low = jnp.where(lanes < 64, 1.0, 0.0)
    return low, 1.0 - low


def attend_kernel(
    ids, r0, r1, r2, r3, gain, w0, w1, w2, w3,
    h0, h1, h2, h3, h4, h5, h6, h7, stack, probs, norm1, place_col, result,
):
    c, f = ids[0], ids[1]
    micros, total = stack.shape[0], stack.shape[1]
    count = h0.shape[0]
    per = count // micros
    eye = iota((per, 128), 0) == iota((per, 128), 1)
    for peer, source in zip((f, f ^ 2, f ^ 1, f ^ 3), (r0, r1, r2, r3)):
        for h in range(2):
            rows = source[h, :count].astype(F32)
            index = ((c >> 2) ^ h) * 4 + peer
            norm1[pl.ds(aligned(index * count, 16), count)] = (
                rows * rms_factor(rows) * gain[...]
            ).astype(BF16)
            places = source[h, count : count + 8, :128].astype(F32)
            for m in range(micros):
                col = jnp.sum(jnp.where(eye, places[m : m + 1], 0.0), axis=1, keepdims=True)
                place_col[m, pl.ds(aligned(index * per, per), per), :] = jnp.broadcast_to(
                    col, (per, 128)
                )
    qkv = jnp.zeros((8 * count, 384), F32)
    for peer, w in zip(share_rows(c, f), (w0, w1, w2, w3)):
        part = w.shape[0]
        qkv = qkv + mm(norm1[:, pl.ds(aligned(peer * part, part), part)], w[...])
    low = qkv.astype(BF16)
    for t in range(8):
        for m in range(micros):
            stack[m, t * per : (t + 1) * per, :] = low[
                t * count + m * per : t * count + (m + 1) * per
            ]
    big_eye = iota((total, total), 0) == iota((total, total), 1)
    masks = head_masks()
    for m in range(micros):
        q, k, v = stack[m, :, :128], stack[m, :, 128:256], stack[m, :, 256:384]
        mine = place_col[m, :, 0:1]
        theirs = jnp.sum(jnp.where(big_eye, mine, 0.0), axis=0, keepdims=True)
        visible = theirs <= mine
        attended = jnp.zeros((total, 128), F32)
        for h in range(2):
            scores = mm_t(q * masks[h].astype(BF16), k) * (HEAD_DIM**-0.5)
            scores = jnp.where(visible, scores, MASKED)
            top = jnp.max(scores, axis=1, keepdims=True)
            grown = jnp.exp(scores - top)
            weight = grown / jnp.sum(grown, axis=1, keepdims=True)
            probs[2 * m + h] = weight
            attended = attended + mm(weight.astype(BF16), v) * masks[h]
        result[m] = attended.astype(BF16)
        for k, out in enumerate((h0, h1, h2, h3, h4, h5, h6, h7)):
            out[m * per : (m + 1) * per, :] = result[m, pl.ds(aligned((c ^ k) * per, per), per), :]


def row_slot(f, s, count):
    k = s ^ f
    return aligned(((k & 1) * 2 + (k >> 1)) * count, 16)


def split_rows(full, send, keep):
    count = send.shape[1]
    for i in range(2):
        keep[i] = full[i * count : (i + 1) * count]
        send[i] = full[(2 + i) * count : (3 + i) * count].astype(BF16)


def block_place(ids, k, count, lanes):
    peer = ids[0] ^ k
    columns = aligned((peer >> 2) * lanes, 128)
    return pl.ds(row_slot(ids[1], peer & 3, count), count), pl.ds(columns, lanes)


def out_kernel(ids, b0, b1, b2, b3, b4, b5, b6, b7, w_out, attended, send, keep, full):
    count = b0.shape[0]
    for k, block in enumerate((b0, b1, b2, b3, b4, b5, b6, b7)):
        attended[block_place(ids, k, count, 128)] = block[...]
    full[...] = mm(attended[...], w_out[...])
    split_rows(full, send, keep)


def add_both_kernel(keep, received, total):
    total[...] = (keep[...] + received[...].astype(F32)).astype(BF16)


def add_own_kernel(keep, received, send2, keep2):
    send2[...] = (keep[1] + received[1].astype(F32)).astype(BF16)
    keep2[...] = keep[0] + received[0].astype(F32)


def mid_kernel(low, received, both0, both1, gain, attn, norm2):
    for i, both in enumerate((both0, both1)):
        value = low[i].astype(F32) + received[1 - i].astype(F32)
        attn[i] = value
        mid = rows_of(both) + value
        norm2[i] = (mid * rms_factor(mid) * gain[...]).astype(BF16)


def mlp_kernel(
    ids, n0, n1, d_mlp, u0, u1, u2, u3, w_down,
    send, keep, act_send, d_send, act_keep, d_keep, norm2, act, d_hidden, back,
):
    c = ids[0]
    part = u0.shape[0]
    count = n0.shape[1]
    shares = tuple(zip(share_rows(ids[0], ids[1]), (u0, u1, u2, u3)))
    for i in range(2):
        norm2[i * count : (i + 1) * count] = n0[i]
        norm2[(2 + i) * count : (3 + i) * count] = n1[i]
    hidden = jnp.zeros(act.shape, F32)
    for peer, u in shares:
        hidden = hidden + mm(norm2[:, pl.ds(aligned(peer * part, part), part)], u[...])
    d_act = mm_t(d_mlp[...], w_down[...])
    phi = 0.5 * (1.0 + lax.erf(hidden * (0.5**0.5)))
    act[...] = (hidden * phi).astype(BF16)
    slope = phi + hidden * jnp.exp(-0.5 * hidden * hidden) * ((2.0 * math.pi) ** -0.5)
    d_hidden[...] = (d_act * slope).astype(BF16)
    for i, (some_act, some_d) in enumerate(((act_keep, d_keep), (act_send, d_send))):
        for high in range(2):
            start = aligned(high * 512 + (((c >> 1) & 1) ^ i) * 256, 128)
            some_act[:, high * 256 : (high + 1) * 256] = act[:, pl.ds(start, 256)]
        some_d[...] = d_hidden[:, pl.ds(aligned(((c & 1) ^ i) * 512, 128), 512)]
    for peer, u in shares:
        back[:, pl.ds(aligned(peer * part, part), part)] = mm_t(d_hidden[...], u[...])
    split_rows(back, send, keep)


def mlp_out_kernel(act, w_down, attn, gate, b0, b1, b2, b3, send, keep, router, full):
    full[...] = mm(act[...], w_down[...])
    split_rows(full, send, keep)
    count = gate.shape[1]
    total = jnp.zeros(router.shape, F32)
    for i, both in enumerate((b0, b1, b2, b3)):
        own = slice(i * count, (i + 1) * count)
        part = jnp.sum(cots_of(both) * (attn[own] + full[own]), axis=1, keepdims=True)
        part = part * gate[i] * (1.0 - gate[i])
        total = total + jnp.sum(rows_of(both) * part, axis=0, keepdims=True)
    router[...] = total


def pick_rows(c, peer, share, out, lanes):
    @pl.when(peer == (c >> 1))
    def _():
        out[:, lanes] = share[pl.ds(aligned((c & 1) * 128, 128), 128), :]


def pick_kernel(ids, *refs):
    shares, (up_rows, qkv_rows) = refs[:12], refs[12:]
    c, f = ids[0], ids[1]
    for peer, u, a in zip(share_rows(c, f), shares[:4], shares[4:8]):
        pick_rows(c, peer, u, up_rows, slice(None))
        pick_rows(c, peer, a, qkv_rows, slice(0, 384))
    for k, b in enumerate(shares[8:]):
        pick_rows(c, f ^ k, b, qkv_rows, slice(384, 768))


def block_order(order):
    one, two, three = order
    keep = (0, three, two, two | three)
    return keep, tuple(k | one for k in keep)


def put_block(order, k, send, keep, where, value):
    kept, sent = block_order(order)
    if k in kept:
        keep[(kept.index(k), *where)] = value
    else:
        send[(sent.index(k), *where)] = value.astype(BF16)


def chunk(f, q):
    return pl.ds(aligned((f ^ q) * 32, 32), 32)


def grad_up_kernel(ids, norm2, near_a, near_b, d_own, d_near, send, keep, rows, columns):
    count = norm2.shape[0]
    half = count // 2
    rows[:count] = norm2[...]
    for i in range(2):
        rows[count + i * (half // 2) : count + (i + 1) * (half // 2)] = near_a[i]
        rows[count + half + i * (half // 2) : count + half + (i + 1) * (half // 2)] = near_b[i]
    columns[:count] = d_own[...]
    columns[count:] = d_near[...]
    for place, (target, index) in enumerate(((keep, 0), (send, 0), (keep, 1), (send, 1))):
        kk = (0, 1, 2, 3)[place]
        start = aligned(((ids[0] >> 1) ^ kk) * 256, 128)
        value = t_mm(rows[:, pl.ds(start, 256)], columns[...])
        for owner in range(2):
            for q in range(4):
                at = pl.ds(aligned(((ids[0] & 1) ^ owner) * 128 + (ids[1] ^ q) * 32, 32), 32)
                piece = value[owner * 128 + q * 32 : owner * 128 + (q + 1) * 32]
                target[index, at] = piece.astype(target.dtype)


def grad_down_kernel(ids, d_mlp, near_a, near_b, a_own, a_near, send, keep, rows, columns):
    count = d_mlp.shape[0]
    half = count // 2
    rows[:count] = d_mlp[...]
    rows[count : count + half] = near_a[...]
    rows[count + half :] = near_b[...]
    columns[:count] = a_own[...]
    columns[count:] = a_near[...]
    c = ids[0]
    for target, index, k in ((keep, 0, 0), (send, 0, 1), (keep, 1, 4), (send, 1, 5)):
        start = aligned(((c >> 2) ^ (k >> 2)) * 256 + ((c & 1) ^ (k & 1)) * 128, 128)
        value = t_mm(columns[:, pl.ds(start, 128)], rows[...])
        target[index] = value.astype(target.dtype)


def grad_attn_kernel(
    ids, norm1, b0, b1, b2, b3, b4, b5, b6, b7, attended, d_attn, router, send, keep, joined, full,
):
    count = b0.shape[0]
    for k, block in enumerate((b0, b1, b2, b3, b4, b5, b6, b7)):
        joined[pl.ds(aligned((ids[0] ^ k) * count, 16), count)] = block[...]
    full[...] = t_mm(attended[...], d_attn[...])
    for k in range(8):
        owner = ids[0] ^ k
        start = aligned(owner * 128, 128)
        value = t_mm(norm1[:, pl.ds(start, 128)], joined[...])
        for q in range(4):
            where = (chunk(ids[1], q), slice(0, 384))
            put_block(UP_ORDER, k, send, keep, where, value[q * 32 : (q + 1) * 32])
            where = (slice(q * 32, (q + 1) * 32), slice(384, 640))
            rows = full[pl.ds(aligned(owner * 32, 32), 32), q * 256 : (q + 1) * 256]
            put_block(UP_ORDER, k, send, keep, where, rows)
        below = slice(128, 136)
        put_block(UP_ORDER, k, send, keep, (below, slice(128, 640)), jnp.zeros((8, 512), F32))
        share = jnp.broadcast_to(router[:, pl.ds(start, 128)], (8, 128))
        put_block(UP_ORDER, k, send, keep, (below, slice(0, 128)), share)


def d_attn_kernel(low, received, attn, both0, both1, gate, gain, d_mid_out, d_attn):
    for i, both in enumerate((both0, both1)):
        mid = rows_of(both) + attn[i]
        r2 = rms_factor(mid)
        d_norm2 = low[i].astype(F32) + received[1 - i].astype(F32)
        t2 = d_norm2 * gain[...]
        d_mid = r2 * t2 - mid * (r2 * r2 * r2) * jnp.mean(t2 * mid, axis=1, keepdims=True)
        d_attn[i] = (gate[i] * cots_of(both) + d_mid).astype(BF16)
        if i == 0:
            d_mid_out[...] = d_mid


def d_attended_kernel(ids, d0, d1, w_out, b0, b1, b2, b3, b4, b5, b6, b7, d_attn, d_att):
    count = d0.shape[1]
    for i in range(2):
        d_attn[i * count : (i + 1) * count] = d0[i]
        d_attn[(2 + i) * count : (3 + i) * count] = d1[i]
    d_att[...] = mm_t(d_attn[...], w_out[...])
    for k, block in enumerate((b0, b1, b2, b3, b4, b5, b6, b7)):
        block[...] = d_att[block_place(ids, k, count, 128)].astype(BF16)


def attend_back_kernel(ids, *refs):
    blocks, (stack, probs), outs, (d_stack, result) = refs[:8], refs[8:10], refs[10:18], refs[18:]
    micros, total = stack.shape[0], stack.shape[1]
    count = outs[0].shape[0]
    per = count // micros
    masks = head_masks()
    for m in range(micros):
        rows = slice(m * per, (m + 1) * per)
        for k in range(8):
            d_stack[pl.ds(aligned((ids[0] ^ k) * per, per), per), :] = blocks[k][rows]
        q, k, v = stack[m, :, :128], stack[m, :, 128:256], stack[m, :, 256:384]
        d_out = d_stack[...]
        d_q = jnp.zeros((total, 128), F32)
        d_k = jnp.zeros((total, 128), F32)
        d_v = jnp.zeros((total, 128), F32)
        for h in range(2):
            weight = probs[2 * m + h]
            d_probs = mm_t(d_out * masks[h].astype(BF16), v)
            inner = jnp.sum(weight * d_probs, axis=1, keepdims=True)
            d_scores = (weight * (d_probs - inner)).astype(BF16)
            d_q = d_q + mm(d_scores, k) * masks[h]
            d_k = d_k + t_mm(d_scores, q) * masks[h]
            d_v = d_v + t_mm(weight.astype(BF16), d_out) * masks[h]
        result[m, :, :128] = (d_q * (HEAD_DIM**-0.5)).astype(BF16)
        result[m, :, 128:256] = (d_k * (HEAD_DIM**-0.5)).astype(BF16)
        result[m, :, 256:384] = d_v.astype(BF16)
        for k in range(8):
            outs[k][rows] = result[m, pl.ds(aligned((ids[0] ^ k) * per, per), per), :]


def d_norm1_kernel(
    ids, d0, d1, d2, d3, d4, d5, d6, d7, a0, a1, a2, a3, b0, b1, b2, b3,
    send, keep, d_qkv, full,
):
    c, f = ids[0], ids[1]
    count = d0.shape[0]
    part = a0.shape[0]
    for k, block in enumerate((d0, d1, d2, d3, d4, d5, d6, d7)):
        rows = pl.ds(row_slot(f, (c ^ k) & 3, count), count)
        d_qkv[rows, (k >> 2) * 384 : (k >> 2) * 384 + 384] = block[...]
    for peer, a in zip(share_rows(c, f), (a0, a1, a2, a3)):
        full[:, pl.ds(aligned(peer * part, part), part)] = mm_t(d_qkv[:, :384], a[...])
    for k, b in enumerate((b0, b1, b2, b3)):
        columns = pl.ds(aligned((f ^ k) * part, part), part)
        full[:, columns] = full[:, columns] + mm_t(d_qkv[:, 384:], b[...])
    split_rows(full, send, keep)


def place_rows(ids, routed, micro, source, rows, out):
    tok_dev = source.shape[0]
    pick = picks(ids, routed, micro, tok_dev)
    changed = jnp.sum(pick, axis=1, keepdims=True) > 0.5
    placed = mm(pick.astype(BF16), rows)
    out[...] = jnp.where(changed, placed, source[...].astype(F32)).astype(BF16)


def output_kernel(
    ids, routed, keep, received, attn, both, gate, tokens, d_logit_out, output,
):
    count = keep.shape[0]
    micros = tokens.shape[0]
    per = count // micros
    branch = attn[0] + keep[...] + received[...].astype(F32)
    rows = rows_of(both)
    open_gate = gate[0]
    d_logit = (
        jnp.sum(cots_of(both) * branch, axis=1, keepdims=True)
        * open_gate
        * (1.0 - open_gate)
    )
    d_logit_out[...] = d_logit
    result = (rows + open_gate * branch).astype(BF16)
    for micro in range(micros):
        own = result[micro * per : (micro + 1) * per]
        place_rows(ids, routed, micro, tokens.at[micro], own, output.at[micro])


def input_grad_kernel(
    ids, routed, keep, received, d_mid, both, d_logit, w_router, gain, cot, input_grad,
):
    count = keep.shape[0]
    micros = cot.shape[0]
    per = count // micros
    rows = rows_of(both)
    r1 = rms_factor(rows)
    t1 = (keep[...] + received[...].astype(F32)) * gain[...]
    d_rows = (
        cots_of(both)
        + d_mid[...]
        + r1 * t1
        - rows * (r1 * r1 * r1) * jnp.mean(t1 * rows, axis=1, keepdims=True)
        + d_logit[...] * w_router[...]
    ).astype(BF16)
    for micro in range(micros):
        own = d_rows[micro * per : (micro + 1) * per]
        place_rows(ids, routed, micro, cot.at[micro], own, input_grad.at[micro])


def as_row(column):
    count = column.shape[0]
    eye = iota((count, count), 0) == iota((count, count), 1)
    return jnp.sum(jnp.where(eye, column, 0.0), axis=0, keepdims=True)


def owned(ids, vector, count):
    start = (4 * ids[0] + ids[1]) * count
    shape = (count, vector.shape[1])
    hit = iota(shape, 1) == iota(shape, 0) + start
    return jnp.sum(jnp.where(hit, vector[...], 0.0), axis=1, keepdims=True)


def join_up_kernel(ids, p0, p1, p2, p3, gain, out, grad_gain):
    rows, part = out.shape[0], out.shape[1] // 4
    total = jnp.zeros((rows, 1), F32)
    for k, piece in enumerate((p0, p1, p2, p3)):
        out[:, pl.ds(aligned((ids[1] ^ k) * part, part), part)] = piece[:, :part]
        total = total + piece[:, part : part + 1]
    grad_gain[...] = as_row(total / owned(ids, gain, rows))


def join_qkv_kernel(ids, p0, p1, p2, p3, gain, out, grad_gain, grad_router):
    rows, width = out.shape[0], out.shape[1] // 3
    part = width // 4
    total = jnp.zeros((rows, 1), F32)
    router = jnp.zeros((rows, 1), F32)
    for k, piece in enumerate((p0, p1, p2, p3)):
        for half in range(2):
            for b in range(3):
                start = b * width + (ids[1] ^ k) * part + ((ids[0] >> 2) ^ half) * 128
                out[:, pl.ds(aligned(start, 128), 128)] = piece[
                    :, (3 * half + b) * 128 : (3 * half + b + 1) * 128
                ]
        total = total + piece[:, 768:769]
        router = router + piece[:, 896:897]
    grad_gain[...] = as_row(total / owned(ids, gain, rows))
    grad_router[...] = as_row(router)


def join_down_kernel(a, b, out):
    out[...] = a[...].astype(F32) + b[...].astype(F32)


def add_halves(keep, received, send2, keep2):
    half = keep.shape[0] // 2
    keep2[...] = keep[:half] + received[:half].astype(F32)
    send2[...] = (keep[half:] + received[half:].astype(F32)).astype(BF16)


def halves_kernel(*refs):
    count = len(refs) // 4
    for i in range(count):
        add_halves(*refs[2 * i : 2 * i + 2], *refs[2 * count + 2 * i : 2 * count + 2 * i + 2])


def hop2_kernel(keep_u, got_u, keep_d, got_d, send, keep, down0, down1):
    add_halves(keep_u, got_u, send, keep)
    down0[...] = (keep_d[0] + got_d[0].astype(F32)).astype(BF16)
    down1[...] = (keep_d[1] + got_d[1].astype(F32)).astype(BF16)


def last_kernel(keep_u, got_u, send, mine):
    total = keep_u[0] + got_u[0].astype(F32)
    half = total.shape[0] // 2
    mine[...] = total[:half]
    send[...] = total[half:].astype(BF16)


def up_pieces_kernel(ids, mine, other, w_rows, c0, c1, c2, c3):
    rows, half = c0.shape[0], mine.shape[1]
    y = ids[0] & 1
    for k, piece in enumerate((c0, c1, c2, c3)):
        own = slice(k * rows, (k + 1) * rows)
        weights = pl.ds(aligned((ids[1] ^ k) * rows, rows), rows)
        total = jnp.zeros((rows, 1), F32)
        for side, value in ((y, mine[own]), (1 - y, other[own].astype(F32))):
            columns = pl.ds(aligned(side * half, 128), half)
            piece[:, columns] = value
            total = total + jnp.sum(
                value * w_rows[weights, columns].astype(F32), axis=1, keepdims=True
            )
        piece[:, 2 * half :] = jnp.broadcast_to(total, (rows, 128))


def pieces_kernel(ids, mine, got, w_rows, c0, c1, c2, c3, out):
    rows = c0.shape[0]
    router = mine[0, 128:129, :128] + got[0, 128:136, :128].astype(F32)[0:1]
    for k, piece in enumerate((c0, c1, c2, c3)):
        own = slice(k * rows, (k + 1) * rows)
        first = (ids[1] ^ k) * rows
        weights = pl.ds(aligned(first, rows), rows)
        a, b = mine[0, own, :384], got[0, own, :384].astype(F32)
        piece[:, :384] = a
        piece[:, 384:768] = b
        total = jnp.sum(a * w_rows[weights, :384].astype(F32), axis=1, keepdims=True)
        total = total + jnp.sum(b * w_rows[weights, 384:].astype(F32), axis=1, keepdims=True)
        piece[:, 768:896] = jnp.broadcast_to(total, (rows, 128))
        hit = iota((rows, 128), 1) == iota((rows, 128), 0) + first
        share = jnp.sum(jnp.where(hit, router, 0.0), axis=1, keepdims=True)
        piece[:, 896:] = jnp.broadcast_to(share, (rows, 128))
        out[:, k * 256 : (k + 1) * 256] = mine[0, own, 384:640] + got[0, own, 384:640].astype(F32)


def halves(call, name, *pairs):
    outs = []
    for keep, _ in pairs:
        shape = (keep.shape[0] // 2, *keep.shape[1:])
        outs += [local(shape, BF16), local(shape, F32)]
    flat = call(halves_kernel, outs, (), [x for pair in pairs for x in pair], name=name)
    return [(flat[2 * i + 1], flat[2 * i]) for i in range(len(pairs))]


def all_rows_sum(call, send, keep):
    received = exchange(send, "fsdp", 4, 1)
    (low,) = call(add_both_kernel, (local(keep.shape, BF16),), (), (keep, received), name="add_both")
    return low, exchange(low, "fsdp", 4, 2)


def own_rows_sum(call, send, keep):
    received = exchange(send, "fsdp", 4, 1)
    shape = keep.shape[1:]
    send2, keep2 = call(
        add_own_kernel, (local(shape, BF16), local(shape, F32)), (), (keep, received), name="add_own"
    )
    return keep2, exchange(send2, "fsdp", 4, 2)


def swap_blocks(blocks):
    got = {k: exchange(blocks[k], "ctx", 8, k) for k in (7, 6, 5, 4, 3, 2, 1)}
    return (blocks[0], *(got[k] for k in range(1, 8)))


def swap_across(parts):
    mine, beside, across = parts
    across = lax.ppermute(
        across, ("ctx", "fsdp"),
        [(4 * a + b, 4 * a + (b ^ (2 + (a & 1)))) for a in range(8) for b in range(4)],
    )
    return mine, exchange(beside, "fsdp", 4, 1), across


def swap_pieces(pieces):
    return (pieces[0], *(exchange(pieces[k], "fsdp", 4, k) for k in (1, 2, 3)))


def shards_8x4(
    tokens, w_router, gain_attn, w_qkv, w_out, gain_mlp, w_up, w_down, routed, deal, cotangent
):
    micros, tok_dev, width = tokens.shape[0], tokens.shape[2], tokens.shape[3]
    per = routed.shape[2]
    count = micros * per
    total = 8 * per
    part = width // 4
    hidden = w_down.shape[0]
    c, f = lax.axis_index("ctx"), lax.axis_index("fsdp")
    ids = jnp.stack([c, f]).astype(jnp.int32)
    tok, cot, routed = tokens[:, 0], cotangent[:, 0], routed[:, 0]
    w_router, gain_attn, gain_mlp = (
        w_router.reshape(1, width), gain_attn.reshape(1, width), gain_mlp.reshape(1, width),
    )
    rows_bf, rows_f = local((count, width), BF16), local((count, width), F32)
    pair_bf, pair_f = local((2, count, width), BF16), local((2, count, width), F32)
    all_bf, all_quarter = local((4 * count, width), BF16), local((4 * count, part), BF16)
    hidden_bf = local((4 * count, hidden), BF16)
    vector = local((1, width), F32)
    dma = pltpu.SemaphoreType.DMA
    call = Chain()

    rowsx, *w_parts = call(
        front_kernel,
        (local((count + 8, width), BF16), *(local((part, 384), BF16),) * 3),
        (ids, deal), (routed,), far=(tok, w_qkv),
        scratch=[pltpu.VMEM(tok.shape, BF16), dma((10,))], name="front",
    )
    turn = [(4 * a + b, 4 * ((a & 4) | b) + (a & 3)) for a in range(8) for b in range(4)]
    turned = lax.ppermute(rowsx, ("ctx", "fsdp"), turn)
    turned_far = lax.ppermute(rowsx, ("ctx", "fsdp"), [(a, b ^ 16) for a, b in turn])
    w_mine, w_beside, w_across = swap_across(w_parts)
    w_parts = (w_mine, w_beside, w_across, exchange(w_across, "ctx", 8, 1))
    (seq,) = call(
        pair_kernel, (local((2, count + 8, width), BF16),), (), (turned, turned_far), name="pair"
    )
    seq_x, seq_c = exchange(seq, "fsdp", 4, 2), exchange(seq, "fsdp", 4, 1)
    seq_xc = exchange(seq_x, "fsdp", 4, 1)
    (both,) = call(
        cot_kernel, (local((2 * count + 8, width), BF16),), (ids,), (routed, cot, rowsx), name="cot_rows"
    )
    both_x, both_c = exchange(both, "fsdp", 4, 2), exchange(both, "fsdp", 4, 1)
    both_xc = exchange(both_x, "fsdp", 4, 1)
    up_mine, up_beside, up_across, *rest = call(
        cut_kernel, (local((part, hidden), BF16),) * 3 + (local((part, 384), BF16),) * 4, (ids,), (),
        far=(w_up, w_qkv), scratch=[dma((15,))], name="cut_shares",
    )
    _, up_beside, up_across = swap_across((up_mine, up_beside, up_across))
    *heads, stack, probs, norm1 = call(
        attend_kernel,
        (
            *(local((count, 128), BF16),) * 8, local((micros, total, 384), BF16),
            local((2 * micros, total, total), F32), local((8 * count, width), BF16),
        ),
        (ids,), (seq, seq_x, seq_c, seq_xc, gain_attn, *w_parts),
        scratch=[pltpu.VMEM((micros, total, 128), F32), pltpu.VMEM((micros, total, 128), BF16)],
        name="attend",
    )
    heads = swap_blocks(heads)
    attended, send, keep, attn_part = call(
        out_kernel, (all_quarter, pair_bf, pair_f, local((4 * count, width), F32)),
        (ids,), (*heads, w_out), name="attn_out", after=(up_across, both_x),
    )
    up_parts = (up_mine, up_beside, up_across, exchange(up_across, "ctx", 8, 1))
    low, received = all_rows_sum(call, send, keep)
    d_mlp, gate = call(
        d_mlp_kernel, (all_bf, local((4, count, 1), F32)), (),
        (both, both_x, both_c, both_xc, w_router), name="d_mlp", weight=0,
    )
    d_mlp_a = exchange(d_mlp[: 2 * count], "ctx", 8, 2)
    d_mlp_b = exchange(d_mlp_a, "fsdp", 4, 1)
    attn, norm2 = call(
        mid_kernel, (pair_f, pair_bf), (), (low, received, both, both_x, gain_mlp), name="mid"
    )
    norm2_a = exchange(norm2, "ctx", 8, 1)
    norm2_b = exchange(norm2_a, "fsdp", 4, 1)
    half_bf = local((4 * count, hidden // 2), BF16)
    send, keep, act_send, d_send, act_keep, d_keep, norm2, act = call(
        mlp_kernel, (pair_bf, pair_f, half_bf, half_bf, half_bf, half_bf, all_bf, hidden_bf), (ids,),
        (norm2, exchange(norm2, "fsdp", 4, 1), d_mlp, *up_parts, w_down),
        scratch=[pltpu.VMEM((4 * count, hidden), BF16), pltpu.VMEM((4 * count, width), F32)],
        name="mlp",
    )
    d_near, act_near = exchange(d_send, "ctx", 8, 1), exchange(act_send, "ctx", 8, 2)
    low, received = all_rows_sum(call, send, keep)
    d_mid, d_attn = call(
        d_attn_kernel, (rows_f, pair_bf), (),
        (low, received, attn, both, both_x, gate, gain_mlp), name="d_attn",
        after=(d_near, act_near),
    )
    *d_heads, d_attn = call(
        d_attended_kernel, (*(local((count, 128), BF16),) * 8, all_bf), (ids,),
        (d_attn, exchange(d_attn, "fsdp", 4, 1), w_out),
        scratch=[pltpu.VMEM((4 * count, part), F32)], name="d_attended",
    )
    d_heads = swap_blocks(d_heads)
    send_u, keep_u = call(
        grad_up_kernel, (local((2, 256, hidden // 2), BF16), local((2, 256, hidden // 2), F32)), (ids,),
        (norm2, norm2_a, norm2_b, d_keep, d_near), name="grad_up", weight=0,
        scratch=[pltpu.VMEM((8 * count, width), BF16), pltpu.VMEM((8 * count, hidden // 2), BF16)],
    )
    send_d, keep_d = call(
        grad_down_kernel, (local((2, 128, width), BF16), local((2, 128, width), F32)), (ids,),
        (d_mlp, d_mlp_a, d_mlp_b, act_keep, act_near), name="grad_down", weight=0,
        scratch=[pltpu.VMEM((8 * count, width), BF16), pltpu.VMEM((8 * count, hidden // 2), BF16)],
    )
    send_m, keep_m, router = call(
        mlp_out_kernel, (pair_bf, pair_f, vector), (),
        (act, w_down, attn_part, gate, both, both_x, both_c, both_xc), name="mlp_out", weight=0,
        scratch=[pltpu.VMEM((4 * count, width), F32)],
    )
    got_u, got_d = exchange(send_u, "ctx", 8, 2), exchange(send_d, "ctx", 8, 1)
    rest = swap_pieces(rest)
    w_up_rows, w_qkv_rows = call(
        pick_kernel, (local((128, hidden), BF16), local((128, 768), BF16)), (ids,),
        (*up_parts, *w_parts, *rest), name="pick", weight=0,
    )
    d_blocks = call(
        attend_back_kernel, (local((count, 384), BF16),) * 8, (ids,), (*d_heads, stack, probs),
        scratch=[pltpu.VMEM((total, 128), BF16), pltpu.VMEM((micros, total, 384), BF16)],
        name="attend_back",
    )
    d_own = swap_blocks(d_blocks)
    send_q, keep_q = call(
        grad_attn_kernel, (local((4, 136, 640), BF16), local((4, 136, 640), F32)), (ids,),
        (norm1, *d_blocks, attended, d_attn, router), name="grad_attn", weight=0,
        scratch=[pltpu.VMEM((8 * count, 384), BF16), pltpu.VMEM((part, width), F32)],
    )
    got_q = exchange(send_q, "ctx", 8, UP_ORDER[0])
    keep_m, received_m = own_rows_sum(call, send_m, keep_m)
    send_u, keep_u, down0, down1 = call(
        hop2_kernel,
        (local((1, 256, hidden // 2), BF16), local((1, 256, hidden // 2), F32))
        + (local((128, width), BF16),) * 2,
        (), (keep_u, got_u, keep_d, got_d), name="hop2", weight=0,
    )
    got_u = exchange(send_u, "ctx", 8, 4)
    owners = [(4 * a + b, 4 * (2 * b + a // 4) + a % 4) for a in range(8) for b in range(4)]
    far_owners = [(a ^ 16, b) for a, b in owners]
    down0 = lax.ppermute(down0, ("ctx", "fsdp"), owners)
    down1 = lax.ppermute(down1, ("ctx", "fsdp"), far_owners)
    d_logit, output = call(
        output_kernel, (local((count, 1), F32), sds(tok.shape, BF16)), (ids,),
        (routed, keep_m, received_m, attn, both, gate, tok), name="output", weight=0,
    )
    send, keep = call(
        d_norm1_kernel, (pair_bf, pair_f), (ids,),
        (*d_own, *w_parts, *rest), name="d_norm1",
        scratch=[pltpu.VMEM((4 * count, 768), BF16), pltpu.VMEM((4 * count, width), F32)],
    )
    keep, received = own_rows_sum(call, send, keep)
    ((keep_q, send_q),) = halves(call, "hop1_attn", (keep_q, got_q))
    got_q = exchange(send_q, "ctx", 8, UP_ORDER[1])
    (input_grad,) = call(
        input_grad_kernel, (sds(cot.shape, BF16),), (ids,),
        (routed, keep, received, d_mid, both, d_logit, w_router, gain_attn, cot), name="input_grad",
    )
    send_u, mine_u = call(
        last_kernel, (local((128, hidden // 2), BF16), local((128, hidden // 2), F32)),
        (), (keep_u, got_u), name="hop3",
    )
    other_u = exchange(send_u, "ctx", 8, 1)
    ((keep_q, send_q),) = halves(call, "hop2_attn", (keep_q, got_q))
    got_q = exchange(send_q, "ctx", 8, 4)
    chunks = call(
        up_pieces_kernel, (local((32, hidden + 128), F32),) * 4, (ids,), (mine_u, other_u, w_up_rows),
        name="up_pieces",
    )
    chunks = swap_pieces(chunks)
    *qkv_chunks, grad_out = call(
        pieces_kernel, (local((32, 1024), F32),) * 4 + (local((32, width), F32),), (ids,),
        (keep_q, got_q, w_qkv_rows), name="qkv_pieces",
    )
    qkv_chunks = swap_pieces(qkv_chunks)
    grad_out = lax.ppermute(grad_out, ("ctx", "fsdp"), owners)
    (grad_down,) = call(
        join_down_kernel, (sds((128, width), F32),), (), (down0, down1), name="join_down"
    )
    row = sds((1, 32), F32)
    grad_up, grad_gain_mlp = call(
        join_up_kernel, (sds((32, 4 * hidden), F32), row), (ids,), (*chunks, gain_mlp), name="join_up"
    )
    grad_qkv, grad_gain_attn, grad_router = call(
        join_qkv_kernel, (sds((32, 3 * width), F32), row, row), (ids,), (*qkv_chunks, gain_attn),
        name="join_qkv",
    )
    return (
        output[:, None], input_grad[:, None], grad_router[0], grad_gain_attn[0], grad_qkv, grad_out,
        grad_gain_mlp[0], grad_up, grad_down,
    )


def solution(mesh):
    placed = (
        P(None, "fsdp", "ctx", None),
        P(),
        P(),
        P("fsdp", None),
        P("fsdp", None),
        P(),
        P("fsdp", None),
        P("fsdp", None),
        P(None, "fsdp", "ctx"),
        P(),
        P(None, "fsdp", "ctx", None),
    )
    fits = mesh.shape["ctx"] == 8 and mesh.shape["fsdp"] == 4
    return jax.shard_map(
        shards_8x4 if fits else shards,
        mesh=mesh,
        in_specs=placed,
        out_specs=(
            P(None, "fsdp", "ctx", None),
            P(None, "fsdp", "ctx", None),
            P(("ctx", "fsdp")),
            P(("ctx", "fsdp")),
            P(("ctx", "fsdp"), None),
            P(("ctx", "fsdp"), None),
            P(("ctx", "fsdp")),
            P(("ctx", "fsdp"), None),
            P(("ctx", "fsdp"), None),
        ),
        check_vma=False,
    )
```

```python
import math

import jax
import jax.numpy as jnp
from jax import lax
from jax.experimental import pallas as pl
from jax.experimental.pallas import tpu as pltpu
from jax.sharding import PartitionSpec as P

HEADS = 16
HEAD_DIM = 64
BLOCK = 256


EPSILON = 1e-06
MASKED = -1e30
HIGHEST = lax.Precision.HIGHEST
BF16, F32 = jnp.bfloat16, jnp.float32
VMEM_LIMIT = 24 * 2**20
WEIGHT = 10**10


def rms_norm(values, gain):
    factor = lax.rsqrt(jnp.mean(values * values, axis=-1, keepdims=True) + EPSILON)
    return values * factor * gain


def exact_gelu(values):
    return jax.nn.gelu(values, approximate=False)


def fetch(w_qkv, w_out, w_up, w_down):
    return (
        lax.all_gather(w_qkv, "fsdp", axis=0, tiled=True),
        lax.all_gather(w_out, "fsdp", axis=0, tiled=True),
        lax.all_gather(w_up, "fsdp", axis=0, tiled=True),
        lax.all_gather(w_down, "fsdp", axis=0, tiled=True),
    )


def lookup(table, index):
    hits = index[..., None] == jnp.arange(table.shape[0], dtype=jnp.int32)
    return jnp.sum(jnp.where(hits, table, 0), axis=-1)


def outer_sum(left, right):
    return lax.dot_general(
        left, right, (((0,), (0,)), ((), ())), preferred_element_type=jnp.float32
    )


def gather_rows(pieces, column):
    return jnp.concatenate([piece[column] for piece in pieces], axis=0)


def shards(
    tokens, w_router, gain_attn, w_qkv, w_out, gain_mlp, w_up, w_down, routed, deal, cotangent
):
    micros, tok_dev, width = (tokens.shape[0], tokens.shape[2], tokens.shape[3])
    span = tok_dev // 2
    rank = lax.axis_index("ctx")
    storage = routed[:, 0, :]
    local_rows = storage - rank * tok_dev
    anchor = lookup(deal, storage // span) * span + storage % span
    own_blocks = anchor // BLOCK
    all_blocks = lax.all_gather(own_blocks, "ctx", axis=1, tiled=True)
    factor = HEAD_DIM ** (-0.5)
    outputs, in_grads, kept = ([], [], [])
    sum_router = jnp.zeros((width,), jnp.float32)
    sum_gain_attn = jnp.zeros((width,), jnp.float32)
    sum_gain_mlp = jnp.zeros((width,), jnp.float32)
    for micro in range(micros):
        full_qkv, full_out, full_up, full_down = fetch(w_qkv, w_out, w_up, w_down)
        resid = tokens[micro, 0].astype(jnp.float32)
        grad_in = cotangent[micro, 0].astype(jnp.float32)
        rows_index = local_rows[micro]
        rows = jnp.take(resid, rows_index, axis=0)
        count = rows.shape[0]
        gate = jax.nn.sigmoid(jnp.dot(rows, w_router, precision=HIGHEST))
        norm1, norm1_back = jax.vjp(rms_norm, rows, gain_attn)
        norm1_low = norm1.astype(jnp.bfloat16)
        qkv = jnp.dot(norm1_low, full_qkv, preferred_element_type=jnp.float32).astype(jnp.bfloat16)
        queries = qkv[:, :width]
        keys_local = qkv[:, width : 2 * width]
        values_local = qkv[:, 2 * width :]
        keys_all, values_all = (
            lax.all_gather(keys_local, "ctx", axis=0, tiled=True),
            lax.all_gather(values_local, "ctx", axis=0, tiled=True),
        )
        total = keys_all.shape[0]
        query_heads = queries.reshape(count, HEADS, HEAD_DIM)
        key_heads = keys_all.reshape(total, HEADS, HEAD_DIM)
        value_heads = values_all.reshape(total, HEADS, HEAD_DIM)
        visible = all_blocks[micro][None, :] <= own_blocks[micro][:, None]
        scores = (
            jnp.einsum("qhd,khd->hqk", query_heads, key_heads, preferred_element_type=jnp.float32)
            * factor
        )
        scores = jnp.where(visible[None], scores, MASKED)
        probs = jax.nn.softmax(scores, axis=-1)
        probs_low = probs.astype(jnp.bfloat16)
        attended = jnp.einsum(
            "hqk,khd->qhd", probs_low, value_heads, preferred_element_type=jnp.float32
        )
        attended_low = attended.reshape(count, width).astype(jnp.bfloat16)
        attn = jnp.dot(attended_low, full_out, preferred_element_type=jnp.float32)
        mid = rows + attn
        norm2, norm2_back = jax.vjp(rms_norm, mid, gain_mlp)
        norm2_low = norm2.astype(jnp.bfloat16)
        hidden = jnp.dot(norm2_low, full_up, preferred_element_type=jnp.float32)
        act, gelu_back = jax.vjp(exact_gelu, hidden)
        act_low = act.astype(jnp.bfloat16)
        mlp = jnp.dot(act_low, full_down, preferred_element_type=jnp.float32)
        branch = attn + mlp
        outputs.append(resid.at[rows_index].set(rows + gate[:, None] * branch).astype(jnp.bfloat16))
        cot_rows = jnp.take(grad_in, rows_index, axis=0)
        d_branch = gate[:, None] * cot_rows
        d_mlp = d_branch.astype(jnp.bfloat16)
        d_logit = jnp.sum(cot_rows * branch, axis=-1) * gate * (1.0 - gate)
        d_act = jnp.dot(d_mlp, full_down.T, preferred_element_type=jnp.float32)
        d_hidden = gelu_back(d_act)[0].astype(jnp.bfloat16)
        d_norm2 = jnp.dot(d_hidden, full_up.T, preferred_element_type=jnp.float32)
        d_mid, d_gain2 = norm2_back(d_norm2)
        d_attn = (d_branch + d_mid).astype(jnp.bfloat16)
        d_attended = jnp.dot(d_attn, full_out.T, preferred_element_type=jnp.float32).astype(
            jnp.bfloat16
        )
        d_heads = d_attended.reshape(count, HEADS, HEAD_DIM)
        d_probs = jnp.einsum(
            "qhd,khd->hqk", d_heads, value_heads, preferred_element_type=jnp.float32
        )
        weighted = jnp.sum(probs * d_probs, axis=-1, keepdims=True)
        d_scores = (probs * (d_probs - weighted)).astype(jnp.bfloat16)
        d_query = (
            jnp.einsum("hqk,khd->qhd", d_scores, key_heads, preferred_element_type=jnp.float32)
            * factor
        )
        d_key_part = (
            jnp.einsum("hqk,qhd->khd", d_scores, query_heads, preferred_element_type=jnp.float32)
            * factor
        )
        d_value_part = jnp.einsum(
            "hqk,qhd->khd", probs_low, d_heads, preferred_element_type=jnp.float32
        )
        d_keys, d_values = (
            lax.psum_scatter(
                d_key_part.reshape(total, width), "ctx", scatter_dimension=0, tiled=True
            ),
            lax.psum_scatter(
                d_value_part.reshape(total, width), "ctx", scatter_dimension=0, tiled=True
            ),
        )
        d_qkv = jnp.concatenate([d_query.reshape(count, width), d_keys, d_values], axis=1).astype(
            jnp.bfloat16
        )
        d_norm1 = jnp.dot(d_qkv, full_qkv.T, preferred_element_type=jnp.float32)
        d_rows_norm, d_gain1 = norm1_back(d_norm1)
        d_rows = cot_rows + d_mid + d_rows_norm + d_logit[:, None] * w_router
        in_grads.append(grad_in.at[rows_index].set(d_rows).astype(jnp.bfloat16))
        sum_router = sum_router + jnp.dot(d_logit, rows, precision=HIGHEST)
        sum_gain_attn = sum_gain_attn + d_gain1
        sum_gain_mlp = sum_gain_mlp + d_gain2
        kept.append((norm1_low, d_qkv, attended_low, d_attn, norm2_low, d_hidden, act_low, d_mlp))
    stacked_rows = tuple((gather_rows(kept, column) for column in range(8)))
    grad_qkv = outer_sum(stacked_rows[0], stacked_rows[1])
    grad_out = outer_sum(stacked_rows[2], stacked_rows[3])
    grad_up = outer_sum(stacked_rows[4], stacked_rows[5])
    grad_down = outer_sum(stacked_rows[6], stacked_rows[7])
    summed = (
        lax.psum_scatter(sum_router, ("ctx", "fsdp"), scatter_dimension=0, tiled=True),
        lax.psum_scatter(sum_gain_attn, ("ctx", "fsdp"), scatter_dimension=0, tiled=True),
        lax.psum_scatter(grad_qkv, ("ctx", "fsdp"), scatter_dimension=0, tiled=True),
        lax.psum_scatter(grad_out, ("ctx", "fsdp"), scatter_dimension=0, tiled=True),
        lax.psum_scatter(sum_gain_mlp, ("ctx", "fsdp"), scatter_dimension=0, tiled=True),
        lax.psum_scatter(grad_up, ("ctx", "fsdp"), scatter_dimension=0, tiled=True),
        lax.psum_scatter(grad_down, ("ctx", "fsdp"), scatter_dimension=0, tiled=True),
    )
    output = jnp.stack(outputs)[:, None]
    input_grad = jnp.stack(in_grads)[:, None]
    return (
        output,
        input_grad,
        summed[0],
        summed[1],
        summed[2],
        summed[3],
        summed[4],
        summed[5],
        summed[6],
    )


ORDER = (0, 2, 1, 3)


def sds(shape, dtype):
    return jax.ShapeDtypeStruct(shape, dtype)


def local(shape, dtype):
    return pltpu.VMEM(shape, dtype)


def near(x):
    return pltpu.with_memory_space_constraint(x, pltpu.VMEM)


class Chain:
    def __init__(self):
        self.last = None

    def __call__(self, kernel, outs, smem, args, scratch=(), name=None, far=(), after=(), weight=WEIGHT):
        count = len(smem) + len(far) + len(args)
        spec = pl.BlockSpec(memory_space=pltpu.VMEM)
        extra = () if self.last is None else (near(self.last),)
        extra = (*extra, *(near(a) for a in after))

        def body(*refs):
            kernel(*refs[:count], *refs[count + len(extra) :])

        results = pl.pallas_call(
            body,
            out_shape=tuple(outs),
            in_specs=[pl.BlockSpec(memory_space=pltpu.SMEM)] * len(smem)
            + [pl.BlockSpec(memory_space=pltpu.HBM)] * len(far)
            + [spec] * (len(args) + len(extra)),
            out_specs=tuple(spec for _ in outs),
            scratch_shapes=list(scratch),
            compiler_params=pltpu.CompilerParams(vmem_limit_bytes=VMEM_LIMIT),
            cost_estimate=pl.CostEstimate(flops=weight, bytes_accessed=weight // 10000, transcendentals=0),
            name=name,
        )(
            *smem, *(pltpu.with_memory_space_constraint(a, pltpu.HBM) for a in far), *(near(a) for a in args), *extra
        )
        if not isinstance(outs[0], jax.ShapeDtypeStruct):
            self.last = results[0]
        return results

    def hold(self, x, *after):
        (x,) = self(hold_kernel, (local(x.shape, x.dtype),), (), (x,), after=after, name="hold", weight=0)
        return x


def hold_kernel(x, out):
    out[...] = x[...]


def mm(left, right):
    return jnp.dot(left, right, preferred_element_type=F32)


def mm_t(left, right):
    return lax.dot_general(left, right, (((1,), (1,)), ((), ())), preferred_element_type=F32)


def t_mm(left, right):
    return lax.dot_general(left, right, (((0,), (0,)), ((), ())), preferred_element_type=F32)


def exchange(x, axis, size, mask):
    return lax.ppermute(x, axis, [(i, i ^ mask) for i in range(size)])


def rms_factor(values):
    return lax.rsqrt(jnp.mean(values * values, axis=-1, keepdims=True) + EPSILON)


def aligned(start, unit):
    return pl.multiple_of(start, unit)


def iota(shape, axis):
    return lax.broadcasted_iota(jnp.int32, shape, axis)


def picks(ids, routed, micro, tok_dev):
    index = routed[micro : micro + 1, :] - ids[0] * tok_dev
    shape = (tok_dev, routed.shape[1])
    return jnp.where(iota(shape, 0) == index, 1.0, 0.0)


def share_peers(ids, bit):
    return ids[1], ids[1] ^ 1, ids[1] ^ (2 + ((ids[0] >> bit) & 1))


def share_rows(c, f, bit):
    side = (c >> bit) & 1
    return f, f ^ 1, f ^ (2 + side), f ^ (3 - side)


def cut_qkv(ids, half, w_qkv, pieces, sem, first, by_y=True):
    width = w_qkv.shape[1] // 3
    copies = []
    peers = share_peers(ids, 0) if by_y else tuple(ids[1] ^ k for k in range(4))
    for k, (peer, piece) in enumerate(zip(peers, pieces)):
        for b in range(3):
            start = b * width + peer * (width // 4) + half * 128
            copies.append(
                pltpu.make_async_copy(
                    w_qkv.at[:, pl.ds(aligned(start, 128), 128)],
                    piece.at[:, pl.ds(b * 128, 128)],
                    sem.at[first + 3 * k + b],
                )
            )
    return copies


def front_kernel(ids, deal, tokens, w_qkv, routed, rowsx, p0, p1, p2, near_tokens, sem):
    micros, tok_dev, width = tokens.shape
    per = routed.shape[1]
    count = micros * per
    span = tok_dev // 2
    first = pltpu.make_async_copy(tokens, near_tokens, sem.at[0])
    first.start()
    copies = cut_qkv(ids, ids[0] >> 2, w_qkv, (p0, p1, p2), sem, 1)
    for copy in copies:
        copy.start()
    stored = routed[...]
    chunk = stored // span
    anchor = jnp.zeros_like(stored)
    for entry in range(deal.shape[0]):
        anchor = jnp.where(chunk == entry, deal[entry], anchor)
    place = ((anchor * span + stored % span) // BLOCK).astype(F32)
    rowsx[count:] = jnp.zeros((8, width), BF16)
    for micro in range(micros):
        rowsx[count + micro : count + micro + 1, :per] = place[micro : micro + 1].astype(BF16)
    first.wait()
    for micro in range(micros):
        pick = picks(ids, routed, micro, tok_dev).astype(BF16)
        rowsx[micro * per : (micro + 1) * per] = t_mm(pick, near_tokens[micro]).astype(BF16)
    for copy in copies:
        copy.wait()


def run(copies):
    for copy in copies:
        copy.start()
    for copy in copies:
        copy.wait()


def cut_up_kernel(ids, w_up, p0, p1, p2, sem):
    share = p0.shape[1]
    run(
        [
            pltpu.make_async_copy(
                w_up.at[:, pl.ds(aligned(peer * share, share), share)], piece, sem.at[k]
            )
            for k, (peer, piece) in enumerate(zip(share_peers(ids, 0), (p0, p1, p2)))
        ]
    )


def cut_rest_kernel(ids, w_qkv, v0, v1, v2, v3, sem):
    run(cut_qkv(ids, 1 - (ids[0] >> 2), w_qkv, (v0, v1, v2, v3), sem, 0, False))


def cot_kernel(ids, routed, cot, rowsx, both):
    micros, tok_dev = cot.shape[:2]
    per = routed.shape[1]
    start = rowsx.shape[0]
    both[:start] = rowsx[...]
    for micro in range(micros):
        pick = picks(ids, routed, micro, tok_dev).astype(BF16)
        both[start + micro * per : start + (micro + 1) * per] = t_mm(pick, cot[micro]).astype(BF16)


def rows_of(both):
    return both[: both.shape[0] // 2 - 4].astype(F32)


def cots_of(both):
    return both[both.shape[0] // 2 + 4 :].astype(F32)


def d_mlp_kernel(b0, b1, b2, b3, w_router, d_mlp, gate_out):
    count = gate_out.shape[1]
    for i, both in enumerate((b0, b1, b2, b3)):
        gate = jax.nn.sigmoid(jnp.sum(rows_of(both) * w_router[...], axis=1, keepdims=True))
        d_mlp[i * count : (i + 1) * count] = (gate * cots_of(both)).astype(BF16)
        gate_out[i] = gate


def head_masks():
    lanes = iota((1, 128), 1)
    low = jnp.where(lanes < 64, 1.0, 0.0)
    return low, 1.0 - low


def attend_kernel(
    ids, near_rows, far_rows, gain, w0, w1, w2, w3,
    far, own, stack, probs, norm1, place_col, result,
):
    c, f = ids[0], ids[1]
    micros, total = stack.shape[0], stack.shape[1]
    count = own.shape[1]
    per = count // micros
    eye = iota((per, 128), 0) == iota((per, 128), 1)
    step = count + 8
    for h, source in enumerate((near_rows, far_rows)):
        for b in range(4):
            rows = source[b * step : b * step + count].astype(F32)
            index = ((c >> 2) ^ h) * 4 + b
            norm1[pl.ds(aligned(index * count, 16), count)] = (
                rows * rms_factor(rows) * gain[...]
            ).astype(BF16)
            places = source[b * step + count : b * step + count + 8, :128].astype(F32)
            for m in range(micros):
                col = jnp.sum(jnp.where(eye, places[m : m + 1], 0.0), axis=1, keepdims=True)
                place_col[m, pl.ds(aligned(index * per, per), per), :] = jnp.broadcast_to(
                    col, (per, 128)
                )
    qkv = jnp.zeros((8 * count, 384), F32)
    for peer, w in zip(share_rows(c, f, 0), (w0, w1, w2, w3)):
        part = w.shape[0]
        qkv = qkv + mm(norm1[:, pl.ds(aligned(peer * part, part), part)], w[...])
    low = qkv.astype(BF16)
    for t in range(8):
        for m in range(micros):
            stack[m, t * per : (t + 1) * per, :] = low[
                t * count + m * per : t * count + (m + 1) * per
            ]
    big_eye = iota((total, total), 0) == iota((total, total), 1)
    masks = head_masks()
    for m in range(micros):
        q, k, v = stack[m, :, :128], stack[m, :, 128:256], stack[m, :, 256:384]
        mine = place_col[m, :, 0:1]
        theirs = jnp.sum(jnp.where(big_eye, mine, 0.0), axis=0, keepdims=True)
        visible = theirs <= mine
        attended = jnp.zeros((total, 128), F32)
        for h in range(2):
            scores = mm_t(q * masks[h].astype(BF16), k) * (HEAD_DIM**-0.5)
            scores = jnp.where(visible, scores, MASKED)
            top = jnp.max(scores, axis=1, keepdims=True)
            grown = jnp.exp(scores - top)
            weight = grown / jnp.sum(grown, axis=1, keepdims=True)
            probs[2 * m + h] = weight
            attended = attended + mm(weight.astype(BF16), v) * masks[h]
        result[m] = attended.astype(BF16)
        for k in range(8):
            out = far if k >= 4 else own
            out[k & 3, m * per : (m + 1) * per, :] = result[
                m, pl.ds(aligned((c ^ k) * per, per), per), :
            ]


def row_slot(f, s, count):
    k = s ^ f
    return aligned(((k & 1) * 2 + (k >> 1)) * count, 16)


def split_rows(full, send, keep):
    count = send.shape[1]
    for i in range(2):
        keep[i] = full[i * count : (i + 1) * count]
        send[i] = full[(2 + i) * count : (3 + i) * count].astype(BF16)


def block_place(ids, k, count, lanes):
    peer = ids[0] ^ k
    columns = aligned((peer >> 2) * lanes, 128)
    return pl.ds(row_slot(ids[1], peer & 3, count), count), pl.ds(columns, lanes)


def out_kernel(ids, b0, b1, b2, b3, w_out, attended, send, keep, full):
    count = b0.shape[1]
    for k, block in enumerate((b0, b1, b2, b3)):
        for far in range(2):
            attended[block_place(ids, k ^ (4 * far), count, 128)] = block[far]
    full[...] = mm(attended[...], w_out[...])
    split_rows(full, send, keep)


def add_both_kernel(keep, received, total):
    total[...] = (keep[...] + received[...].astype(F32)).astype(BF16)


def add_own_kernel(keep, received, send2, keep2):
    send2[...] = (keep[1] + received[1].astype(F32)).astype(BF16)
    keep2[...] = keep[0] + received[0].astype(F32)


def mid_kernel(low, received, both0, both1, gain, attn, norm2):
    for i, both in enumerate((both0, both1)):
        value = low[i].astype(F32) + received[1 - i].astype(F32)
        attn[i] = value
        mid = rows_of(both) + value
        norm2[i] = (mid * rms_factor(mid) * gain[...]).astype(BF16)


def mlp_kernel(
    ids, n0, n1, d_mlp, u0, u1, u2, u3, w_down,
    send, keep, act_send, d_send, act_keep, d_keep, norm2, act, d_hidden, back,
):
    c = ids[0]
    part = u0.shape[0]
    count = n0.shape[1]
    shares = tuple(zip(share_rows(ids[0], ids[1], 0), (u0, u1, u2, u3)))
    for i in range(2):
        norm2[i * count : (i + 1) * count] = n0[i]
        norm2[(2 + i) * count : (3 + i) * count] = n1[i]
    hidden = jnp.zeros(act.shape, F32)
    for peer, u in shares:
        hidden = hidden + mm(norm2[:, pl.ds(aligned(peer * part, part), part)], u[...])
    d_act = mm_t(d_mlp[...], w_down[...])
    phi = 0.5 * (1.0 + lax.erf(hidden * (0.5**0.5)))
    act[...] = (hidden * phi).astype(BF16)
    slope = phi + hidden * jnp.exp(-0.5 * hidden * hidden) * ((2.0 * math.pi) ** -0.5)
    d_hidden[...] = (d_act * slope).astype(BF16)
    for i, (some_act, some_d) in enumerate(((act_keep, d_keep), (act_send, d_send))):
        for high in range(2):
            start = aligned(high * 512 + (((c >> 1) & 1) ^ i) * 256, 128)
            some_act[:, high * 256 : (high + 1) * 256] = act[:, pl.ds(start, 256)]
        some_d[...] = d_hidden[:, pl.ds(aligned(((c & 1) ^ i) * 512, 128), 512)]
    for peer, u in shares:
        back[:, pl.ds(aligned(peer * part, part), part)] = mm_t(d_hidden[...], u[...])
    split_rows(back, send, keep)


def mlp_out_kernel(act, w_down, attn, gate, b0, b1, b2, b3, send, keep, router, full):
    full[...] = mm(act[...], w_down[...])
    split_rows(full, send, keep)
    count = gate.shape[1]
    total = jnp.zeros(router.shape, F32)
    for i, both in enumerate((b0, b1, b2, b3)):
        own = slice(i * count, (i + 1) * count)
        part = jnp.sum(cots_of(both) * (attn[own] + full[own]), axis=1, keepdims=True)
        part = part * gate[i] * (1.0 - gate[i])
        total = total + jnp.sum(rows_of(both) * part, axis=0, keepdims=True)
    router[...] = total


def pick_rows(c, peer, share, out, lanes):
    @pl.when(peer == (c >> 1))
    def _():
        out[:, lanes] = share[pl.ds(aligned((c & 1) * 128, 128), 128), :]


def pick_kernel(ids, *refs):
    shares, (up_rows, qkv_rows) = refs[:12], refs[12:]
    c, f = ids[0], ids[1]
    for peer, u in zip(share_rows(c, f, 0), shares[:4]):
        pick_rows(c, peer, u, up_rows, slice(None))
    for peer, a in zip(share_rows(c, f, 0), shares[4:8]):
        pick_rows(c, peer, a, qkv_rows, slice(0, 384))
    for k, b in enumerate(shares[8:]):
        pick_rows(c, f ^ k, b, qkv_rows, slice(384, 768))


def chunk(f, q):
    return pl.ds(aligned((f ^ q) * 32, 32), 32)


def grad_up_kernel(ids, norm2, near_a, near_b, d_own, d_near, send, keep, rows, columns):
    count = norm2.shape[0]
    half = count // 2
    rows[:count] = norm2[...]
    for i in range(2):
        rows[count + i * (half // 2) : count + (i + 1) * (half // 2)] = near_a[i]
        rows[count + half + i * (half // 2) : count + half + (i + 1) * (half // 2)] = near_b[i]
    columns[:count] = d_own[...]
    columns[count:] = d_near[...]
    for place, (target, index) in enumerate(((keep, 0), (send, 0), (keep, 1), (send, 1))):
        kk = (0, 1, 2, 3)[place]
        start = aligned(((ids[0] >> 1) ^ kk) * 256, 128)
        value = t_mm(rows[:, pl.ds(start, 256)], columns[...])
        for owner in range(2):
            for q in range(4):
                at = pl.ds(aligned(((ids[0] & 1) ^ owner) * 128 + (ids[1] ^ q) * 32, 32), 32)
                piece = value[owner * 128 + q * 32 : owner * 128 + (q + 1) * 32]
                target[index, at] = piece.astype(target.dtype)


def grad_down_kernel(ids, d_mlp, near_a, near_b, a_own, a_near, send, keep, rows, columns):
    count = d_mlp.shape[0]
    half = count // 2
    rows[:count] = d_mlp[...]
    rows[count : count + half] = near_a[...]
    rows[count + half :] = near_b[...]
    columns[:count] = a_own[...]
    columns[count:] = a_near[...]
    c = ids[0]
    for target, index, k in ((keep, 0, 0), (send, 0, 1), (keep, 1, 4), (send, 1, 5)):
        start = aligned(((c >> 2) ^ (k >> 2)) * 256 + ((c & 1) ^ (k & 1)) * 128, 128)
        value = t_mm(columns[:, pl.ds(start, 128)], rows[...])
        target[index] = value.astype(target.dtype)


def grad_attn_kernel(
    ids, norm1, b0, b1, b2, b3, b4, b5, b6, b7, attended, d_attn, router,
    keep, send1, send2, send3, joined, full,
):
    count = b0.shape[0]
    for k, block in enumerate((b0, b1, b2, b3, b4, b5, b6, b7)):
        joined[pl.ds(aligned((ids[0] ^ k) * count, 16), count)] = block[...]
    full[...] = t_mm(attended[...], d_attn[...])
    for k in range(8):
        target, index = (keep, send1, send2, send3)[k & 3], k >> 2
        owner = ids[0] ^ k
        start = aligned(owner * 128, 128)
        value = t_mm(norm1[:, pl.ds(start, 128)], joined[...])
        for q in range(4):
            piece = value[q * 32 : (q + 1) * 32]
            target[index, chunk(ids[1], q), :384] = piece.astype(target.dtype)
            rows = full[pl.ds(aligned(owner * 32, 32), 32), q * 256 : (q + 1) * 256]
            target[index, q * 32 : (q + 1) * 32, 384:640] = rows.astype(target.dtype)
        target[index, 128:136, :] = jnp.zeros((8, 640), target.dtype)
        share = jnp.broadcast_to(router[:, pl.ds(start, 128)], (8, 128))
        target[index, 128:136, 384:512] = share.astype(target.dtype)


def sum_attn_kernel(keep, got1, got2, got3, send, mine):
    for index, target in ((0, mine), (1, send)):
        total = (keep[index] + got1[index].astype(F32)) + (
            got2[index].astype(F32) + got3[index].astype(F32)
        )
        target[0] = total.astype(target.dtype)


def d_attn_kernel(low, received, attn, both0, both1, gate, gain, d_mid_out, d_attn):
    for i, both in enumerate((both0, both1)):
        mid = rows_of(both) + attn[i]
        r2 = rms_factor(mid)
        d_norm2 = low[i].astype(F32) + received[1 - i].astype(F32)
        t2 = d_norm2 * gain[...]
        d_mid = r2 * t2 - mid * (r2 * r2 * r2) * jnp.mean(t2 * mid, axis=1, keepdims=True)
        d_attn[i] = (gate[i] * cots_of(both) + d_mid).astype(BF16)
        if i == 0:
            d_mid_out[...] = d_mid


def d_attended_kernel(ids, d0, d1, w_out, far, own, d_attn, d_att):
    count = d0.shape[1]
    for i in range(2):
        d_attn[i * count : (i + 1) * count] = d0[i]
        d_attn[(2 + i) * count : (3 + i) * count] = d1[i]
    d_att[...] = mm_t(d_attn[...], w_out[...])
    for k in range(8):
        block = far if k >= 4 else own
        block[k & 3] = d_att[block_place(ids, k, count, 128)].astype(BF16)


def attend_back_kernel(ids, *refs):
    blocks, (stack, probs), outs, (d_stack, result) = refs[:4], refs[4:6], refs[6:14], refs[14:]
    micros, total = stack.shape[0], stack.shape[1]
    count = outs[0].shape[0]
    per = count // micros
    masks = head_masks()
    for m in range(micros):
        rows = slice(m * per, (m + 1) * per)
        for k in range(8):
            d_stack[pl.ds(aligned((ids[0] ^ k) * per, per), per), :] = blocks[k & 3][k >> 2, rows]
        q, k, v = stack[m, :, :128], stack[m, :, 128:256], stack[m, :, 256:384]
        d_out = d_stack[...]
        d_q = jnp.zeros((total, 128), F32)
        d_k = jnp.zeros((total, 128), F32)
        d_v = jnp.zeros((total, 128), F32)
        for h in range(2):
            weight = probs[2 * m + h]
            d_probs = mm_t(d_out * masks[h].astype(BF16), v)
            inner = jnp.sum(weight * d_probs, axis=1, keepdims=True)
            d_scores = (weight * (d_probs - inner)).astype(BF16)
            d_q = d_q + mm(d_scores, k) * masks[h]
            d_k = d_k + t_mm(d_scores, q) * masks[h]
            d_v = d_v + t_mm(weight.astype(BF16), d_out) * masks[h]
        result[m, :, :128] = (d_q * (HEAD_DIM**-0.5)).astype(BF16)
        result[m, :, 128:256] = (d_k * (HEAD_DIM**-0.5)).astype(BF16)
        result[m, :, 256:384] = d_v.astype(BF16)
        for k in range(8):
            outs[k][rows] = result[m, pl.ds(aligned((ids[0] ^ k) * per, per), per), :]


def d_norm1_kernel(
    ids, d0, d1, d2, d3, d4, d5, d6, d7, a0, a1, a2, a3, b0, b1, b2, b3,
    send, keep, d_qkv, full,
):
    c, f = ids[0], ids[1]
    count = d0.shape[0]
    part = a0.shape[0]
    for k, block in enumerate((d0, d1, d2, d3, d4, d5, d6, d7)):
        rows = pl.ds(row_slot(f, (c ^ k) & 3, count), count)
        d_qkv[rows, (k >> 2) * 384 : (k >> 2) * 384 + 384] = block[...]
    for peer, a in zip(share_rows(c, f, 0), (a0, a1, a2, a3)):
        full[:, pl.ds(aligned(peer * part, part), part)] = mm_t(d_qkv[:, :384], a[...])
    for k, b in enumerate((b0, b1, b2, b3)):
        columns = pl.ds(aligned((f ^ k) * part, part), part)
        full[:, columns] = full[:, columns] + mm_t(d_qkv[:, 384:], b[...])
    split_rows(full, send, keep)


def place_rows(ids, routed, micro, source, rows, out):
    tok_dev = source.shape[0]
    pick = picks(ids, routed, micro, tok_dev)
    changed = jnp.sum(pick, axis=1, keepdims=True) > 0.5
    placed = mm(pick.astype(BF16), rows)
    out[...] = jnp.where(changed, placed, source[...].astype(F32)).astype(BF16)


def output_kernel(
    ids, routed, keep, received, attn, both, gate, tokens, d_logit_out, output,
):
    count = keep.shape[0]
    micros = tokens.shape[0]
    per = count // micros
    branch = attn[0] + keep[...] + received[...].astype(F32)
    rows = rows_of(both)
    open_gate = gate[0]
    d_logit = (
        jnp.sum(cots_of(both) * branch, axis=1, keepdims=True)
        * open_gate
        * (1.0 - open_gate)
    )
    d_logit_out[...] = d_logit
    result = (rows + open_gate * branch).astype(BF16)
    for micro in range(micros):
        own = result[micro * per : (micro + 1) * per]
        place_rows(ids, routed, micro, tokens.at[micro], own, output.at[micro])


def input_grad_kernel(
    ids, routed, keep, received, d_mid, both, d_logit, w_router, gain, cot, input_grad,
):
    count = keep.shape[0]
    micros = cot.shape[0]
    per = count // micros
    rows = rows_of(both)
    r1 = rms_factor(rows)
    t1 = (keep[...] + received[...].astype(F32)) * gain[...]
    d_rows = (
        cots_of(both)
        + d_mid[...]
        + r1 * t1
        - rows * (r1 * r1 * r1) * jnp.mean(t1 * rows, axis=1, keepdims=True)
        + d_logit[...] * w_router[...]
    ).astype(BF16)
    for micro in range(micros):
        own = d_rows[micro * per : (micro + 1) * per]
        place_rows(ids, routed, micro, cot.at[micro], own, input_grad.at[micro])


def as_row(column):
    count = column.shape[0]
    eye = iota((count, count), 0) == iota((count, count), 1)
    return jnp.sum(jnp.where(eye, column, 0.0), axis=0, keepdims=True)


def owned(ids, vector, count):
    start = (4 * ids[0] + ids[1]) * count
    shape = (count, vector.shape[1])
    hit = iota(shape, 1) == iota(shape, 0) + start
    return jnp.sum(jnp.where(hit, vector[...], 0.0), axis=1, keepdims=True)


def join_up_kernel(ids, p0, p1, p2, p3, gain, out, grad_gain):
    rows, part = out.shape[0], out.shape[1] // 4
    total = jnp.zeros((rows, 1), F32)
    for k, piece in enumerate((p0, p1, p2, p3)):
        out[:, pl.ds(aligned((ids[1] ^ k) * part, part), part)] = piece[:, :part].astype(F32)
        total = total + piece[:, part : part + 128].astype(F32)[:, :1]
    grad_gain[...] = as_row(total / owned(ids, gain, rows))


def join_qkv_kernel(ids, p0, p1, p2, p3, gain, out, grad_gain, grad_router):
    rows, width = out.shape[0], out.shape[1] // 3
    part = width // 4
    total = jnp.zeros((rows, 1), F32)
    router = jnp.zeros((rows, 1), F32)
    for k, piece in enumerate((p0, p1, p2, p3)):
        for half in range(2):
            for b in range(3):
                start = b * width + (ids[1] ^ k) * part + ((ids[0] >> 2) ^ half) * 128
                out[:, pl.ds(aligned(start, 128), 128)] = piece[
                    :, (3 * half + b) * 128 : (3 * half + b + 1) * 128
                ].astype(F32)
        total = total + piece[:, 768:896].astype(F32)[:, :1]
        router = router + piece[:, 896:1024].astype(F32)[:, :1]
    grad_gain[...] = as_row(total / owned(ids, gain, rows))
    grad_router[...] = as_row(router)


def join_down_kernel(block, out):
    out[...] = block[...].astype(F32)


def hop2_kernel(keep_u, got_u, keep_d, got_d, send, own_u, own_d):
    for i in range(2):
        total = keep_u[i] + got_u[i].astype(F32)
        half, width = total.shape[0] // 2, total.shape[1]
        if i:
            send[0, :, :width] = total[:half].astype(BF16)
            send[0, :, width:] = total[half:].astype(BF16)
        else:
            own_u[...] = total
    own_d[...] = keep_d[0] + got_d[0].astype(F32)
    send[1] = (keep_d[1] + got_d[1].astype(F32)).astype(BF16)


def hop3_kernel(own_u, own_d, got, send, mine, down):
    half, width = own_u.shape[0] // 2, own_u.shape[1]
    mine[...] = own_u[:half] + got[0, :, :width].astype(F32)
    send[...] = (own_u[half:] + got[0, :, width:].astype(F32)).astype(BF16)
    down[...] = (own_d[...] + got[1].astype(F32)).astype(BF16)


def up_pieces_kernel(ids, mine, other, w_rows, c0, c1, c2, c3):
    rows, half = c0.shape[0], mine.shape[1]
    y = ids[0] & 1
    for k, piece in enumerate((c0, c1, c2, c3)):
        own = slice(k * rows, (k + 1) * rows)
        weights = pl.ds(aligned((ids[1] ^ k) * rows, rows), rows)
        total = jnp.zeros((rows, 1), F32)
        for side, value in ((y, mine[own]), (1 - y, other[own].astype(F32))):
            columns = pl.ds(aligned(side * half, 128), half)
            piece[:, columns] = value.astype(BF16)
            total = total + jnp.sum(
                value * w_rows[weights, columns].astype(F32), axis=1, keepdims=True
            )
        piece[:, 2 * half :] = jnp.broadcast_to(total, (rows, 128)).astype(BF16)


def pieces_kernel(ids, mine, got, w_rows, c0, c1, c2, c3, out):
    rows = c0.shape[0]
    router = mine[0, 128:129, 384:512] + got[0, 128:136, 384:512].astype(F32)[0:1]
    for k, piece in enumerate((c0, c1, c2, c3)):
        own = slice(k * rows, (k + 1) * rows)
        first = (ids[1] ^ k) * rows
        weights = pl.ds(aligned(first, rows), rows)
        a, b = mine[0, own, :384], got[0, own, :384].astype(F32)
        piece[:, :384] = a.astype(BF16)
        piece[:, 384:768] = b.astype(BF16)
        total = jnp.sum(a * w_rows[weights, :384].astype(F32), axis=1, keepdims=True)
        total = total + jnp.sum(b * w_rows[weights, 384:].astype(F32), axis=1, keepdims=True)
        piece[:, 768:896] = jnp.broadcast_to(total, (rows, 128)).astype(BF16)
        hit = iota((rows, 128), 1) == iota((rows, 128), 0) + first
        share = jnp.sum(jnp.where(hit, router, 0.0), axis=1, keepdims=True)
        piece[:, 896:] = jnp.broadcast_to(share, (rows, 128)).astype(BF16)
        out[:, k * 256 : (k + 1) * 256] = mine[0, own, 384:640] + got[0, own, 384:640].astype(F32)


def all_rows_sum(call, send, keep, after=()):
    received = exchange(send, "fsdp", 4, 1)
    (low,) = call(
        add_both_kernel, (local(keep.shape, BF16),), (), (keep, received), name="add_both", after=after
    )
    return low, exchange(low, "fsdp", 4, 2)


def own_rows_sum(call, send, keep):
    received = exchange(send, "fsdp", 4, 1)
    shape = keep.shape[1:]
    send2, keep2 = call(
        add_own_kernel, (local(shape, BF16), local(shape, F32)), (), (keep, received), name="add_own"
    )
    return keep2, exchange(send2, "fsdp", 4, 2)


def swap_blocks(blocks):
    got = {k: exchange(blocks[k], "ctx", 8, k) for k in (7, 6, 5, 4, 3, 2, 1)}
    return (blocks[0], *(got[k] for k in range(1, 8)))


def swap_across(across, bit):
    return lax.ppermute(
        across, ("ctx", "fsdp"),
        [(4 * a + b, 4 * a + (b ^ (2 + ((a >> bit) & 1)))) for a in range(8) for b in range(4)],
    )


def pair_kernel(own, far, *outs):
    for k, out in enumerate(outs):
        out[0] = own[k]
        out[1] = far[k]


def swap_in_two(call, own, far, *after):
    came = exchange(far, "ctx", 8, 4)
    shape = (2, *own.shape[1:])
    pairs = call(pair_kernel, (local(shape, own.dtype),) * 4, (), (own, came), name="pair", after=after)
    return (pairs[0], *(exchange(pairs[k], "ctx", 8, k) for k in (1, 2, 3)))


def swap_pieces(pieces):
    return (pieces[0], *(exchange(pieces[k], "fsdp", 4, k) for k in (1, 2, 3)))


def shards_8x4(
    tokens, w_router, gain_attn, w_qkv, w_out, gain_mlp, w_up, w_down, routed, deal, cotangent
):
    micros, tok_dev, width = tokens.shape[0], tokens.shape[2], tokens.shape[3]
    per = routed.shape[2]
    count = micros * per
    total = 8 * per
    part = width // 4
    hidden = w_down.shape[0]
    c, f = lax.axis_index("ctx"), lax.axis_index("fsdp")
    ids = jnp.stack([c, f]).astype(jnp.int32)
    tok, cot, routed = tokens[:, 0], cotangent[:, 0], routed[:, 0]
    w_router, gain_attn, gain_mlp = (
        w_router.reshape(1, width), gain_attn.reshape(1, width), gain_mlp.reshape(1, width),
    )
    rows_bf, rows_f = local((count, width), BF16), local((count, width), F32)
    pair_bf, pair_f = local((2, count, width), BF16), local((2, count, width), F32)
    all_bf, all_quarter = local((4 * count, width), BF16), local((4 * count, part), BF16)
    hidden_bf = local((4 * count, hidden), BF16)
    vector = local((1, width), F32)
    dma = pltpu.SemaphoreType.DMA
    call = Chain()

    rowsx, *w_parts = call(
        front_kernel,
        (local((count + 8, width), BF16), *(local((part, 384), BF16),) * 3),
        (ids, deal), (routed,), far=(tok, w_qkv),
        scratch=[pltpu.VMEM(tok.shape, BF16), dma((10,))], name="front",
    )
    turn = [(4 * a + b, 4 * ((a & 4) | b) + (a & 3)) for a in range(8) for b in range(4)]
    turned = lax.ppermute(rowsx, ("ctx", "fsdp"), turn)
    turned_far = exchange(turned, "ctx", 8, 4)
    w_mine, w_beside, w_across = w_parts
    w_across = swap_across(w_across, 0)
    up_mine, up_beside, up_across = call(
        cut_up_kernel, (local((part, hidden), BF16),) * 3, (ids,), (), far=(w_up,),
        scratch=[dma((3,))], name="cut_up", weight=0,
    )
    near_rows = lax.all_gather(turned, "fsdp", axis=0, tiled=True)
    far_rows = lax.all_gather(turned_far, "fsdp", axis=0, tiled=True)
    w_across = call.hold(w_across, near_rows)
    w_parts = (w_mine, exchange(w_beside, "fsdp", 4, 1), w_across, exchange(w_across, "ctx", 8, 1))
    up_beside, up_across = exchange(up_beside, "fsdp", 4, 1), swap_across(up_across, 0)
    far_heads, heads, stack, probs, norm1 = call(
        attend_kernel,
        (
            *(local((4, count, 128), BF16),) * 2, local((micros, total, 384), BF16),
            local((2 * micros, total, total), F32), local((8 * count, width), BF16),
        ),
        (ids,), (near_rows, far_rows, gain_attn, *w_parts),
        scratch=[pltpu.VMEM((micros, total, 128), F32), pltpu.VMEM((micros, total, 128), BF16)],
        name="attend",
    )
    (both,) = call(
        cot_kernel, (local((2 * count + 8, width), BF16),), (ids,), (routed, cot, rowsx), name="cot_rows",
        weight=0,
    )
    both_x, both_c = exchange(both, "fsdp", 4, 2), exchange(both, "fsdp", 4, 1)
    both_xc = exchange(both_x, "fsdp", 4, 1)
    rest = call(
        cut_rest_kernel, (local((part, 384), BF16),) * 4, (ids,), (), far=(w_qkv,),
        scratch=[dma((12,))], name="cut_rest", weight=0,
    )
    heads = swap_in_two(call, heads, far_heads)
    attended, send, keep, attn_part = call(
        out_kernel, (all_quarter, pair_bf, pair_f, local((4 * count, width), F32)),
        (ids,), (*heads, w_out), name="attn_out", after=(up_across,),
    )
    up_parts = (up_mine, up_beside, up_across, exchange(up_across, "ctx", 8, 1))
    rest = swap_pieces(rest)
    low, received = all_rows_sum(call, send, keep)
    d_mlp, gate = call(
        d_mlp_kernel, (all_bf, local((4, count, 1), F32)), (),
        (both, both_x, both_c, both_xc, w_router), name="d_mlp", weight=0,
    )
    d_mlp_a = exchange(d_mlp[: 2 * count], "ctx", 8, 2)
    d_mlp_b = exchange(d_mlp_a, "fsdp", 4, 1)
    attn, norm2 = call(
        mid_kernel, (pair_f, pair_bf), (), (low, received, both, both_x, gain_mlp), name="mid",
    )
    norm2_a = exchange(norm2, "ctx", 8, 1)
    norm2_b = exchange(norm2_a, "fsdp", 4, 1)
    half_bf = local((4 * count, hidden // 2), BF16)
    send, keep, act_send, d_send, act_keep, d_keep, norm2, act = call(
        mlp_kernel, (pair_bf, pair_f, half_bf, half_bf, half_bf, half_bf, all_bf, hidden_bf), (ids,),
        (norm2, exchange(norm2, "fsdp", 4, 1), d_mlp, *up_parts, w_down),
        scratch=[pltpu.VMEM((4 * count, hidden), BF16), pltpu.VMEM((4 * count, width), F32)],
        name="mlp",
    )
    d_near, act_near = exchange(d_send, "ctx", 8, 1), exchange(act_send, "ctx", 8, 2)
    low, received = all_rows_sum(call, send, keep, (norm2_a, d_mlp_a))
    d_mid, d_attn = call(
        d_attn_kernel, (rows_f, pair_bf), (),
        (low, received, attn, both, both_x, gate, gain_mlp), name="d_attn",
        after=(d_near, act_near),
    )
    far_heads, d_heads, d_attn = call(
        d_attended_kernel, (*(local((4, count, 128), BF16),) * 2, all_bf), (ids,),
        (d_attn, exchange(d_attn, "fsdp", 4, 1), w_out),
        scratch=[pltpu.VMEM((4 * count, part), F32)], name="d_attended",
    )
    send_u, keep_u = call(
        grad_up_kernel, (local((2, 256, hidden // 2), BF16), local((2, 256, hidden // 2), F32)), (ids,),
        (norm2, norm2_a, norm2_b, d_keep, d_near), name="grad_up", weight=0,
        scratch=[pltpu.VMEM((8 * count, width), BF16), pltpu.VMEM((8 * count, hidden // 2), BF16)],
    )
    send_d, keep_d = call(
        grad_down_kernel, (local((2, 128, width), BF16), local((2, 128, width), F32)), (ids,),
        (d_mlp, d_mlp_a, d_mlp_b, act_keep, act_near), name="grad_down", weight=0,
        scratch=[pltpu.VMEM((8 * count, width), BF16), pltpu.VMEM((8 * count, hidden // 2), BF16)],
    )
    got_u, got_d = exchange(send_u, "ctx", 8, 2), exchange(send_d, "ctx", 8, 1)
    d_heads = swap_in_two(call, d_heads, far_heads)
    d_blocks = call(
        attend_back_kernel, (local((count, 384), BF16),) * 8, (ids,), (*d_heads, stack, probs),
        scratch=[pltpu.VMEM((total, 128), BF16), pltpu.VMEM((micros, total, 384), BF16)],
        name="attend_back", after=(*rest[1:], got_u, got_d),
    )
    d_own = swap_blocks(d_blocks)
    send_z, own_u, own_d = call(
        hop2_kernel,
        (local((2, 128, width), BF16), local((256, hidden // 2), F32), local((128, width), F32)),
        (), (keep_u, got_u, keep_d, got_d), name="hop2", weight=0,
    )
    got_z = exchange(send_z, "ctx", 8, 4)
    owners = [(4 * a + b, 4 * (2 * b + a // 4) + a % 4) for a in range(8) for b in range(4)]
    send_m, keep_m, router = call(
        mlp_out_kernel, (pair_bf, pair_f, vector), (),
        (act, w_down, attn_part, gate, both, both_x, both_c, both_xc), name="mlp_out", weight=0,
        scratch=[pltpu.VMEM((4 * count, width), F32)],
    )
    part_bf = local((2, 136, 640), BF16)
    keep_q, *send_q = call(
        grad_attn_kernel, (local((2, 136, 640), F32), part_bf, part_bf, part_bf), (ids,),
        (norm1, *d_blocks, attended, d_attn, router), name="grad_attn", weight=0,
        scratch=[pltpu.VMEM((8 * count, 384), BF16), pltpu.VMEM((part, width), F32)],
    )
    got_q = [exchange(x, "ctx", 8, k + 1) for k, x in enumerate(send_q)]
    send, keep = call(
        d_norm1_kernel, (pair_bf, pair_f), (ids,),
        (*d_own, *w_parts, *rest), name="d_norm1",
        scratch=[pltpu.VMEM((4 * count, 768), BF16), pltpu.VMEM((4 * count, width), F32)],
    )
    keep, received = own_rows_sum(call, send, keep)
    keep_m, received_m = own_rows_sum(call, send_m, keep_m)
    send_u, mine_u, down = call(
        hop3_kernel,
        (local((128, hidden // 2), BF16), local((128, hidden // 2), F32), local((128, width), BF16)),
        (), (own_u, own_d, got_z), name="hop3", weight=0,
    )
    down = lax.ppermute(down, ("ctx", "fsdp"), owners)
    other_u = exchange(send_u, "ctx", 8, 1)
    send_q, keep_q = call(
        sum_attn_kernel, (local((1, 136, 640), BF16), local((1, 136, 640), F32)), (),
        (keep_q, *got_q), name="sum_attn", weight=0,
    )
    got_q = exchange(send_q, "ctx", 8, 4)
    d_logit, output = call(
        output_kernel, (local((count, 1), F32), sds(tok.shape, BF16)), (ids,),
        (routed, keep_m, received_m, attn, both, gate, tok), name="output", weight=0,
    )
    (input_grad,) = call(
        input_grad_kernel, (sds(cot.shape, BF16),), (ids,),
        (routed, keep, received, d_mid, both, d_logit, w_router, gain_attn, cot), name="input_grad",
        weight=0,
    )
    w_up_rows, w_qkv_rows = call(
        pick_kernel, (local((128, hidden), BF16), local((128, 768), BF16)), (ids,),
        (*up_parts, *w_parts, *rest), name="pick", weight=0,
    )
    chunks = call(
        up_pieces_kernel, (local((32, hidden + 128), BF16),) * 4, (ids,), (mine_u, other_u, w_up_rows),
        name="up_pieces",
    )
    chunks = swap_pieces(chunks)
    *qkv_chunks, grad_out = call(
        pieces_kernel, (local((32, 1024), BF16),) * 4 + (local((32, width), F32),), (ids,),
        (keep_q, got_q, w_qkv_rows), name="qkv_pieces",
    )
    qkv_chunks = swap_pieces(qkv_chunks)
    grad_out = lax.ppermute(grad_out, ("ctx", "fsdp"), owners)
    (grad_down,) = call(
        join_down_kernel, (sds((128, width), F32),), (), (down,), name="join_down"
    )
    row = sds((1, 32), F32)
    grad_up, grad_gain_mlp = call(
        join_up_kernel, (sds((32, 4 * hidden), F32), row), (ids,), (*chunks, gain_mlp), name="join_up"
    )
    grad_qkv, grad_gain_attn, grad_router = call(
        join_qkv_kernel, (sds((32, 3 * width), F32), row, row), (ids,), (*qkv_chunks, gain_attn),
        name="join_qkv",
    )
    return (
        output[:, None], input_grad[:, None], grad_router[0], grad_gain_attn[0], grad_qkv, grad_out,
        grad_gain_mlp[0], grad_up, grad_down,
    )


def solution(mesh):
    placed = (
        P(None, "fsdp", "ctx", None),
        P(),
        P(),
        P("fsdp", None),
        P("fsdp", None),
        P(),
        P("fsdp", None),
        P("fsdp", None),
        P(None, "fsdp", "ctx"),
        P(),
        P(None, "fsdp", "ctx", None),
    )
    fits = mesh.shape["ctx"] == 8 and mesh.shape["fsdp"] == 4
    return jax.shard_map(
        shards_8x4 if fits else shards,
        mesh=mesh,
        in_specs=placed,
        out_specs=(
            P(None, "fsdp", "ctx", None),
            P(None, "fsdp", "ctx", None),
            P(("ctx", "fsdp")),
            P(("ctx", "fsdp")),
            P(("ctx", "fsdp"), None),
            P(("ctx", "fsdp"), None),
            P(("ctx", "fsdp")),
            P(("ctx", "fsdp"), None),
            P(("ctx", "fsdp"), None),
        ),
        check_vma=False,
    )
```

```python
import math

import jax
import jax.numpy as jnp
from jax import lax
from jax.experimental import pallas as pl
from jax.experimental.pallas import tpu as pltpu
from jax.sharding import PartitionSpec as P

HEADS = 16
HEAD_DIM = 64
BLOCK = 256


EPSILON = 1e-06
MASKED = -1e30
HIGHEST = lax.Precision.HIGHEST
BF16, F32 = jnp.bfloat16, jnp.float32
VMEM_LIMIT = 24 * 2**20
WEIGHT = 10**10


def rms_norm(values, gain):
    factor = lax.rsqrt(jnp.mean(values * values, axis=-1, keepdims=True) + EPSILON)
    return values * factor * gain


def exact_gelu(values):
    return jax.nn.gelu(values, approximate=False)


def fetch(w_qkv, w_out, w_up, w_down):
    return (
        lax.all_gather(w_qkv, "fsdp", axis=0, tiled=True),
        lax.all_gather(w_out, "fsdp", axis=0, tiled=True),
        lax.all_gather(w_up, "fsdp", axis=0, tiled=True),
        lax.all_gather(w_down, "fsdp", axis=0, tiled=True),
    )


def lookup(table, index):
    hits = index[..., None] == jnp.arange(table.shape[0], dtype=jnp.int32)
    return jnp.sum(jnp.where(hits, table, 0), axis=-1)


def outer_sum(left, right):
    return lax.dot_general(
        left, right, (((0,), (0,)), ((), ())), preferred_element_type=jnp.float32
    )


def gather_rows(pieces, column):
    return jnp.concatenate([piece[column] for piece in pieces], axis=0)


def shards(
    tokens, w_router, gain_attn, w_qkv, w_out, gain_mlp, w_up, w_down, routed, deal, cotangent
):
    micros, tok_dev, width = (tokens.shape[0], tokens.shape[2], tokens.shape[3])
    span = tok_dev // 2
    rank = lax.axis_index("ctx")
    storage = routed[:, 0, :]
    local_rows = storage - rank * tok_dev
    anchor = lookup(deal, storage // span) * span + storage % span
    own_blocks = anchor // BLOCK
    all_blocks = lax.all_gather(own_blocks, "ctx", axis=1, tiled=True)
    factor = HEAD_DIM ** (-0.5)
    outputs, in_grads, kept = ([], [], [])
    sum_router = jnp.zeros((width,), jnp.float32)
    sum_gain_attn = jnp.zeros((width,), jnp.float32)
    sum_gain_mlp = jnp.zeros((width,), jnp.float32)
    for micro in range(micros):
        full_qkv, full_out, full_up, full_down = fetch(w_qkv, w_out, w_up, w_down)
        resid = tokens[micro, 0].astype(jnp.float32)
        grad_in = cotangent[micro, 0].astype(jnp.float32)
        rows_index = local_rows[micro]
        rows = jnp.take(resid, rows_index, axis=0)
        count = rows.shape[0]
        gate = jax.nn.sigmoid(jnp.dot(rows, w_router, precision=HIGHEST))
        norm1, norm1_back = jax.vjp(rms_norm, rows, gain_attn)
        norm1_low = norm1.astype(jnp.bfloat16)
        qkv = jnp.dot(norm1_low, full_qkv, preferred_element_type=jnp.float32).astype(jnp.bfloat16)
        queries = qkv[:, :width]
        keys_local = qkv[:, width : 2 * width]
        values_local = qkv[:, 2 * width :]
        keys_all, values_all = (
            lax.all_gather(keys_local, "ctx", axis=0, tiled=True),
            lax.all_gather(values_local, "ctx", axis=0, tiled=True),
        )
        total = keys_all.shape[0]
        query_heads = queries.reshape(count, HEADS, HEAD_DIM)
        key_heads = keys_all.reshape(total, HEADS, HEAD_DIM)
        value_heads = values_all.reshape(total, HEADS, HEAD_DIM)
        visible = all_blocks[micro][None, :] <= own_blocks[micro][:, None]
        scores = (
            jnp.einsum("qhd,khd->hqk", query_heads, key_heads, preferred_element_type=jnp.float32)
            * factor
        )
        scores = jnp.where(visible[None], scores, MASKED)
        probs = jax.nn.softmax(scores, axis=-1)
        probs_low = probs.astype(jnp.bfloat16)
        attended = jnp.einsum(
            "hqk,khd->qhd", probs_low, value_heads, preferred_element_type=jnp.float32
        )
        attended_low = attended.reshape(count, width).astype(jnp.bfloat16)
        attn = jnp.dot(attended_low, full_out, preferred_element_type=jnp.float32)
        mid = rows + attn
        norm2, norm2_back = jax.vjp(rms_norm, mid, gain_mlp)
        norm2_low = norm2.astype(jnp.bfloat16)
        hidden = jnp.dot(norm2_low, full_up, preferred_element_type=jnp.float32)
        act, gelu_back = jax.vjp(exact_gelu, hidden)
        act_low = act.astype(jnp.bfloat16)
        mlp = jnp.dot(act_low, full_down, preferred_element_type=jnp.float32)
        branch = attn + mlp
        outputs.append(resid.at[rows_index].set(rows + gate[:, None] * branch).astype(jnp.bfloat16))
        cot_rows = jnp.take(grad_in, rows_index, axis=0)
        d_branch = gate[:, None] * cot_rows
        d_mlp = d_branch.astype(jnp.bfloat16)
        d_logit = jnp.sum(cot_rows * branch, axis=-1) * gate * (1.0 - gate)
        d_act = jnp.dot(d_mlp, full_down.T, preferred_element_type=jnp.float32)
        d_hidden = gelu_back(d_act)[0].astype(jnp.bfloat16)
        d_norm2 = jnp.dot(d_hidden, full_up.T, preferred_element_type=jnp.float32)
        d_mid, d_gain2 = norm2_back(d_norm2)
        d_attn = (d_branch + d_mid).astype(jnp.bfloat16)
        d_attended = jnp.dot(d_attn, full_out.T, preferred_element_type=jnp.float32).astype(
            jnp.bfloat16
        )
        d_heads = d_attended.reshape(count, HEADS, HEAD_DIM)
        d_probs = jnp.einsum(
            "qhd,khd->hqk", d_heads, value_heads, preferred_element_type=jnp.float32
        )
        weighted = jnp.sum(probs * d_probs, axis=-1, keepdims=True)
        d_scores = (probs * (d_probs - weighted)).astype(jnp.bfloat16)
        d_query = (
            jnp.einsum("hqk,khd->qhd", d_scores, key_heads, preferred_element_type=jnp.float32)
            * factor
        )
        d_key_part = (
            jnp.einsum("hqk,qhd->khd", d_scores, query_heads, preferred_element_type=jnp.float32)
            * factor
        )
        d_value_part = jnp.einsum(
            "hqk,qhd->khd", probs_low, d_heads, preferred_element_type=jnp.float32
        )
        d_keys, d_values = (
            lax.psum_scatter(
                d_key_part.reshape(total, width), "ctx", scatter_dimension=0, tiled=True
            ),
            lax.psum_scatter(
                d_value_part.reshape(total, width), "ctx", scatter_dimension=0, tiled=True
            ),
        )
        d_qkv = jnp.concatenate([d_query.reshape(count, width), d_keys, d_values], axis=1).astype(
            jnp.bfloat16
        )
        d_norm1 = jnp.dot(d_qkv, full_qkv.T, preferred_element_type=jnp.float32)
        d_rows_norm, d_gain1 = norm1_back(d_norm1)
        d_rows = cot_rows + d_mid + d_rows_norm + d_logit[:, None] * w_router
        in_grads.append(grad_in.at[rows_index].set(d_rows).astype(jnp.bfloat16))
        sum_router = sum_router + jnp.dot(d_logit, rows, precision=HIGHEST)
        sum_gain_attn = sum_gain_attn + d_gain1
        sum_gain_mlp = sum_gain_mlp + d_gain2
        kept.append((norm1_low, d_qkv, attended_low, d_attn, norm2_low, d_hidden, act_low, d_mlp))
    stacked_rows = tuple((gather_rows(kept, column) for column in range(8)))
    grad_qkv = outer_sum(stacked_rows[0], stacked_rows[1])
    grad_out = outer_sum(stacked_rows[2], stacked_rows[3])
    grad_up = outer_sum(stacked_rows[4], stacked_rows[5])
    grad_down = outer_sum(stacked_rows[6], stacked_rows[7])
    summed = (
        lax.psum_scatter(sum_router, ("ctx", "fsdp"), scatter_dimension=0, tiled=True),
        lax.psum_scatter(sum_gain_attn, ("ctx", "fsdp"), scatter_dimension=0, tiled=True),
        lax.psum_scatter(grad_qkv, ("ctx", "fsdp"), scatter_dimension=0, tiled=True),
        lax.psum_scatter(grad_out, ("ctx", "fsdp"), scatter_dimension=0, tiled=True),
        lax.psum_scatter(sum_gain_mlp, ("ctx", "fsdp"), scatter_dimension=0, tiled=True),
        lax.psum_scatter(grad_up, ("ctx", "fsdp"), scatter_dimension=0, tiled=True),
        lax.psum_scatter(grad_down, ("ctx", "fsdp"), scatter_dimension=0, tiled=True),
    )
    output = jnp.stack(outputs)[:, None]
    input_grad = jnp.stack(in_grads)[:, None]
    return (
        output,
        input_grad,
        summed[0],
        summed[1],
        summed[2],
        summed[3],
        summed[4],
        summed[5],
        summed[6],
    )


ORDER = (0, 2, 1, 3)


def sds(shape, dtype):
    return jax.ShapeDtypeStruct(shape, dtype)


def local(shape, dtype):
    return pltpu.VMEM(shape, dtype)


def near(x):
    return pltpu.with_memory_space_constraint(x, pltpu.VMEM)


class Chain:
    def __init__(self):
        self.last = None

    def __call__(self, kernel, outs, smem, args, scratch=(), name=None, far=(), after=(), weight=WEIGHT):
        count = len(smem) + len(far) + len(args)
        spec = pl.BlockSpec(memory_space=pltpu.VMEM)
        extra = () if self.last is None else (near(self.last),)
        extra = (*extra, *(near(a) for a in after))

        def body(*refs):
            kernel(*refs[:count], *refs[count + len(extra) :])

        results = pl.pallas_call(
            body,
            out_shape=tuple(outs),
            in_specs=[pl.BlockSpec(memory_space=pltpu.SMEM)] * len(smem)
            + [pl.BlockSpec(memory_space=pltpu.HBM)] * len(far)
            + [spec] * (len(args) + len(extra)),
            out_specs=tuple(spec for _ in outs),
            scratch_shapes=list(scratch),
            compiler_params=pltpu.CompilerParams(vmem_limit_bytes=VMEM_LIMIT),
            cost_estimate=pl.CostEstimate(flops=weight, bytes_accessed=weight // 10000, transcendentals=0),
            name=name,
        )(
            *smem, *(pltpu.with_memory_space_constraint(a, pltpu.HBM) for a in far), *(near(a) for a in args), *extra
        )
        if not isinstance(outs[0], jax.ShapeDtypeStruct):
            self.last = results[0]
        return results

    def hold(self, x, *after):
        (x,) = self(hold_kernel, (local(x.shape, x.dtype),), (), (x,), after=after, name="hold", weight=0)
        return x


def hold_kernel(x, out):
    out[...] = x[...]


def mm(left, right):
    return jnp.dot(left, right, preferred_element_type=F32)


def mm_t(left, right):
    return lax.dot_general(left, right, (((1,), (1,)), ((), ())), preferred_element_type=F32)


def t_mm(left, right):
    return lax.dot_general(left, right, (((0,), (0,)), ((), ())), preferred_element_type=F32)


def exchange(x, axis, size, mask):
    return lax.ppermute(x, axis, [(i, i ^ mask) for i in range(size)])


def rms_factor(values):
    return lax.rsqrt(jnp.mean(values * values, axis=-1, keepdims=True) + EPSILON)


def aligned(start, unit):
    return pl.multiple_of(start, unit)


def iota(shape, axis):
    return lax.broadcasted_iota(jnp.int32, shape, axis)


def picks(ids, routed, micro, tok_dev):
    index = routed[micro : micro + 1, :] - ids[0] * tok_dev
    shape = (tok_dev, routed.shape[1])
    return jnp.where(iota(shape, 0) == index, 1.0, 0.0)


def share_peers(ids, bit):
    return ids[1], ids[1] ^ 1, ids[1] ^ (2 + ((ids[0] >> bit) & 1))


def share_rows(c, f, bit):
    side = (c >> bit) & 1
    return f, f ^ 1, f ^ (2 + side), f ^ (3 - side)


def cut_qkv(ids, half, w_qkv, pieces, sem, first, by_y=True):
    width = w_qkv.shape[1] // 3
    copies = []
    peers = share_peers(ids, 0) if by_y else tuple(ids[1] ^ k for k in range(4))
    for k, (peer, piece) in enumerate(zip(peers, pieces)):
        for b in range(3):
            start = b * width + peer * (width // 4) + half * 128
            copies.append(
                pltpu.make_async_copy(
                    w_qkv.at[:, pl.ds(aligned(start, 128), 128)],
                    piece.at[:, pl.ds(b * 128, 128)],
                    sem.at[first + 3 * k + b],
                )
            )
    return copies


def front_kernel(ids, deal, tokens, w_qkv, routed, rowsx, p0, p1, p2, near_tokens, sem):
    micros, tok_dev, width = tokens.shape
    per = routed.shape[1]
    count = micros * per
    span = tok_dev // 2
    first = pltpu.make_async_copy(tokens, near_tokens, sem.at[0])
    first.start()
    copies = cut_qkv(ids, ids[0] >> 2, w_qkv, (p0, p1, p2), sem, 1)
    for copy in copies:
        copy.start()
    stored = routed[...]
    chunk = stored // span
    anchor = jnp.zeros_like(stored)
    for entry in range(deal.shape[0]):
        anchor = jnp.where(chunk == entry, deal[entry], anchor)
    place = ((anchor * span + stored % span) // BLOCK).astype(F32)
    rowsx[count:] = jnp.zeros((8, width), BF16)
    for micro in range(micros):
        rowsx[count + micro : count + micro + 1, :per] = place[micro : micro + 1].astype(BF16)
    first.wait()
    for micro in range(micros):
        pick = picks(ids, routed, micro, tok_dev).astype(BF16)
        rowsx[micro * per : (micro + 1) * per] = t_mm(pick, near_tokens[micro]).astype(BF16)
    for copy in copies:
        copy.wait()


def run(copies):
    for copy in copies:
        copy.start()
    for copy in copies:
        copy.wait()


def cut_up_kernel(ids, w_up, p0, p1, p2, sem):
    share = p0.shape[1]
    run(
        [
            pltpu.make_async_copy(
                w_up.at[:, pl.ds(aligned(peer * share, share), share)], piece, sem.at[k]
            )
            for k, (peer, piece) in enumerate(zip(share_peers(ids, 0), (p0, p1, p2)))
        ]
    )


def cut_rest_kernel(ids, w_qkv, v0, v1, v2, v3, sem):
    run(cut_qkv(ids, 1 - (ids[0] >> 2), w_qkv, (v0, v1, v2, v3), sem, 0, False))


def cot_kernel(ids, routed, cot, rowsx, both):
    micros, tok_dev = cot.shape[:2]
    per = routed.shape[1]
    start = rowsx.shape[0]
    both[:start] = rowsx[...]
    for micro in range(micros):
        pick = picks(ids, routed, micro, tok_dev).astype(BF16)
        both[start + micro * per : start + (micro + 1) * per] = t_mm(pick, cot[micro]).astype(BF16)


def rows_of(both):
    return both[: both.shape[0] // 2 - 4].astype(F32)


def cots_of(both):
    return both[both.shape[0] // 2 + 4 :].astype(F32)


def d_mlp_kernel(b0, b1, b2, b3, w_router, d_mlp, gate_out):
    count = gate_out.shape[1]
    for i, both in enumerate((b0, b1, b2, b3)):
        gate = jax.nn.sigmoid(jnp.sum(rows_of(both) * w_router[...], axis=1, keepdims=True))
        d_mlp[i * count : (i + 1) * count] = (gate * cots_of(both)).astype(BF16)
        gate_out[i] = gate


def head_masks():
    lanes = iota((1, 128), 1)
    low = jnp.where(lanes < 64, 1.0, 0.0)
    return low, 1.0 - low


def attend_kernel(
    ids, near_rows, far_rows, gain, w0, w1, w2, w3,
    far, own, stack, probs, norm1, place_col, result,
):
    c, f = ids[0], ids[1]
    micros, total = stack.shape[0], stack.shape[1]
    count = own.shape[1]
    per = count // micros
    eye = iota((per, 128), 0) == iota((per, 128), 1)
    step = count + 8
    for h, source in enumerate((near_rows, far_rows)):
        for b in range(4):
            rows = source[b * step : b * step + count].astype(F32)
            index = ((c >> 2) ^ h) * 4 + b
            norm1[pl.ds(aligned(index * count, 16), count)] = (
                rows * rms_factor(rows) * gain[...]
            ).astype(BF16)
            places = source[b * step + count : b * step + count + 8, :128].astype(F32)
            for m in range(micros):
                col = jnp.sum(jnp.where(eye, places[m : m + 1], 0.0), axis=1, keepdims=True)
                place_col[m, pl.ds(aligned(index * per, per), per), :] = jnp.broadcast_to(
                    col, (per, 128)
                )
    qkv = jnp.zeros((8 * count, 384), F32)
    for peer, w in zip(share_rows(c, f, 0), (w0, w1, w2, w3)):
        part = w.shape[0]
        qkv = qkv + mm(norm1[:, pl.ds(aligned(peer * part, part), part)], w[...])
    low = qkv.astype(BF16)
    for t in range(8):
        for m in range(micros):
            stack[m, t * per : (t + 1) * per, :] = low[
                t * count + m * per : t * count + (m + 1) * per
            ]
    big_eye = iota((total, total), 0) == iota((total, total), 1)
    masks = head_masks()
    for m in range(micros):
        q, k, v = stack[m, :, :128], stack[m, :, 128:256], stack[m, :, 256:384]
        mine = place_col[m, :, 0:1]
        theirs = jnp.sum(jnp.where(big_eye, mine, 0.0), axis=0, keepdims=True)
        visible = theirs <= mine
        attended = jnp.zeros((total, 128), F32)
        for h in range(2):
            scores = mm_t(q * masks[h].astype(BF16), k) * (HEAD_DIM**-0.5)
            scores = jnp.where(visible, scores, MASKED)
            top = jnp.max(scores, axis=1, keepdims=True)
            grown = jnp.exp(scores - top)
            weight = grown / jnp.sum(grown, axis=1, keepdims=True)
            probs[2 * m + h] = weight
            attended = attended + mm(weight.astype(BF16), v) * masks[h]
        result[m] = attended.astype(BF16)
        for k in range(8):
            out = far if k >= 4 else own
            out[k & 3, m * per : (m + 1) * per, :] = result[
                m, pl.ds(aligned((c ^ k) * per, per), per), :
            ]


def row_slot(f, s, count):
    k = s ^ f
    return aligned(((k & 1) * 2 + (k >> 1)) * count, 16)


def split_rows(full, send, keep):
    count = send.shape[1]
    for i in range(2):
        keep[i] = full[i * count : (i + 1) * count]
        send[i] = full[(2 + i) * count : (3 + i) * count].astype(BF16)


def block_place(ids, k, count, lanes):
    peer = ids[0] ^ k
    columns = aligned((peer >> 2) * lanes, 128)
    return pl.ds(row_slot(ids[1], peer & 3, count), count), pl.ds(columns, lanes)


def out_kernel(ids, b0, b1, b2, b3, w_out, attended, send, keep, full):
    count = b0.shape[1]
    for k, block in enumerate((b0, b1, b2, b3)):
        for far in range(2):
            attended[block_place(ids, k ^ (4 * far), count, 128)] = block[far]
    full[...] = mm(attended[...], w_out[...])
    split_rows(full, send, keep)


def add_both_kernel(keep, received, total):
    total[...] = (keep[...] + received[...].astype(F32)).astype(BF16)


def add_own_kernel(keep, received, send2, keep2):
    send2[...] = (keep[1] + received[1].astype(F32)).astype(BF16)
    keep2[...] = keep[0] + received[0].astype(F32)


def mid_kernel(low, received, both0, both1, gain, attn, norm2):
    for i, both in enumerate((both0, both1)):
        value = low[i].astype(F32) + received[1 - i].astype(F32)
        attn[i] = value
        mid = rows_of(both) + value
        norm2[i] = (mid * rms_factor(mid) * gain[...]).astype(BF16)


def mlp_kernel(
    ids, n0, n1, d_mlp, u0, u1, u2, u3, w_down,
    send, keep, act_send, d_send, act_keep, d_keep, norm2, act, d_hidden, back,
):
    c = ids[0]
    part = u0.shape[0]
    count = n0.shape[1]
    shares = tuple(zip(share_rows(ids[0], ids[1], 0), (u0, u1, u2, u3)))
    for i in range(2):
        norm2[i * count : (i + 1) * count] = n0[i]
        norm2[(2 + i) * count : (3 + i) * count] = n1[i]
    hidden = jnp.zeros(act.shape, F32)
    for peer, u in shares:
        hidden = hidden + mm(norm2[:, pl.ds(aligned(peer * part, part), part)], u[...])
    d_act = mm_t(d_mlp[...], w_down[...])
    phi = 0.5 * (1.0 + lax.erf(hidden * (0.5**0.5)))
    act[...] = (hidden * phi).astype(BF16)
    slope = phi + hidden * jnp.exp(-0.5 * hidden * hidden) * ((2.0 * math.pi) ** -0.5)
    d_hidden[...] = (d_act * slope).astype(BF16)
    for i, (some_act, some_d) in enumerate(((act_keep, d_keep), (act_send, d_send))):
        for high in range(2):
            start = aligned(high * 512 + (((c >> 1) & 1) ^ i) * 256, 128)
            some_act[:, high * 256 : (high + 1) * 256] = act[:, pl.ds(start, 256)]
        some_d[...] = d_hidden[:, pl.ds(aligned(((c & 1) ^ i) * 512, 128), 512)]
    for peer, u in shares:
        back[:, pl.ds(aligned(peer * part, part), part)] = mm_t(d_hidden[...], u[...])
    split_rows(back, send, keep)


def mlp_out_kernel(act, w_down, attn, gate, b0, b1, b2, b3, send, keep, router, full):
    full[...] = mm(act[...], w_down[...])
    split_rows(full, send, keep)
    count = gate.shape[1]
    total = jnp.zeros(router.shape, F32)
    for i, both in enumerate((b0, b1, b2, b3)):
        own = slice(i * count, (i + 1) * count)
        part = jnp.sum(cots_of(both) * (attn[own] + full[own]), axis=1, keepdims=True)
        part = part * gate[i] * (1.0 - gate[i])
        total = total + jnp.sum(rows_of(both) * part, axis=0, keepdims=True)
    router[...] = total


def pick_rows(c, peer, share, out, lanes):
    @pl.when(peer == (c >> 1))
    def _():
        out[:, lanes] = share[pl.ds(aligned((c & 1) * 128, 128), 128), :]


def pick_kernel(ids, *refs):
    shares, (up_rows, qkv_rows) = refs[:12], refs[12:]
    c, f = ids[0], ids[1]
    for peer, u in zip(share_rows(c, f, 0), shares[:4]):
        pick_rows(c, peer, u, up_rows, slice(None))
    for peer, a in zip(share_rows(c, f, 0), shares[4:8]):
        pick_rows(c, peer, a, qkv_rows, slice(0, 384))
    for k, b in enumerate(shares[8:]):
        pick_rows(c, f ^ k, b, qkv_rows, slice(384, 768))


def chunk(f, q):
    return pl.ds(aligned((f ^ q) * 32, 32), 32)


def grad_up_kernel(ids, norm2, near_a, near_b, d_own, d_near, send, keep, rows, columns):
    count = norm2.shape[0]
    half = count // 2
    rows[:count] = norm2[...]
    for i in range(2):
        rows[count + i * (half // 2) : count + (i + 1) * (half // 2)] = near_a[i]
        rows[count + half + i * (half // 2) : count + half + (i + 1) * (half // 2)] = near_b[i]
    columns[:count] = d_own[...]
    columns[count:] = d_near[...]
    for place, (target, index) in enumerate(((keep, 0), (send, 0), (keep, 1), (send, 1))):
        kk = (0, 1, 2, 3)[place]
        start = aligned(((ids[0] >> 1) ^ kk) * 256, 128)
        value = t_mm(rows[:, pl.ds(start, 256)], columns[...])
        for owner in range(2):
            for q in range(4):
                at = pl.ds(aligned(((ids[0] & 1) ^ owner) * 128 + (ids[1] ^ q) * 32, 32), 32)
                piece = value[owner * 128 + q * 32 : owner * 128 + (q + 1) * 32]
                target[index, at] = piece.astype(target.dtype)


def grad_down_kernel(ids, d_mlp, near_a, near_b, a_own, a_near, send, keep, rows, columns):
    count = d_mlp.shape[0]
    half = count // 2
    rows[:count] = d_mlp[...]
    rows[count : count + half] = near_a[...]
    rows[count + half :] = near_b[...]
    columns[:count] = a_own[...]
    columns[count:] = a_near[...]
    c = ids[0]
    for target, index, k in ((keep, 0, 0), (send, 0, 1), (keep, 1, 4), (send, 1, 5)):
        start = aligned(((c >> 2) ^ (k >> 2)) * 256 + ((c & 1) ^ (k & 1)) * 128, 128)
        value = t_mm(columns[:, pl.ds(start, 128)], rows[...])
        target[index] = value.astype(target.dtype)


def grad_attn_kernel(
    ids, norm1, b0, b1, b2, b3, b4, b5, b6, b7, attended, d_attn, router,
    keep, send1, send2, send3, joined, full,
):
    count = b0.shape[0]
    for k, block in enumerate((b0, b1, b2, b3, b4, b5, b6, b7)):
        joined[pl.ds(aligned((ids[0] ^ k) * count, 16), count)] = block[...]
    full[...] = t_mm(attended[...], d_attn[...])
    for k in range(8):
        target, index = (keep, send1, send2, send3)[k & 3], k >> 2
        owner = ids[0] ^ k
        start = aligned(owner * 128, 128)
        value = t_mm(norm1[:, pl.ds(start, 128)], joined[...])
        for q in range(4):
            piece = value[q * 32 : (q + 1) * 32]
            target[index, chunk(ids[1], q), :384] = piece.astype(target.dtype)
            rows = full[pl.ds(aligned(owner * 32, 32), 32), q * 256 : (q + 1) * 256]
            target[index, q * 32 : (q + 1) * 32, 384:640] = rows.astype(target.dtype)
        target[index, 128:136, :] = jnp.zeros((8, 640), target.dtype)
        share = jnp.broadcast_to(router[:, pl.ds(start, 128)], (8, 128))
        target[index, 128:136, 384:512] = share.astype(target.dtype)


def sum_attn_kernel(keep, got1, got2, got3, send, mine):
    for index, target in ((0, mine), (1, send)):
        total = (keep[index] + got1[index].astype(F32)) + (
            got2[index].astype(F32) + got3[index].astype(F32)
        )
        target[0] = total.astype(target.dtype)


def d_attn_kernel(low, received, attn, both0, both1, gate, gain, d_mid_out, d_attn):
    for i, both in enumerate((both0, both1)):
        mid = rows_of(both) + attn[i]
        r2 = rms_factor(mid)
        d_norm2 = low[i].astype(F32) + received[1 - i].astype(F32)
        t2 = d_norm2 * gain[...]
        d_mid = r2 * t2 - mid * (r2 * r2 * r2) * jnp.mean(t2 * mid, axis=1, keepdims=True)
        d_attn[i] = (gate[i] * cots_of(both) + d_mid).astype(BF16)
        if i == 0:
            d_mid_out[...] = d_mid


def d_attended_kernel(ids, d0, d1, w_out, far, own, d_attn, d_att):
    count = d0.shape[1]
    for i in range(2):
        d_attn[i * count : (i + 1) * count] = d0[i]
        d_attn[(2 + i) * count : (3 + i) * count] = d1[i]
    d_att[...] = mm_t(d_attn[...], w_out[...])
    for k in range(8):
        block = far if k >= 4 else own
        block[k & 3] = d_att[block_place(ids, k, count, 128)].astype(BF16)


def attend_back_kernel(ids, *refs):
    blocks, (stack, probs), outs, (d_stack, result) = refs[:4], refs[4:6], refs[6:14], refs[14:]
    micros, total = stack.shape[0], stack.shape[1]
    count = outs[0].shape[0]
    per = count // micros
    masks = head_masks()
    for m in range(micros):
        rows = slice(m * per, (m + 1) * per)
        for k in range(8):
            d_stack[pl.ds(aligned((ids[0] ^ k) * per, per), per), :] = blocks[k & 3][k >> 2, rows]
        q, k, v = stack[m, :, :128], stack[m, :, 128:256], stack[m, :, 256:384]
        d_out = d_stack[...]
        d_q = jnp.zeros((total, 128), F32)
        d_k = jnp.zeros((total, 128), F32)
        d_v = jnp.zeros((total, 128), F32)
        for h in range(2):
            weight = probs[2 * m + h]
            d_probs = mm_t(d_out * masks[h].astype(BF16), v)
            inner = jnp.sum(weight * d_probs, axis=1, keepdims=True)
            d_scores = (weight * (d_probs - inner)).astype(BF16)
            d_q = d_q + mm(d_scores, k) * masks[h]
            d_k = d_k + t_mm(d_scores, q) * masks[h]
            d_v = d_v + t_mm(weight.astype(BF16), d_out) * masks[h]
        result[m, :, :128] = (d_q * (HEAD_DIM**-0.5)).astype(BF16)
        result[m, :, 128:256] = (d_k * (HEAD_DIM**-0.5)).astype(BF16)
        result[m, :, 256:384] = d_v.astype(BF16)
        for k in range(8):
            outs[k][rows] = result[m, pl.ds(aligned((ids[0] ^ k) * per, per), per), :]


def d_norm1_kernel(
    ids, d0, d1, d2, d3, d4, d5, d6, d7, a0, a1, a2, a3, b0, b1, b2, b3,
    send, keep, d_qkv, full,
):
    c, f = ids[0], ids[1]
    count = d0.shape[0]
    part = a0.shape[0]
    for k, block in enumerate((d0, d1, d2, d3, d4, d5, d6, d7)):
        rows = pl.ds(row_slot(f, (c ^ k) & 3, count), count)
        d_qkv[rows, (k >> 2) * 384 : (k >> 2) * 384 + 384] = block[...]
    for peer, a in zip(share_rows(c, f, 0), (a0, a1, a2, a3)):
        full[:, pl.ds(aligned(peer * part, part), part)] = mm_t(d_qkv[:, :384], a[...])
    for k, b in enumerate((b0, b1, b2, b3)):
        columns = pl.ds(aligned((f ^ k) * part, part), part)
        full[:, columns] = full[:, columns] + mm_t(d_qkv[:, 384:], b[...])
    split_rows(full, send, keep)


def place_rows(ids, routed, micro, source, rows, out):
    tok_dev = source.shape[0]
    pick = picks(ids, routed, micro, tok_dev)
    changed = jnp.sum(pick, axis=1, keepdims=True) > 0.5
    placed = mm(pick.astype(BF16), rows)
    out[...] = jnp.where(changed, placed, source[...].astype(F32)).astype(BF16)


def output_kernel(
    ids, routed, keep, received, attn, both, gate, tokens, d_logit_out, output,
):
    count = keep.shape[0]
    micros = tokens.shape[0]
    per = count // micros
    branch = attn[0] + keep[...] + received[...].astype(F32)
    rows = rows_of(both)
    open_gate = gate[0]
    d_logit = (
        jnp.sum(cots_of(both) * branch, axis=1, keepdims=True)
        * open_gate
        * (1.0 - open_gate)
    )
    d_logit_out[...] = d_logit
    result = (rows + open_gate * branch).astype(BF16)
    for micro in range(micros):
        own = result[micro * per : (micro + 1) * per]
        place_rows(ids, routed, micro, tokens.at[micro], own, output.at[micro])


def input_grad_kernel(
    ids, routed, keep, received, d_mid, both, d_logit, w_router, gain, cot, input_grad,
):
    count = keep.shape[0]
    micros = cot.shape[0]
    per = count // micros
    rows = rows_of(both)
    r1 = rms_factor(rows)
    t1 = (keep[...] + received[...].astype(F32)) * gain[...]
    d_rows = (
        cots_of(both)
        + d_mid[...]
        + r1 * t1
        - rows * (r1 * r1 * r1) * jnp.mean(t1 * rows, axis=1, keepdims=True)
        + d_logit[...] * w_router[...]
    ).astype(BF16)
    for micro in range(micros):
        own = d_rows[micro * per : (micro + 1) * per]
        place_rows(ids, routed, micro, cot.at[micro], own, input_grad.at[micro])


def as_row(column):
    count = column.shape[0]
    eye = iota((count, count), 0) == iota((count, count), 1)
    return jnp.sum(jnp.where(eye, column, 0.0), axis=0, keepdims=True)


def owned(ids, vector, count):
    start = (4 * ids[0] + ids[1]) * count
    shape = (count, vector.shape[1])
    hit = iota(shape, 1) == iota(shape, 0) + start
    return jnp.sum(jnp.where(hit, vector[...], 0.0), axis=1, keepdims=True)


def join_up_kernel(ids, p0, p1, p2, p3, gain, out, grad_gain):
    rows, part = out.shape[0], out.shape[1] // 4
    total = jnp.zeros((rows, 1), F32)
    for k, piece in enumerate((p0, p1, p2, p3)):
        out[:, pl.ds(aligned((ids[1] ^ k) * part, part), part)] = piece[:, :part].astype(F32)
        total = total + piece[:, part : part + 128].astype(F32)[:, :1]
    grad_gain[...] = as_row(total / owned(ids, gain, rows))


def join_qkv_kernel(ids, p0, p1, p2, p3, gain, out, grad_gain, grad_router):
    rows, width = out.shape[0], out.shape[1] // 3
    part = width // 4
    total = jnp.zeros((rows, 1), F32)
    router = jnp.zeros((rows, 1), F32)
    for k, piece in enumerate((p0, p1, p2, p3)):
        for half in range(2):
            for b in range(3):
                start = b * width + (ids[1] ^ k) * part + ((ids[0] >> 2) ^ half) * 128
                out[:, pl.ds(aligned(start, 128), 128)] = piece[
                    :, (3 * half + b) * 128 : (3 * half + b + 1) * 128
                ].astype(F32)
        total = total + piece[:, 768:896].astype(F32)[:, :1]
        router = router + piece[:, 896:1024].astype(F32)[:, :1]
    grad_gain[...] = as_row(total / owned(ids, gain, rows))
    grad_router[...] = as_row(router)


def join_down_kernel(block, out):
    out[...] = block[...].astype(F32)


def hop2_kernel(keep_u, got_u, keep_d, got_d, send, own_u, own_d):
    for i in range(2):
        total = keep_u[i] + got_u[i].astype(F32)
        half, width = total.shape[0] // 2, total.shape[1]
        if i:
            send[0, :, :width] = total[:half].astype(BF16)
            send[0, :, width:] = total[half:].astype(BF16)
        else:
            own_u[...] = total
    own_d[...] = keep_d[0] + got_d[0].astype(F32)
    send[1] = (keep_d[1] + got_d[1].astype(F32)).astype(BF16)


def hop3_kernel(own_u, own_d, got, send, mine, down):
    half, width = own_u.shape[0] // 2, own_u.shape[1]
    mine[...] = own_u[:half] + got[0, :, :width].astype(F32)
    send[...] = (own_u[half:] + got[0, :, width:].astype(F32)).astype(BF16)
    down[...] = (own_d[...] + got[1].astype(F32)).astype(BF16)


def up_pieces_kernel(ids, mine, other, w_rows, c0, c1, c2, c3):
    rows, half = c0.shape[0], mine.shape[1]
    y = ids[0] & 1
    for k, piece in enumerate((c0, c1, c2, c3)):
        own = slice(k * rows, (k + 1) * rows)
        weights = pl.ds(aligned((ids[1] ^ k) * rows, rows), rows)
        total = jnp.zeros((rows, 1), F32)
        for side, value in ((y, mine[own]), (1 - y, other[own].astype(F32))):
            columns = pl.ds(aligned(side * half, 128), half)
            piece[:, columns] = value.astype(BF16)
            total = total + jnp.sum(
                value * w_rows[weights, columns].astype(F32), axis=1, keepdims=True
            )
        piece[:, 2 * half :] = jnp.broadcast_to(total, (rows, 128)).astype(BF16)


def pieces_kernel(ids, mine, got, w_rows, c0, c1, c2, c3, out):
    rows = c0.shape[0]
    router = mine[0, 128:129, 384:512] + got[0, 128:136, 384:512].astype(F32)[0:1]
    for k, piece in enumerate((c0, c1, c2, c3)):
        own = slice(k * rows, (k + 1) * rows)
        first = (ids[1] ^ k) * rows
        weights = pl.ds(aligned(first, rows), rows)
        a, b = mine[0, own, :384], got[0, own, :384].astype(F32)
        piece[:, :384] = a.astype(BF16)
        piece[:, 384:768] = b.astype(BF16)
        total = jnp.sum(a * w_rows[weights, :384].astype(F32), axis=1, keepdims=True)
        total = total + jnp.sum(b * w_rows[weights, 384:].astype(F32), axis=1, keepdims=True)
        piece[:, 768:896] = jnp.broadcast_to(total, (rows, 128)).astype(BF16)
        hit = iota((rows, 128), 1) == iota((rows, 128), 0) + first
        share = jnp.sum(jnp.where(hit, router, 0.0), axis=1, keepdims=True)
        piece[:, 896:] = jnp.broadcast_to(share, (rows, 128)).astype(BF16)
        out[:, k * 256 : (k + 1) * 256] = mine[0, own, 384:640] + got[0, own, 384:640].astype(F32)


def all_rows_sum(call, send, keep, after=()):
    received = exchange(send, "fsdp", 4, 1)
    (low,) = call(
        add_both_kernel, (local(keep.shape, BF16),), (), (keep, received), name="add_both", after=after
    )
    return low, exchange(low, "fsdp", 4, 2)


def own_rows_sum(call, send, keep):
    received = exchange(send, "fsdp", 4, 1)
    shape = keep.shape[1:]
    send2, keep2 = call(
        add_own_kernel, (local(shape, BF16), local(shape, F32)), (), (keep, received), name="add_own"
    )
    return keep2, exchange(send2, "fsdp", 4, 2)


def swap_blocks(blocks):
    got = {k: exchange(blocks[k], "ctx", 8, k) for k in (7, 6, 5, 4, 3, 2, 1)}
    return (blocks[0], *(got[k] for k in range(1, 8)))


def swap_across(across, bit):
    return lax.ppermute(
        across, ("ctx", "fsdp"),
        [(4 * a + b, 4 * a + (b ^ (2 + ((a >> bit) & 1)))) for a in range(8) for b in range(4)],
    )


def pair_kernel(own, far, *outs):
    for k, out in enumerate(outs):
        out[0] = own[k]
        out[1] = far[k]


def swap_in_two(call, own, far, *after):
    came = exchange(far, "ctx", 8, 4)
    shape = (2, *own.shape[1:])
    pairs = call(pair_kernel, (local(shape, own.dtype),) * 4, (), (own, came), name="pair", after=after)
    return (pairs[0], *(exchange(pairs[k], "ctx", 8, k) for k in (1, 2, 3)))


def swap_pieces(pieces):
    return (pieces[0], *(exchange(pieces[k], "fsdp", 4, k) for k in (1, 2, 3)))


def shards_8x4(
    tokens, w_router, gain_attn, w_qkv, w_out, gain_mlp, w_up, w_down, routed, deal, cotangent
):
    micros, tok_dev, width = tokens.shape[0], tokens.shape[2], tokens.shape[3]
    per = routed.shape[2]
    count = micros * per
    total = 8 * per
    part = width // 4
    hidden = w_down.shape[0]
    c, f = lax.axis_index("ctx"), lax.axis_index("fsdp")
    ids = jnp.stack([c, f]).astype(jnp.int32)
    tok, cot, routed = tokens[:, 0], cotangent[:, 0], routed[:, 0]
    w_router, gain_attn, gain_mlp = (
        w_router.reshape(1, width), gain_attn.reshape(1, width), gain_mlp.reshape(1, width),
    )
    rows_bf, rows_f = local((count, width), BF16), local((count, width), F32)
    pair_bf, pair_f = local((2, count, width), BF16), local((2, count, width), F32)
    all_bf, all_quarter = local((4 * count, width), BF16), local((4 * count, part), BF16)
    hidden_bf = local((4 * count, hidden), BF16)
    vector = local((1, width), F32)
    dma = pltpu.SemaphoreType.DMA
    call = Chain()

    rowsx, *w_parts = call(
        front_kernel,
        (local((count + 8, width), BF16), *(local((part, 384), BF16),) * 3),
        (ids, deal), (routed,), far=(tok, w_qkv),
        scratch=[pltpu.VMEM(tok.shape, BF16), dma((10,))], name="front",
    )
    turn = [(4 * a + b, 4 * ((a & 4) | b) + (a & 3)) for a in range(8) for b in range(4)]
    turned = lax.ppermute(rowsx, ("ctx", "fsdp"), turn)
    turned_far = exchange(turned, "ctx", 8, 4)
    w_mine, w_beside, w_across = w_parts
    w_across = swap_across(w_across, 0)
    up_mine, up_beside, up_across = call(
        cut_up_kernel, (local((part, hidden), BF16),) * 3, (ids,), (), far=(w_up,),
        scratch=[dma((3,))], name="cut_up", weight=0,
    )
    near_rows = lax.all_gather(turned, "fsdp", axis=0, tiled=True)
    far_rows = lax.all_gather(turned_far, "fsdp", axis=0, tiled=True)
    w_across = call.hold(w_across, near_rows)
    up_across = call.hold(up_across, far_rows)
    w_parts = (w_mine, exchange(w_beside, "fsdp", 4, 1), w_across, exchange(w_across, "ctx", 8, 1))
    up_beside, up_across = exchange(up_beside, "fsdp", 4, 1), swap_across(up_across, 0)
    far_heads, heads, stack, probs, norm1 = call(
        attend_kernel,
        (
            *(local((4, count, 128), BF16),) * 2, local((micros, total, 384), BF16),
            local((2 * micros, total, total), F32), local((8 * count, width), BF16),
        ),
        (ids,), (near_rows, far_rows, gain_attn, *w_parts),
        scratch=[pltpu.VMEM((micros, total, 128), F32), pltpu.VMEM((micros, total, 128), BF16)],
        name="attend",
    )
    (both,) = call(
        cot_kernel, (local((2 * count + 8, width), BF16),), (ids,), (routed, cot, rowsx), name="cot_rows",
        weight=0,
    )
    both_x, both_c = exchange(both, "fsdp", 4, 2), exchange(both, "fsdp", 4, 1)
    both_xc = exchange(both_x, "fsdp", 4, 1)
    rest = call(
        cut_rest_kernel, (local((part, 384), BF16),) * 4, (ids,), (), far=(w_qkv,),
        scratch=[dma((12,))], name="cut_rest", weight=0,
    )
    heads = swap_in_two(call, heads, far_heads, up_across)
    attended, send, keep, attn_part = call(
        out_kernel, (all_quarter, pair_bf, pair_f, local((4 * count, width), F32)),
        (ids,), (*heads, w_out), name="attn_out", after=(up_across, both_x),
    )
    up_parts = (up_mine, up_beside, up_across, exchange(up_across, "ctx", 8, 1))
    rest = swap_pieces(rest)
    low, received = all_rows_sum(call, send, keep)
    d_mlp, gate = call(
        d_mlp_kernel, (all_bf, local((4, count, 1), F32)), (),
        (both, both_x, both_c, both_xc, w_router), name="d_mlp", weight=0,
    )
    d_mlp_a = exchange(d_mlp[: 2 * count], "ctx", 8, 2)
    d_mlp_b = exchange(d_mlp_a, "fsdp", 4, 1)
    attn, norm2 = call(
        mid_kernel, (pair_f, pair_bf), (), (low, received, both, both_x, gain_mlp), name="mid",
    )
    norm2_a = exchange(norm2, "ctx", 8, 1)
    norm2_b = exchange(norm2_a, "fsdp", 4, 1)
    half_bf = local((4 * count, hidden // 2), BF16)
    send, keep, act_send, d_send, act_keep, d_keep, norm2, act = call(
        mlp_kernel, (pair_bf, pair_f, half_bf, half_bf, half_bf, half_bf, all_bf, hidden_bf), (ids,),
        (norm2, exchange(norm2, "fsdp", 4, 1), d_mlp, *up_parts, w_down),
        scratch=[pltpu.VMEM((4 * count, hidden), BF16), pltpu.VMEM((4 * count, width), F32)],
        name="mlp",
    )
    d_near, act_near = exchange(d_send, "ctx", 8, 1), exchange(act_send, "ctx", 8, 2)
    low, received = all_rows_sum(call, send, keep, (norm2_a, d_mlp_a))
    d_mid, d_attn = call(
        d_attn_kernel, (rows_f, pair_bf), (),
        (low, received, attn, both, both_x, gate, gain_mlp), name="d_attn",
        after=(d_near, act_near),
    )
    far_heads, d_heads, d_attn = call(
        d_attended_kernel, (*(local((4, count, 128), BF16),) * 2, all_bf), (ids,),
        (d_attn, exchange(d_attn, "fsdp", 4, 1), w_out),
        scratch=[pltpu.VMEM((4 * count, part), F32)], name="d_attended",
    )
    send_u, keep_u = call(
        grad_up_kernel, (local((2, 256, hidden // 2), BF16), local((2, 256, hidden // 2), F32)), (ids,),
        (norm2, norm2_a, norm2_b, d_keep, d_near), name="grad_up", weight=0,
        scratch=[pltpu.VMEM((8 * count, width), BF16), pltpu.VMEM((8 * count, hidden // 2), BF16)],
    )
    send_d, keep_d = call(
        grad_down_kernel, (local((2, 128, width), BF16), local((2, 128, width), F32)), (ids,),
        (d_mlp, d_mlp_a, d_mlp_b, act_keep, act_near), name="grad_down", weight=0,
        scratch=[pltpu.VMEM((8 * count, width), BF16), pltpu.VMEM((8 * count, hidden // 2), BF16)],
    )
    got_u, got_d = exchange(send_u, "ctx", 8, 2), exchange(send_d, "ctx", 8, 1)
    d_heads = swap_in_two(call, d_heads, far_heads)
    d_blocks = call(
        attend_back_kernel, (local((count, 384), BF16),) * 8, (ids,), (*d_heads, stack, probs),
        scratch=[pltpu.VMEM((total, 128), BF16), pltpu.VMEM((micros, total, 384), BF16)],
        name="attend_back", after=(*rest[1:], got_u, got_d),
    )
    d_own = swap_blocks(d_blocks)
    send_z, own_u, own_d = call(
        hop2_kernel,
        (local((2, 128, width), BF16), local((256, hidden // 2), F32), local((128, width), F32)),
        (), (keep_u, got_u, keep_d, got_d), name="hop2", weight=0,
    )
    got_z = exchange(send_z, "ctx", 8, 4)
    owners = [(4 * a + b, 4 * (2 * b + a // 4) + a % 4) for a in range(8) for b in range(4)]
    send_m, keep_m, router = call(
        mlp_out_kernel, (pair_bf, pair_f, vector), (),
        (act, w_down, attn_part, gate, both, both_x, both_c, both_xc), name="mlp_out", weight=0,
        scratch=[pltpu.VMEM((4 * count, width), F32)],
    )
    part_bf = local((2, 136, 640), BF16)
    keep_q, *send_q = call(
        grad_attn_kernel, (local((2, 136, 640), F32), part_bf, part_bf, part_bf), (ids,),
        (norm1, *d_blocks, attended, d_attn, router), name="grad_attn", weight=0,
        scratch=[pltpu.VMEM((8 * count, 384), BF16), pltpu.VMEM((part, width), F32)],
    )
    got_q = [exchange(x, "ctx", 8, k + 1) for k, x in enumerate(send_q)]
    send, keep = call(
        d_norm1_kernel, (pair_bf, pair_f), (ids,),
        (*d_own, *w_parts, *rest), name="d_norm1",
        scratch=[pltpu.VMEM((4 * count, 768), BF16), pltpu.VMEM((4 * count, width), F32)],
    )
    keep, received = own_rows_sum(call, send, keep)
    keep_m, received_m = own_rows_sum(call, send_m, keep_m)
    send_u, mine_u, down = call(
        hop3_kernel,
        (local((128, hidden // 2), BF16), local((128, hidden // 2), F32), local((128, width), BF16)),
        (), (own_u, own_d, got_z), name="hop3", weight=0,
    )
    down = lax.ppermute(down, ("ctx", "fsdp"), owners)
    other_u = exchange(send_u, "ctx", 8, 1)
    send_q, keep_q = call(
        sum_attn_kernel, (local((1, 136, 640), BF16), local((1, 136, 640), F32)), (),
        (keep_q, *got_q), name="sum_attn", weight=0,
    )
    got_q = exchange(send_q, "ctx", 8, 4)
    d_logit, output = call(
        output_kernel, (local((count, 1), F32), sds(tok.shape, BF16)), (ids,),
        (routed, keep_m, received_m, attn, both, gate, tok), name="output", weight=0,
    )
    (input_grad,) = call(
        input_grad_kernel, (sds(cot.shape, BF16),), (ids,),
        (routed, keep, received, d_mid, both, d_logit, w_router, gain_attn, cot), name="input_grad",
        weight=0,
    )
    w_up_rows, w_qkv_rows = call(
        pick_kernel, (local((128, hidden), BF16), local((128, 768), BF16)), (ids,),
        (*up_parts, *w_parts, *rest), name="pick", weight=0,
    )
    chunks = call(
        up_pieces_kernel, (local((32, hidden + 128), BF16),) * 4, (ids,), (mine_u, other_u, w_up_rows),
        name="up_pieces",
    )
    chunks = swap_pieces(chunks)
    *qkv_chunks, grad_out = call(
        pieces_kernel, (local((32, 1024), BF16),) * 4 + (local((32, width), F32),), (ids,),
        (keep_q, got_q, w_qkv_rows), name="qkv_pieces",
    )
    qkv_chunks = swap_pieces(qkv_chunks)
    grad_out = lax.ppermute(grad_out, ("ctx", "fsdp"), owners)
    row = sds((1, 32), F32)
    (grad_down,) = call(
        join_down_kernel, (sds((128, width), F32),), (), (down,), name="join_down"
    )
    grad_up, grad_gain_mlp = call(
        join_up_kernel, (sds((32, 4 * hidden), F32), row), (ids,), (*chunks, gain_mlp), name="join_up"
    )
    grad_qkv, grad_gain_attn, grad_router = call(
        join_qkv_kernel, (sds((32, 3 * width), F32), row, row), (ids,), (*qkv_chunks, gain_attn),
        name="join_qkv",
    )
    return (
        output[:, None], input_grad[:, None], grad_router[0], grad_gain_attn[0], grad_qkv, grad_out,
        grad_gain_mlp[0], grad_up, grad_down,
    )


def solution(mesh):
    placed = (
        P(None, "fsdp", "ctx", None),
        P(),
        P(),
        P("fsdp", None),
        P("fsdp", None),
        P(),
        P("fsdp", None),
        P("fsdp", None),
        P(None, "fsdp", "ctx"),
        P(),
        P(None, "fsdp", "ctx", None),
    )
    fits = mesh.shape["ctx"] == 8 and mesh.shape["fsdp"] == 4
    return jax.shard_map(
        shards_8x4 if fits else shards,
        mesh=mesh,
        in_specs=placed,
        out_specs=(
            P(None, "fsdp", "ctx", None),
            P(None, "fsdp", "ctx", None),
            P(("ctx", "fsdp")),
            P(("ctx", "fsdp")),
            P(("ctx", "fsdp"), None),
            P(("ctx", "fsdp"), None),
            P(("ctx", "fsdp")),
            P(("ctx", "fsdp"), None),
            P(("ctx", "fsdp"), None),
        ),
        check_vma=False,
    )
```

```python
import math

import jax
import jax.numpy as jnp
from jax import lax
from jax.experimental import pallas as pl
from jax.experimental.pallas import tpu as pltpu
from jax.sharding import PartitionSpec as P

HEADS = 16
HEAD_DIM = 64
BLOCK = 256


EPSILON = 1e-06
MASKED = -1e30
HIGHEST = lax.Precision.HIGHEST
BF16, F32 = jnp.bfloat16, jnp.float32
VMEM_LIMIT = 24 * 2**20
WEIGHT = 10**10


def rms_norm(values, gain):
    factor = lax.rsqrt(jnp.mean(values * values, axis=-1, keepdims=True) + EPSILON)
    return values * factor * gain


def exact_gelu(values):
    return jax.nn.gelu(values, approximate=False)


def fetch(w_qkv, w_out, w_up, w_down):
    return (
        lax.all_gather(w_qkv, "fsdp", axis=0, tiled=True),
        lax.all_gather(w_out, "fsdp", axis=0, tiled=True),
        lax.all_gather(w_up, "fsdp", axis=0, tiled=True),
        lax.all_gather(w_down, "fsdp", axis=0, tiled=True),
    )


def lookup(table, index):
    hits = index[..., None] == jnp.arange(table.shape[0], dtype=jnp.int32)
    return jnp.sum(jnp.where(hits, table, 0), axis=-1)


def outer_sum(left, right):
    return lax.dot_general(
        left, right, (((0,), (0,)), ((), ())), preferred_element_type=jnp.float32
    )


def gather_rows(pieces, column):
    return jnp.concatenate([piece[column] for piece in pieces], axis=0)


def shards(
    tokens, w_router, gain_attn, w_qkv, w_out, gain_mlp, w_up, w_down, routed, deal, cotangent
):
    micros, tok_dev, width = (tokens.shape[0], tokens.shape[2], tokens.shape[3])
    span = tok_dev // 2
    rank = lax.axis_index("ctx")
    storage = routed[:, 0, :]
    local_rows = storage - rank * tok_dev
    anchor = lookup(deal, storage // span) * span + storage % span
    own_blocks = anchor // BLOCK
    all_blocks = lax.all_gather(own_blocks, "ctx", axis=1, tiled=True)
    factor = HEAD_DIM ** (-0.5)
    outputs, in_grads, kept = ([], [], [])
    sum_router = jnp.zeros((width,), jnp.float32)
    sum_gain_attn = jnp.zeros((width,), jnp.float32)
    sum_gain_mlp = jnp.zeros((width,), jnp.float32)
    for micro in range(micros):
        full_qkv, full_out, full_up, full_down = fetch(w_qkv, w_out, w_up, w_down)
        resid = tokens[micro, 0].astype(jnp.float32)
        grad_in = cotangent[micro, 0].astype(jnp.float32)
        rows_index = local_rows[micro]
        rows = jnp.take(resid, rows_index, axis=0)
        count = rows.shape[0]
        gate = jax.nn.sigmoid(jnp.dot(rows, w_router, precision=HIGHEST))
        norm1, norm1_back = jax.vjp(rms_norm, rows, gain_attn)
        norm1_low = norm1.astype(jnp.bfloat16)
        qkv = jnp.dot(norm1_low, full_qkv, preferred_element_type=jnp.float32).astype(jnp.bfloat16)
        queries = qkv[:, :width]
        keys_local = qkv[:, width : 2 * width]
        values_local = qkv[:, 2 * width :]
        keys_all, values_all = (
            lax.all_gather(keys_local, "ctx", axis=0, tiled=True),
            lax.all_gather(values_local, "ctx", axis=0, tiled=True),
        )
        total = keys_all.shape[0]
        query_heads = queries.reshape(count, HEADS, HEAD_DIM)
        key_heads = keys_all.reshape(total, HEADS, HEAD_DIM)
        value_heads = values_all.reshape(total, HEADS, HEAD_DIM)
        visible = all_blocks[micro][None, :] <= own_blocks[micro][:, None]
        scores = (
            jnp.einsum("qhd,khd->hqk", query_heads, key_heads, preferred_element_type=jnp.float32)
            * factor
        )
        scores = jnp.where(visible[None], scores, MASKED)
        probs = jax.nn.softmax(scores, axis=-1)
        probs_low = probs.astype(jnp.bfloat16)
        attended = jnp.einsum(
            "hqk,khd->qhd", probs_low, value_heads, preferred_element_type=jnp.float32
        )
        attended_low = attended.reshape(count, width).astype(jnp.bfloat16)
        attn = jnp.dot(attended_low, full_out, preferred_element_type=jnp.float32)
        mid = rows + attn
        norm2, norm2_back = jax.vjp(rms_norm, mid, gain_mlp)
        norm2_low = norm2.astype(jnp.bfloat16)
        hidden = jnp.dot(norm2_low, full_up, preferred_element_type=jnp.float32)
        act, gelu_back = jax.vjp(exact_gelu, hidden)
        act_low = act.astype(jnp.bfloat16)
        mlp = jnp.dot(act_low, full_down, preferred_element_type=jnp.float32)
        branch = attn + mlp
        outputs.append(resid.at[rows_index].set(rows + gate[:, None] * branch).astype(jnp.bfloat16))
        cot_rows = jnp.take(grad_in, rows_index, axis=0)
        d_branch = gate[:, None] * cot_rows
        d_mlp = d_branch.astype(jnp.bfloat16)
        d_logit = jnp.sum(cot_rows * branch, axis=-1) * gate * (1.0 - gate)
        d_act = jnp.dot(d_mlp, full_down.T, preferred_element_type=jnp.float32)
        d_hidden = gelu_back(d_act)[0].astype(jnp.bfloat16)
        d_norm2 = jnp.dot(d_hidden, full_up.T, preferred_element_type=jnp.float32)
        d_mid, d_gain2 = norm2_back(d_norm2)
        d_attn = (d_branch + d_mid).astype(jnp.bfloat16)
        d_attended = jnp.dot(d_attn, full_out.T, preferred_element_type=jnp.float32).astype(
            jnp.bfloat16
        )
        d_heads = d_attended.reshape(count, HEADS, HEAD_DIM)
        d_probs = jnp.einsum(
            "qhd,khd->hqk", d_heads, value_heads, preferred_element_type=jnp.float32
        )
        weighted = jnp.sum(probs * d_probs, axis=-1, keepdims=True)
        d_scores = (probs * (d_probs - weighted)).astype(jnp.bfloat16)
        d_query = (
            jnp.einsum("hqk,khd->qhd", d_scores, key_heads, preferred_element_type=jnp.float32)
            * factor
        )
        d_key_part = (
            jnp.einsum("hqk,qhd->khd", d_scores, query_heads, preferred_element_type=jnp.float32)
            * factor
        )
        d_value_part = jnp.einsum(
            "hqk,qhd->khd", probs_low, d_heads, preferred_element_type=jnp.float32
        )
        d_keys, d_values = (
            lax.psum_scatter(
                d_key_part.reshape(total, width), "ctx", scatter_dimension=0, tiled=True
            ),
            lax.psum_scatter(
                d_value_part.reshape(total, width), "ctx", scatter_dimension=0, tiled=True
            ),
        )
        d_qkv = jnp.concatenate([d_query.reshape(count, width), d_keys, d_values], axis=1).astype(
            jnp.bfloat16
        )
        d_norm1 = jnp.dot(d_qkv, full_qkv.T, preferred_element_type=jnp.float32)
        d_rows_norm, d_gain1 = norm1_back(d_norm1)
        d_rows = cot_rows + d_mid + d_rows_norm + d_logit[:, None] * w_router
        in_grads.append(grad_in.at[rows_index].set(d_rows).astype(jnp.bfloat16))
        sum_router = sum_router + jnp.dot(d_logit, rows, precision=HIGHEST)
        sum_gain_attn = sum_gain_attn + d_gain1
        sum_gain_mlp = sum_gain_mlp + d_gain2
        kept.append((norm1_low, d_qkv, attended_low, d_attn, norm2_low, d_hidden, act_low, d_mlp))
    stacked_rows = tuple((gather_rows(kept, column) for column in range(8)))
    grad_qkv = outer_sum(stacked_rows[0], stacked_rows[1])
    grad_out = outer_sum(stacked_rows[2], stacked_rows[3])
    grad_up = outer_sum(stacked_rows[4], stacked_rows[5])
    grad_down = outer_sum(stacked_rows[6], stacked_rows[7])
    summed = (
        lax.psum_scatter(sum_router, ("ctx", "fsdp"), scatter_dimension=0, tiled=True),
        lax.psum_scatter(sum_gain_attn, ("ctx", "fsdp"), scatter_dimension=0, tiled=True),
        lax.psum_scatter(grad_qkv, ("ctx", "fsdp"), scatter_dimension=0, tiled=True),
        lax.psum_scatter(grad_out, ("ctx", "fsdp"), scatter_dimension=0, tiled=True),
        lax.psum_scatter(sum_gain_mlp, ("ctx", "fsdp"), scatter_dimension=0, tiled=True),
        lax.psum_scatter(grad_up, ("ctx", "fsdp"), scatter_dimension=0, tiled=True),
        lax.psum_scatter(grad_down, ("ctx", "fsdp"), scatter_dimension=0, tiled=True),
    )
    output = jnp.stack(outputs)[:, None]
    input_grad = jnp.stack(in_grads)[:, None]
    return (
        output,
        input_grad,
        summed[0],
        summed[1],
        summed[2],
        summed[3],
        summed[4],
        summed[5],
        summed[6],
    )


ORDER = (0, 2, 1, 3)


def sds(shape, dtype):
    return jax.ShapeDtypeStruct(shape, dtype)


def local(shape, dtype):
    return pltpu.VMEM(shape, dtype)


def near(x):
    return pltpu.with_memory_space_constraint(x, pltpu.VMEM)


class Chain:
    def __init__(self):
        self.last = None

    def __call__(self, kernel, outs, smem, args, scratch=(), name=None, far=(), after=(), weight=WEIGHT):
        count = len(smem) + len(far) + len(args)
        spec = pl.BlockSpec(memory_space=pltpu.VMEM)
        extra = () if self.last is None else (near(self.last),)
        extra = (*extra, *(near(a) for a in after))

        def body(*refs):
            kernel(*refs[:count], *refs[count + len(extra) :])

        results = pl.pallas_call(
            body,
            out_shape=tuple(outs),
            in_specs=[pl.BlockSpec(memory_space=pltpu.SMEM)] * len(smem)
            + [pl.BlockSpec(memory_space=pltpu.HBM)] * len(far)
            + [spec] * (len(args) + len(extra)),
            out_specs=tuple(spec for _ in outs),
            scratch_shapes=list(scratch),
            compiler_params=pltpu.CompilerParams(vmem_limit_bytes=VMEM_LIMIT),
            cost_estimate=pl.CostEstimate(flops=weight, bytes_accessed=weight // 10000, transcendentals=0),
            name=name,
        )(
            *smem, *(pltpu.with_memory_space_constraint(a, pltpu.HBM) for a in far), *(near(a) for a in args), *extra
        )
        if not isinstance(outs[0], jax.ShapeDtypeStruct):
            self.last = results[0]
        return results

    def hold(self, x, *after):
        (x,) = self(hold_kernel, (local(x.shape, x.dtype),), (), (x,), after=after, name="hold", weight=0)
        return x


def hold_kernel(x, out):
    out[...] = x[...]


def mm(left, right):
    return jnp.dot(left, right, preferred_element_type=F32)


def mm_t(left, right):
    return lax.dot_general(left, right, (((1,), (1,)), ((), ())), preferred_element_type=F32)


def t_mm(left, right):
    return lax.dot_general(left, right, (((0,), (0,)), ((), ())), preferred_element_type=F32)


def exchange(x, axis, size, mask):
    return lax.ppermute(x, axis, [(i, i ^ mask) for i in range(size)])


def rms_factor(values):
    return lax.rsqrt(jnp.mean(values * values, axis=-1, keepdims=True) + EPSILON)


def aligned(start, unit):
    return pl.multiple_of(start, unit)


def iota(shape, axis):
    return lax.broadcasted_iota(jnp.int32, shape, axis)


def picks(ids, routed, micro, tok_dev):
    index = routed[micro : micro + 1, :] - ids[0] * tok_dev
    shape = (tok_dev, routed.shape[1])
    return jnp.where(iota(shape, 0) == index, 1.0, 0.0)


def share_peers(ids, bit):
    return ids[1], ids[1] ^ 1, ids[1] ^ (2 + ((ids[0] >> bit) & 1))


def share_rows(c, f, bit):
    side = (c >> bit) & 1
    return f, f ^ 1, f ^ (2 + side), f ^ (3 - side)


def cut_qkv(ids, half, w_qkv, pieces, sem, first, by_y=True):
    width = w_qkv.shape[1] // 3
    copies = []
    peers = share_peers(ids, 0) if by_y else tuple(ids[1] ^ k for k in range(4))
    for k, (peer, piece) in enumerate(zip(peers, pieces)):
        for b in range(3):
            start = b * width + peer * (width // 4) + half * 128
            copies.append(
                pltpu.make_async_copy(
                    w_qkv.at[:, pl.ds(aligned(start, 128), 128)],
                    piece.at[:, pl.ds(b * 128, 128)],
                    sem.at[first + 3 * k + b],
                )
            )
    return copies


def front_kernel(ids, deal, tokens, w_qkv, routed, rowsx, p0, p1, p2, near_tokens, sem):
    micros, tok_dev, width = tokens.shape
    per = routed.shape[1]
    count = micros * per
    span = tok_dev // 2
    first = pltpu.make_async_copy(tokens, near_tokens, sem.at[0])
    first.start()
    copies = cut_qkv(ids, ids[0] >> 2, w_qkv, (p0, p1, p2), sem, 1)
    for copy in copies:
        copy.start()
    stored = routed[...]
    chunk = stored // span
    anchor = jnp.zeros_like(stored)
    for entry in range(deal.shape[0]):
        anchor = jnp.where(chunk == entry, deal[entry], anchor)
    place = ((anchor * span + stored % span) // BLOCK).astype(F32)
    rowsx[count:] = jnp.zeros((8, width), BF16)
    for micro in range(micros):
        rowsx[count + micro : count + micro + 1, :per] = place[micro : micro + 1].astype(BF16)
    first.wait()
    for micro in range(micros):
        pick = picks(ids, routed, micro, tok_dev).astype(BF16)
        rowsx[micro * per : (micro + 1) * per] = t_mm(pick, near_tokens[micro]).astype(BF16)
    for copy in copies:
        copy.wait()


def run(copies):
    for copy in copies:
        copy.start()
    for copy in copies:
        copy.wait()


def cut_up_kernel(ids, w_up, p0, p1, p2, sem):
    share = p0.shape[1]
    run(
        [
            pltpu.make_async_copy(
                w_up.at[:, pl.ds(aligned(peer * share, share), share)], piece, sem.at[k]
            )
            for k, (peer, piece) in enumerate(zip(share_peers(ids, 0), (p0, p1, p2)))
        ]
    )


def cut_rest_kernel(ids, w_qkv, v0, v1, v2, v3, sem):
    run(cut_qkv(ids, 1 - (ids[0] >> 2), w_qkv, (v0, v1, v2, v3), sem, 0, False))


def cot_kernel(ids, routed, cot, rowsx, both):
    micros, tok_dev = cot.shape[:2]
    per = routed.shape[1]
    start = rowsx.shape[0]
    both[:start] = rowsx[...]
    for micro in range(micros):
        pick = picks(ids, routed, micro, tok_dev).astype(BF16)
        both[start + micro * per : start + (micro + 1) * per] = t_mm(pick, cot[micro]).astype(BF16)


def rows_of(both):
    return both[: both.shape[0] // 2 - 4].astype(F32)


def cots_of(both):
    return both[both.shape[0] // 2 + 4 :].astype(F32)


def d_mlp_kernel(b0, b1, b2, b3, w_router, d_mlp, gate_out):
    count = gate_out.shape[1]
    for i, both in enumerate((b0, b1, b2, b3)):
        gate = jax.nn.sigmoid(jnp.sum(rows_of(both) * w_router[...], axis=1, keepdims=True))
        d_mlp[i * count : (i + 1) * count] = (gate * cots_of(both)).astype(BF16)
        gate_out[i] = gate


def head_masks():
    lanes = iota((1, 128), 1)
    low = jnp.where(lanes < 64, 1.0, 0.0)
    return low, 1.0 - low


def attend_kernel(
    ids, near_rows, far_rows, gain, w0, w1, w2, w3,
    far, own, stack, probs, norm1, place_col, result,
):
    c, f = ids[0], ids[1]
    micros, total = stack.shape[0], stack.shape[1]
    count = own.shape[1]
    per = count // micros
    eye = iota((per, 128), 0) == iota((per, 128), 1)
    step = count + 8
    for h, source in enumerate((near_rows, far_rows)):
        for b in range(4):
            rows = source[b * step : b * step + count].astype(F32)
            index = ((c >> 2) ^ h) * 4 + b
            norm1[pl.ds(aligned(index * count, 16), count)] = (
                rows * rms_factor(rows) * gain[...]
            ).astype(BF16)
            places = source[b * step + count : b * step + count + 8, :128].astype(F32)
            for m in range(micros):
                col = jnp.sum(jnp.where(eye, places[m : m + 1], 0.0), axis=1, keepdims=True)
                place_col[m, pl.ds(aligned(index * per, per), per), :] = jnp.broadcast_to(
                    col, (per, 128)
                )
    qkv = jnp.zeros((8 * count, 384), F32)
    for peer, w in zip(share_rows(c, f, 0), (w0, w1, w2, w3)):
        part = w.shape[0]
        qkv = qkv + mm(norm1[:, pl.ds(aligned(peer * part, part), part)], w[...])
    low = qkv.astype(BF16)
    for t in range(8):
        for m in range(micros):
            stack[m, t * per : (t + 1) * per, :] = low[
                t * count + m * per : t * count + (m + 1) * per
            ]
    big_eye = iota((total, total), 0) == iota((total, total), 1)
    masks = head_masks()
    for m in range(micros):
        q, k, v = stack[m, :, :128], stack[m, :, 128:256], stack[m, :, 256:384]
        mine = place_col[m, :, 0:1]
        theirs = jnp.sum(jnp.where(big_eye, mine, 0.0), axis=0, keepdims=True)
        visible = theirs <= mine
        attended = jnp.zeros((total, 128), F32)
        for h in range(2):
            scores = mm_t(q * masks[h].astype(BF16), k) * (HEAD_DIM**-0.5)
            scores = jnp.where(visible, scores, MASKED)
            top = jnp.max(scores, axis=1, keepdims=True)
            grown = jnp.exp(scores - top)
            weight = grown / jnp.sum(grown, axis=1, keepdims=True)
            probs[2 * m + h] = weight
            attended = attended + mm(weight.astype(BF16), v) * masks[h]
        result[m] = attended.astype(BF16)
        for k in range(8):
            out = far if k >= 4 else own
            out[k & 3, m * per : (m + 1) * per, :] = result[
                m, pl.ds(aligned((c ^ k) * per, per), per), :
            ]


def row_slot(f, s, count):
    k = s ^ f
    return aligned(((k & 1) * 2 + (k >> 1)) * count, 16)


def split_rows(full, send, keep):
    count = send.shape[1]
    for i in range(2):
        keep[i] = full[i * count : (i + 1) * count]
        send[i] = full[(2 + i) * count : (3 + i) * count].astype(BF16)


def block_place(ids, k, count, lanes):
    peer = ids[0] ^ k
    columns = aligned((peer >> 2) * lanes, 128)
    return pl.ds(row_slot(ids[1], peer & 3, count), count), pl.ds(columns, lanes)


def out_kernel(ids, b0, b1, b2, b3, w_out, attended, send, keep, full):
    count = b0.shape[1]
    for k, block in enumerate((b0, b1, b2, b3)):
        for far in range(2):
            attended[block_place(ids, k ^ (4 * far), count, 128)] = block[far]
    full[...] = mm(attended[...], w_out[...])
    split_rows(full, send, keep)


def add_both_kernel(keep, received, total):
    total[...] = (keep[...] + received[...].astype(F32)).astype(BF16)


def add_own_kernel(keep, received, send2, keep2):
    send2[...] = (keep[1] + received[1].astype(F32)).astype(BF16)
    keep2[...] = keep[0] + received[0].astype(F32)


def mid_kernel(low, received, both0, both1, gain, attn, norm2):
    for i, both in enumerate((both0, both1)):
        value = low[i].astype(F32) + received[1 - i].astype(F32)
        attn[i] = value
        mid = rows_of(both) + value
        norm2[i] = (mid * rms_factor(mid) * gain[...]).astype(BF16)


def mlp_kernel(
    ids, n0, n1, d_mlp, u0, u1, u2, u3, w_down,
    send, keep, act_send, d_send, act_keep, d_keep, norm2, act, d_hidden, back,
):
    c = ids[0]
    part = u0.shape[0]
    count = n0.shape[1]
    shares = tuple(zip(share_rows(ids[0], ids[1], 0), (u0, u1, u2, u3)))
    for i in range(2):
        norm2[i * count : (i + 1) * count] = n0[i]
        norm2[(2 + i) * count : (3 + i) * count] = n1[i]
    hidden = jnp.zeros(act.shape, F32)
    for peer, u in shares:
        hidden = hidden + mm(norm2[:, pl.ds(aligned(peer * part, part), part)], u[...])
    d_act = mm_t(d_mlp[...], w_down[...])
    phi = 0.5 * (1.0 + lax.erf(hidden * (0.5**0.5)))
    act[...] = (hidden * phi).astype(BF16)
    slope = phi + hidden * jnp.exp(-0.5 * hidden * hidden) * ((2.0 * math.pi) ** -0.5)
    d_hidden[...] = (d_act * slope).astype(BF16)
    for i, (some_act, some_d) in enumerate(((act_keep, d_keep), (act_send, d_send))):
        for high in range(2):
            start = aligned(high * 512 + (((c >> 1) & 1) ^ i) * 256, 128)
            some_act[:, high * 256 : (high + 1) * 256] = act[:, pl.ds(start, 256)]
        some_d[...] = d_hidden[:, pl.ds(aligned(((c & 1) ^ i) * 512, 128), 512)]
    for peer, u in shares:
        back[:, pl.ds(aligned(peer * part, part), part)] = mm_t(d_hidden[...], u[...])
    split_rows(back, send, keep)


def mlp_out_kernel(act, w_down, attn, gate, b0, b1, b2, b3, send, keep, router, full):
    full[...] = mm(act[...], w_down[...])
    split_rows(full, send, keep)
    count = gate.shape[1]
    total = jnp.zeros(router.shape, F32)
    for i, both in enumerate((b0, b1, b2, b3)):
        own = slice(i * count, (i + 1) * count)
        part = jnp.sum(cots_of(both) * (attn[own] + full[own]), axis=1, keepdims=True)
        part = part * gate[i] * (1.0 - gate[i])
        total = total + jnp.sum(rows_of(both) * part, axis=0, keepdims=True)
    router[...] = total


def pick_rows(c, peer, share, out, lanes):
    @pl.when(peer == (c >> 1))
    def _():
        out[:, lanes] = share[pl.ds(aligned((c & 1) * 128, 128), 128), :]


def pick_kernel(ids, *refs):
    shares, (up_rows, qkv_rows) = refs[:12], refs[12:]
    c, f = ids[0], ids[1]
    for peer, u in zip(share_rows(c, f, 0), shares[:4]):
        pick_rows(c, peer, u, up_rows, slice(None))
    for peer, a in zip(share_rows(c, f, 0), shares[4:8]):
        pick_rows(c, peer, a, qkv_rows, slice(0, 384))
    for k, b in enumerate(shares[8:]):
        pick_rows(c, f ^ k, b, qkv_rows, slice(384, 768))


def chunk(f, q):
    return pl.ds(aligned((f ^ q) * 32, 32), 32)


def grad_up_kernel(ids, norm2, near_a, near_b, d_own, d_near, send, keep, rows, columns):
    count = norm2.shape[0]
    half = count // 2
    rows[:count] = norm2[...]
    for i in range(2):
        rows[count + i * (half // 2) : count + (i + 1) * (half // 2)] = near_a[i]
        rows[count + half + i * (half // 2) : count + half + (i + 1) * (half // 2)] = near_b[i]
    columns[:count] = d_own[...]
    columns[count:] = d_near[...]
    for place, (target, index) in enumerate(((keep, 0), (send, 0), (keep, 1), (send, 1))):
        kk = (0, 1, 2, 3)[place]
        start = aligned(((ids[0] >> 1) ^ kk) * 256, 128)
        value = t_mm(rows[:, pl.ds(start, 256)], columns[...])
        for owner in range(2):
            for q in range(4):
                at = pl.ds(aligned(((ids[0] & 1) ^ owner) * 128 + (ids[1] ^ q) * 32, 32), 32)
                piece = value[owner * 128 + q * 32 : owner * 128 + (q + 1) * 32]
                target[index, at] = piece.astype(target.dtype)


def grad_down_kernel(ids, d_mlp, near_a, near_b, a_own, a_near, send, keep, rows, columns):
    count = d_mlp.shape[0]
    half = count // 2
    rows[:count] = d_mlp[...]
    rows[count : count + half] = near_a[...]
    rows[count + half :] = near_b[...]
    columns[:count] = a_own[...]
    columns[count:] = a_near[...]
    c = ids[0]
    for target, index, k in ((keep, 0, 0), (send, 0, 1), (keep, 1, 4), (send, 1, 5)):
        start = aligned(((c >> 2) ^ (k >> 2)) * 256 + ((c & 1) ^ (k & 1)) * 128, 128)
        value = t_mm(columns[:, pl.ds(start, 128)], rows[...])
        target[index] = value.astype(target.dtype)


def grad_attn_kernel(
    ids, norm1, b0, b1, b2, b3, b4, b5, b6, b7, attended, d_attn, router,
    keep, send1, send2, send3, joined, full,
):
    count = b0.shape[0]
    for k, block in enumerate((b0, b1, b2, b3, b4, b5, b6, b7)):
        joined[pl.ds(aligned((ids[0] ^ k) * count, 16), count)] = block[...]
    full[...] = t_mm(attended[...], d_attn[...])
    for k in range(8):
        target, index = (keep, send1, send2, send3)[k & 3], k >> 2
        owner = ids[0] ^ k
        start = aligned(owner * 128, 128)
        value = t_mm(norm1[:, pl.ds(start, 128)], joined[...])
        for q in range(4):
            piece = value[q * 32 : (q + 1) * 32]
            target[index, chunk(ids[1], q), :384] = piece.astype(target.dtype)
            rows = full[pl.ds(aligned(owner * 32, 32), 32), q * 256 : (q + 1) * 256]
            target[index, q * 32 : (q + 1) * 32, 384:640] = rows.astype(target.dtype)
        target[index, 128:136, :] = jnp.zeros((8, 640), target.dtype)
        share = jnp.broadcast_to(router[:, pl.ds(start, 128)], (8, 128))
        target[index, 128:136, 384:512] = share.astype(target.dtype)


def sum_attn_kernel(keep, got1, got2, got3, send, mine):
    for index, target in ((0, mine), (1, send)):
        total = (keep[index] + got1[index].astype(F32)) + (
            got2[index].astype(F32) + got3[index].astype(F32)
        )
        target[0] = total.astype(target.dtype)


def d_attn_kernel(low, received, attn, both0, both1, gate, gain, d_mid_out, d_attn):
    for i, both in enumerate((both0, both1)):
        mid = rows_of(both) + attn[i]
        r2 = rms_factor(mid)
        d_norm2 = low[i].astype(F32) + received[1 - i].astype(F32)
        t2 = d_norm2 * gain[...]
        d_mid = r2 * t2 - mid * (r2 * r2 * r2) * jnp.mean(t2 * mid, axis=1, keepdims=True)
        d_attn[i] = (gate[i] * cots_of(both) + d_mid).astype(BF16)
        if i == 0:
            d_mid_out[...] = d_mid


def d_attended_kernel(ids, d0, d1, w_out, far, own, d_attn, d_att):
    count = d0.shape[1]
    for i in range(2):
        d_attn[i * count : (i + 1) * count] = d0[i]
        d_attn[(2 + i) * count : (3 + i) * count] = d1[i]
    d_att[...] = mm_t(d_attn[...], w_out[...])
    for k in range(8):
        block = far if k >= 4 else own
        block[k & 3] = d_att[block_place(ids, k, count, 128)].astype(BF16)


def attend_back_kernel(ids, *refs):
    blocks, (stack, probs), outs, (d_stack, result) = refs[:4], refs[4:6], refs[6:14], refs[14:]
    micros, total = stack.shape[0], stack.shape[1]
    count = outs[0].shape[0]
    per = count // micros
    masks = head_masks()
    for m in range(micros):
        rows = slice(m * per, (m + 1) * per)
        for k in range(8):
            d_stack[pl.ds(aligned((ids[0] ^ k) * per, per), per), :] = blocks[k & 3][k >> 2, rows]
        q, k, v = stack[m, :, :128], stack[m, :, 128:256], stack[m, :, 256:384]
        d_out = d_stack[...]
        d_q = jnp.zeros((total, 128), F32)
        d_k = jnp.zeros((total, 128), F32)
        d_v = jnp.zeros((total, 128), F32)
        for h in range(2):
            weight = probs[2 * m + h]
            d_probs = mm_t(d_out * masks[h].astype(BF16), v)
            inner = jnp.sum(weight * d_probs, axis=1, keepdims=True)
            d_scores = (weight * (d_probs - inner)).astype(BF16)
            d_q = d_q + mm(d_scores, k) * masks[h]
            d_k = d_k + t_mm(d_scores, q) * masks[h]
            d_v = d_v + t_mm(weight.astype(BF16), d_out) * masks[h]
        result[m, :, :128] = (d_q * (HEAD_DIM**-0.5)).astype(BF16)
        result[m, :, 128:256] = (d_k * (HEAD_DIM**-0.5)).astype(BF16)
        result[m, :, 256:384] = d_v.astype(BF16)
        for k in range(8):
            outs[k][rows] = result[m, pl.ds(aligned((ids[0] ^ k) * per, per), per), :]


def d_norm1_kernel(
    ids, d0, d1, d2, d3, d4, d5, d6, d7, a0, a1, a2, a3, b0, b1, b2, b3,
    send, keep, d_qkv, full,
):
    c, f = ids[0], ids[1]
    count = d0.shape[0]
    part = a0.shape[0]
    for k, block in enumerate((d0, d1, d2, d3, d4, d5, d6, d7)):
        rows = pl.ds(row_slot(f, (c ^ k) & 3, count), count)
        d_qkv[rows, (k >> 2) * 384 : (k >> 2) * 384 + 384] = block[...]
    for peer, a in zip(share_rows(c, f, 0), (a0, a1, a2, a3)):
        full[:, pl.ds(aligned(peer * part, part), part)] = mm_t(d_qkv[:, :384], a[...])
    for k, b in enumerate((b0, b1, b2, b3)):
        columns = pl.ds(aligned((f ^ k) * part, part), part)
        full[:, columns] = full[:, columns] + mm_t(d_qkv[:, 384:], b[...])
    split_rows(full, send, keep)


def place_rows(ids, routed, micro, source, rows, out):
    tok_dev = source.shape[0]
    pick = picks(ids, routed, micro, tok_dev)
    changed = jnp.sum(pick, axis=1, keepdims=True) > 0.5
    placed = mm(pick.astype(BF16), rows)
    out[...] = jnp.where(changed, placed, source[...].astype(F32)).astype(BF16)


def output_kernel(
    ids, routed, keep, received, attn, both, gate, tokens, d_logit_out, output,
):
    count = keep.shape[0]
    micros = tokens.shape[0]
    per = count // micros
    branch = attn[0] + keep[...] + received[...].astype(F32)
    rows = rows_of(both)
    open_gate = gate[0]
    d_logit = (
        jnp.sum(cots_of(both) * branch, axis=1, keepdims=True)
        * open_gate
        * (1.0 - open_gate)
    )
    d_logit_out[...] = d_logit
    result = (rows + open_gate * branch).astype(BF16)
    for micro in range(micros):
        own = result[micro * per : (micro + 1) * per]
        place_rows(ids, routed, micro, tokens.at[micro], own, output.at[micro])


def input_grad_kernel(
    ids, routed, keep, received, d_mid, both, d_logit, w_router, gain, cot, input_grad,
):
    count = keep.shape[0]
    micros = cot.shape[0]
    per = count // micros
    rows = rows_of(both)
    r1 = rms_factor(rows)
    t1 = (keep[...] + received[...].astype(F32)) * gain[...]
    d_rows = (
        cots_of(both)
        + d_mid[...]
        + r1 * t1
        - rows * (r1 * r1 * r1) * jnp.mean(t1 * rows, axis=1, keepdims=True)
        + d_logit[...] * w_router[...]
    ).astype(BF16)
    for micro in range(micros):
        own = d_rows[micro * per : (micro + 1) * per]
        place_rows(ids, routed, micro, cot.at[micro], own, input_grad.at[micro])


def as_row(column):
    count = column.shape[0]
    eye = iota((count, count), 0) == iota((count, count), 1)
    return jnp.sum(jnp.where(eye, column, 0.0), axis=0, keepdims=True)


def owned(ids, vector, count):
    start = (4 * ids[0] + ids[1]) * count
    shape = (count, vector.shape[1])
    hit = iota(shape, 1) == iota(shape, 0) + start
    return jnp.sum(jnp.where(hit, vector[...], 0.0), axis=1, keepdims=True)


def join_up_kernel(ids, p0, p1, p2, p3, gain, token, out, grad_gain):
    token[...] = jnp.zeros(token.shape, F32)
    rows, part = out.shape[0], out.shape[1] // 4
    total = jnp.zeros((rows, 1), F32)
    for k, piece in enumerate((p0, p1, p2, p3)):
        out[:, pl.ds(aligned((ids[1] ^ k) * part, part), part)] = piece[:, :part].astype(F32)
        total = total + piece[:, part : part + 128].astype(F32)[:, :1]
    grad_gain[...] = as_row(total / owned(ids, gain, rows))


def join_qkv_kernel(ids, p0, p1, p2, p3, gain, out, grad_gain, grad_router):
    rows, width = out.shape[0], out.shape[1] // 3
    part = width // 4
    total = jnp.zeros((rows, 1), F32)
    router = jnp.zeros((rows, 1), F32)
    for k, piece in enumerate((p0, p1, p2, p3)):
        for half in range(2):
            for b in range(3):
                start = b * width + (ids[1] ^ k) * part + ((ids[0] >> 2) ^ half) * 128
                out[:, pl.ds(aligned(start, 128), 128)] = piece[
                    :, (3 * half + b) * 128 : (3 * half + b + 1) * 128
                ].astype(F32)
        total = total + piece[:, 768:896].astype(F32)[:, :1]
        router = router + piece[:, 896:1024].astype(F32)[:, :1]
    grad_gain[...] = as_row(total / owned(ids, gain, rows))
    grad_router[...] = as_row(router)


def join_down_kernel(block, token, out):
    token[...] = jnp.zeros(token.shape, F32)
    out[...] = block[...].astype(F32)


def hop2_kernel(keep_u, got_u, keep_d, got_d, send, own_u, own_d):
    for i in range(2):
        total = keep_u[i] + got_u[i].astype(F32)
        half, width = total.shape[0] // 2, total.shape[1]
        if i:
            send[0, :, :width] = total[:half].astype(BF16)
            send[0, :, width:] = total[half:].astype(BF16)
        else:
            own_u[...] = total
    own_d[...] = keep_d[0] + got_d[0].astype(F32)
    send[1] = (keep_d[1] + got_d[1].astype(F32)).astype(BF16)


def hop3_kernel(own_u, own_d, got, send, mine, down):
    half, width = own_u.shape[0] // 2, own_u.shape[1]
    mine[...] = own_u[:half] + got[0, :, :width].astype(F32)
    send[...] = (own_u[half:] + got[0, :, width:].astype(F32)).astype(BF16)
    down[...] = (own_d[...] + got[1].astype(F32)).astype(BF16)


def up_pieces_kernel(ids, mine, other, w_rows, c0, c1, c2, c3):
    rows, half = c0.shape[0], mine.shape[1]
    y = ids[0] & 1
    for k, piece in enumerate((c0, c1, c2, c3)):
        own = slice(k * rows, (k + 1) * rows)
        weights = pl.ds(aligned((ids[1] ^ k) * rows, rows), rows)
        total = jnp.zeros((rows, 1), F32)
        for side, value in ((y, mine[own]), (1 - y, other[own].astype(F32))):
            columns = pl.ds(aligned(side * half, 128), half)
            piece[:, columns] = value.astype(BF16)
            total = total + jnp.sum(
                value * w_rows[weights, columns].astype(F32), axis=1, keepdims=True
            )
        piece[:, 2 * half :] = jnp.broadcast_to(total, (rows, 128)).astype(BF16)


def pieces_kernel(ids, mine, got, w_rows, c0, c1, c2, c3, out):
    rows = c0.shape[0]
    router = mine[0, 128:129, 384:512] + got[0, 128:136, 384:512].astype(F32)[0:1]
    for k, piece in enumerate((c0, c1, c2, c3)):
        own = slice(k * rows, (k + 1) * rows)
        first = (ids[1] ^ k) * rows
        weights = pl.ds(aligned(first, rows), rows)
        a, b = mine[0, own, :384], got[0, own, :384].astype(F32)
        piece[:, :384] = a.astype(BF16)
        piece[:, 384:768] = b.astype(BF16)
        total = jnp.sum(a * w_rows[weights, :384].astype(F32), axis=1, keepdims=True)
        total = total + jnp.sum(b * w_rows[weights, 384:].astype(F32), axis=1, keepdims=True)
        piece[:, 768:896] = jnp.broadcast_to(total, (rows, 128)).astype(BF16)
        hit = iota((rows, 128), 1) == iota((rows, 128), 0) + first
        share = jnp.sum(jnp.where(hit, router, 0.0), axis=1, keepdims=True)
        piece[:, 896:] = jnp.broadcast_to(share, (rows, 128)).astype(BF16)
        out[:, k * 256 : (k + 1) * 256] = mine[0, own, 384:640] + got[0, own, 384:640].astype(F32)


def all_rows_sum(call, send, keep, after=()):
    received = exchange(send, "fsdp", 4, 1)
    (low,) = call(
        add_both_kernel, (local(keep.shape, BF16),), (), (keep, received), name="add_both", after=after
    )
    return low, exchange(low, "fsdp", 4, 2)


def own_rows_sum(call, send, keep):
    received = exchange(send, "fsdp", 4, 1)
    shape = keep.shape[1:]
    send2, keep2 = call(
        add_own_kernel, (local(shape, BF16), local(shape, F32)), (), (keep, received), name="add_own"
    )
    return keep2, exchange(send2, "fsdp", 4, 2)


def swap_blocks(blocks):
    got = {k: exchange(blocks[k], "ctx", 8, k) for k in (7, 6, 5, 4, 3, 2, 1)}
    return (blocks[0], *(got[k] for k in range(1, 8)))


def swap_across(across, bit):
    return lax.ppermute(
        across, ("ctx", "fsdp"),
        [(4 * a + b, 4 * a + (b ^ (2 + ((a >> bit) & 1)))) for a in range(8) for b in range(4)],
    )


def pair_kernel(own, far, *outs):
    for k, out in enumerate(outs):
        out[0] = own[k]
        out[1] = far[k]


def swap_in_two(call, own, far, *after):
    came = exchange(far, "ctx", 8, 4)
    shape = (2, *own.shape[1:])
    pairs = call(pair_kernel, (local(shape, own.dtype),) * 4, (), (own, came), name="pair", after=after)
    return (pairs[0], *(exchange(pairs[k], "ctx", 8, k) for k in (1, 2, 3)))


def swap_pieces(pieces):
    return (pieces[0], *(exchange(pieces[k], "fsdp", 4, k) for k in (1, 2, 3)))


def shards_8x4(
    tokens, w_router, gain_attn, w_qkv, w_out, gain_mlp, w_up, w_down, routed, deal, cotangent
):
    micros, tok_dev, width = tokens.shape[0], tokens.shape[2], tokens.shape[3]
    per = routed.shape[2]
    count = micros * per
    total = 8 * per
    part = width // 4
    hidden = w_down.shape[0]
    c, f = lax.axis_index("ctx"), lax.axis_index("fsdp")
    ids = jnp.stack([c, f]).astype(jnp.int32)
    tok, cot, routed = tokens[:, 0], cotangent[:, 0], routed[:, 0]
    w_router, gain_attn, gain_mlp = (
        w_router.reshape(1, width), gain_attn.reshape(1, width), gain_mlp.reshape(1, width),
    )
    rows_bf, rows_f = local((count, width), BF16), local((count, width), F32)
    pair_bf, pair_f = local((2, count, width), BF16), local((2, count, width), F32)
    all_bf, all_quarter = local((4 * count, width), BF16), local((4 * count, part), BF16)
    hidden_bf = local((4 * count, hidden), BF16)
    vector = local((1, width), F32)
    dma = pltpu.SemaphoreType.DMA
    call = Chain()

    rowsx, *w_parts = call(
        front_kernel,
        (local((count + 8, width), BF16), *(local((part, 384), BF16),) * 3),
        (ids, deal), (routed,), far=(tok, w_qkv),
        scratch=[pltpu.VMEM(tok.shape, BF16), dma((10,))], name="front",
    )
    turn = [(4 * a + b, 4 * ((a & 4) | b) + (a & 3)) for a in range(8) for b in range(4)]
    turned = lax.ppermute(rowsx, ("ctx", "fsdp"), turn)
    turned_far = exchange(turned, "ctx", 8, 4)
    w_mine, w_beside, w_across = w_parts
    w_across = swap_across(w_across, 0)
    up_mine, up_beside, up_across = call(
        cut_up_kernel, (local((part, hidden), BF16),) * 3, (ids,), (), far=(w_up,),
        scratch=[dma((3,))], name="cut_up", weight=0,
    )
    near_rows = lax.all_gather(turned, "fsdp", axis=0, tiled=True)
    far_rows = lax.all_gather(turned_far, "fsdp", axis=0, tiled=True)
    w_across = call.hold(w_across, near_rows)
    up_across = call.hold(up_across, far_rows)
    w_parts = (w_mine, exchange(w_beside, "fsdp", 4, 1), w_across, exchange(w_across, "ctx", 8, 1))
    up_beside, up_across = exchange(up_beside, "fsdp", 4, 1), swap_across(up_across, 0)
    far_heads, heads, stack, probs, norm1 = call(
        attend_kernel,
        (
            *(local((4, count, 128), BF16),) * 2, local((micros, total, 384), BF16),
            local((2 * micros, total, total), F32), local((8 * count, width), BF16),
        ),
        (ids,), (near_rows, far_rows, gain_attn, *w_parts),
        scratch=[pltpu.VMEM((micros, total, 128), F32), pltpu.VMEM((micros, total, 128), BF16)],
        name="attend",
    )
    (both,) = call(
        cot_kernel, (local((2 * count + 8, width), BF16),), (ids,), (routed, cot, rowsx), name="cot_rows",
        weight=0,
    )
    both_x, both_c = exchange(both, "fsdp", 4, 2), exchange(both, "fsdp", 4, 1)
    both_xc = exchange(both_x, "fsdp", 4, 1)
    rest = call(
        cut_rest_kernel, (local((part, 384), BF16),) * 4, (ids,), (), far=(w_qkv,),
        scratch=[dma((12,))], name="cut_rest", weight=0,
    )
    heads = swap_in_two(call, heads, far_heads, up_across)
    attended, send, keep, attn_part = call(
        out_kernel, (all_quarter, pair_bf, pair_f, local((4 * count, width), F32)),
        (ids,), (*heads, w_out), name="attn_out", after=(up_across, both_x),
    )
    up_parts = (up_mine, up_beside, up_across, exchange(up_across, "ctx", 8, 1))
    rest = swap_pieces(rest)
    low, received = all_rows_sum(call, send, keep)
    d_mlp, gate = call(
        d_mlp_kernel, (all_bf, local((4, count, 1), F32)), (),
        (both, both_x, both_c, both_xc, w_router), name="d_mlp", weight=0,
    )
    d_mlp_a = exchange(d_mlp[: 2 * count], "ctx", 8, 2)
    d_mlp_b = exchange(d_mlp_a, "fsdp", 4, 1)
    attn, norm2 = call(
        mid_kernel, (pair_f, pair_bf), (), (low, received, both, both_x, gain_mlp), name="mid",
    )
    norm2_a = exchange(norm2, "ctx", 8, 1)
    norm2_b = exchange(norm2_a, "fsdp", 4, 1)
    half_bf = local((4 * count, hidden // 2), BF16)
    send, keep, act_send, d_send, act_keep, d_keep, norm2, act = call(
        mlp_kernel, (pair_bf, pair_f, half_bf, half_bf, half_bf, half_bf, all_bf, hidden_bf), (ids,),
        (norm2, exchange(norm2, "fsdp", 4, 1), d_mlp, *up_parts, w_down),
        scratch=[pltpu.VMEM((4 * count, hidden), BF16), pltpu.VMEM((4 * count, width), F32)],
        name="mlp",
    )
    d_near, act_near = exchange(d_send, "ctx", 8, 1), exchange(act_send, "ctx", 8, 2)
    low, received = all_rows_sum(call, send, keep, (norm2_a, d_mlp_a))
    d_mid, d_attn = call(
        d_attn_kernel, (rows_f, pair_bf), (),
        (low, received, attn, both, both_x, gate, gain_mlp), name="d_attn",
        after=(d_near, act_near),
    )
    far_heads, d_heads, d_attn = call(
        d_attended_kernel, (*(local((4, count, 128), BF16),) * 2, all_bf), (ids,),
        (d_attn, exchange(d_attn, "fsdp", 4, 1), w_out),
        scratch=[pltpu.VMEM((4 * count, part), F32)], name="d_attended",
    )
    send_u, keep_u = call(
        grad_up_kernel, (local((2, 256, hidden // 2), BF16), local((2, 256, hidden // 2), F32)), (ids,),
        (norm2, norm2_a, norm2_b, d_keep, d_near), name="grad_up", weight=0,
        scratch=[pltpu.VMEM((8 * count, width), BF16), pltpu.VMEM((8 * count, hidden // 2), BF16)],
    )
    send_d, keep_d = call(
        grad_down_kernel, (local((2, 128, width), BF16), local((2, 128, width), F32)), (ids,),
        (d_mlp, d_mlp_a, d_mlp_b, act_keep, act_near), name="grad_down", weight=0,
        scratch=[pltpu.VMEM((8 * count, width), BF16), pltpu.VMEM((8 * count, hidden // 2), BF16)],
    )
    got_u, got_d = exchange(send_u, "ctx", 8, 2), exchange(send_d, "ctx", 8, 1)
    d_heads = swap_in_two(call, d_heads, far_heads)
    d_blocks = call(
        attend_back_kernel, (local((count, 384), BF16),) * 8, (ids,), (*d_heads, stack, probs),
        scratch=[pltpu.VMEM((total, 128), BF16), pltpu.VMEM((micros, total, 384), BF16)],
        name="attend_back", after=(*rest[1:], got_u, got_d),
    )
    d_own = swap_blocks(d_blocks)
    send_z, own_u, own_d = call(
        hop2_kernel,
        (local((2, 128, width), BF16), local((256, hidden // 2), F32), local((128, width), F32)),
        (), (keep_u, got_u, keep_d, got_d), name="hop2", weight=0,
    )
    got_z = exchange(send_z, "ctx", 8, 4)
    owners = [(4 * a + b, 4 * (2 * b + a // 4) + a % 4) for a in range(8) for b in range(4)]
    send_m, keep_m, router = call(
        mlp_out_kernel, (pair_bf, pair_f, vector), (),
        (act, w_down, attn_part, gate, both, both_x, both_c, both_xc), name="mlp_out", weight=0,
        scratch=[pltpu.VMEM((4 * count, width), F32)],
    )
    part_bf = local((2, 136, 640), BF16)
    keep_q, *send_q = call(
        grad_attn_kernel, (local((2, 136, 640), F32), part_bf, part_bf, part_bf), (ids,),
        (norm1, *d_blocks, attended, d_attn, router), name="grad_attn", weight=0,
        scratch=[pltpu.VMEM((8 * count, 384), BF16), pltpu.VMEM((part, width), F32)],
    )
    got_q = [exchange(x, "ctx", 8, k + 1) for k, x in enumerate(send_q)]
    send, keep = call(
        d_norm1_kernel, (pair_bf, pair_f), (ids,),
        (*d_own, *w_parts, *rest), name="d_norm1",
        scratch=[pltpu.VMEM((4 * count, 768), BF16), pltpu.VMEM((4 * count, width), F32)],
    )
    keep, received = own_rows_sum(call, send, keep)
    keep_m, received_m = own_rows_sum(call, send_m, keep_m)
    send_u, mine_u, down = call(
        hop3_kernel,
        (local((128, hidden // 2), BF16), local((128, hidden // 2), F32), local((128, width), BF16)),
        (), (own_u, own_d, got_z), name="hop3", weight=0,
    )
    down = lax.ppermute(down, ("ctx", "fsdp"), owners)
    other_u = exchange(send_u, "ctx", 8, 1)
    send_q, keep_q = call(
        sum_attn_kernel, (local((1, 136, 640), BF16), local((1, 136, 640), F32)), (),
        (keep_q, *got_q), name="sum_attn", weight=0,
    )
    got_q = exchange(send_q, "ctx", 8, 4)
    d_logit, output = call(
        output_kernel, (local((count, 1), F32), sds(tok.shape, BF16)), (ids,),
        (routed, keep_m, received_m, attn, both, gate, tok), name="output", weight=0,
    )
    (input_grad,) = call(
        input_grad_kernel, (sds(cot.shape, BF16),), (ids,),
        (routed, keep, received, d_mid, both, d_logit, w_router, gain_attn, cot), name="input_grad",
        weight=0,
    )
    w_up_rows, w_qkv_rows = call(
        pick_kernel, (local((128, hidden), BF16), local((128, 768), BF16)), (ids,),
        (*up_parts, *w_parts, *rest), name="pick", weight=0,
    )
    chunks = call(
        up_pieces_kernel, (local((32, hidden + 128), BF16),) * 4, (ids,), (mine_u, other_u, w_up_rows),
        name="up_pieces",
    )
    chunks = swap_pieces(chunks)
    *qkv_chunks, grad_out = call(
        pieces_kernel, (local((32, 1024), BF16),) * 4 + (local((32, width), F32),), (ids,),
        (keep_q, got_q, w_qkv_rows), name="qkv_pieces",
    )
    qkv_chunks = swap_pieces(qkv_chunks)
    grad_out = lax.ppermute(grad_out, ("ctx", "fsdp"), owners)
    row = sds((1, 32), F32)
    token = local((8, 128), F32)
    _, grad_down = call(
        join_down_kernel, (token, sds((128, width), F32)), (), (down,), name="join_down", weight=0
    )
    _, grad_up, grad_gain_mlp = call(
        join_up_kernel, (token, sds((32, 4 * hidden), F32), row), (ids,), (*chunks, gain_mlp),
        name="join_up", weight=0,
    )
    grad_qkv, grad_gain_attn, grad_router = call(
        join_qkv_kernel, (sds((32, 3 * width), F32), row, row), (ids,), (*qkv_chunks, gain_attn),
        name="join_qkv",
    )
    return (
        output[:, None], input_grad[:, None], grad_router[0], grad_gain_attn[0], grad_qkv, grad_out,
        grad_gain_mlp[0], grad_up, grad_down,
    )


def solution(mesh):
    placed = (
        P(None, "fsdp", "ctx", None),
        P(),
        P(),
        P("fsdp", None),
        P("fsdp", None),
        P(),
        P("fsdp", None),
        P("fsdp", None),
        P(None, "fsdp", "ctx"),
        P(),
        P(None, "fsdp", "ctx", None),
    )
    fits = mesh.shape["ctx"] == 8 and mesh.shape["fsdp"] == 4
    return jax.shard_map(
        shards_8x4 if fits else shards,
        mesh=mesh,
        in_specs=placed,
        out_specs=(
            P(None, "fsdp", "ctx", None),
            P(None, "fsdp", "ctx", None),
            P(("ctx", "fsdp")),
            P(("ctx", "fsdp")),
            P(("ctx", "fsdp"), None),
            P(("ctx", "fsdp"), None),
            P(("ctx", "fsdp")),
            P(("ctx", "fsdp"), None),
            P(("ctx", "fsdp"), None),
        ),
        check_vma=False,
    )
```

```python
import math

import jax
import jax.numpy as jnp
from jax import lax
from jax.experimental import pallas as pl
from jax.experimental.pallas import tpu as pltpu
from jax.sharding import PartitionSpec as P

HEADS = 16
HEAD_DIM = 64
BLOCK = 256


EPSILON = 1e-06
MASKED = -1e30
HIGHEST = lax.Precision.HIGHEST
BF16, F32 = jnp.bfloat16, jnp.float32
VMEM_LIMIT = 24 * 2**20
WEIGHT = 10**10


def rms_norm(values, gain):
    factor = lax.rsqrt(jnp.mean(values * values, axis=-1, keepdims=True) + EPSILON)
    return values * factor * gain


def exact_gelu(values):
    return jax.nn.gelu(values, approximate=False)


def fetch(w_qkv, w_out, w_up, w_down):
    return (
        lax.all_gather(w_qkv, "fsdp", axis=0, tiled=True),
        lax.all_gather(w_out, "fsdp", axis=0, tiled=True),
        lax.all_gather(w_up, "fsdp", axis=0, tiled=True),
        lax.all_gather(w_down, "fsdp", axis=0, tiled=True),
    )


def lookup(table, index):
    hits = index[..., None] == jnp.arange(table.shape[0], dtype=jnp.int32)
    return jnp.sum(jnp.where(hits, table, 0), axis=-1)


def outer_sum(left, right):
    return lax.dot_general(
        left, right, (((0,), (0,)), ((), ())), preferred_element_type=jnp.float32
    )


def gather_rows(pieces, column):
    return jnp.concatenate([piece[column] for piece in pieces], axis=0)


def shards(
    tokens, w_router, gain_attn, w_qkv, w_out, gain_mlp, w_up, w_down, routed, deal, cotangent
):
    micros, tok_dev, width = (tokens.shape[0], tokens.shape[2], tokens.shape[3])
    span = tok_dev // 2
    rank = lax.axis_index("ctx")
    storage = routed[:, 0, :]
    local_rows = storage - rank * tok_dev
    anchor = lookup(deal, storage // span) * span + storage % span
    own_blocks = anchor // BLOCK
    all_blocks = lax.all_gather(own_blocks, "ctx", axis=1, tiled=True)
    factor = HEAD_DIM ** (-0.5)
    outputs, in_grads, kept = ([], [], [])
    sum_router = jnp.zeros((width,), jnp.float32)
    sum_gain_attn = jnp.zeros((width,), jnp.float32)
    sum_gain_mlp = jnp.zeros((width,), jnp.float32)
    for micro in range(micros):
        full_qkv, full_out, full_up, full_down = fetch(w_qkv, w_out, w_up, w_down)
        resid = tokens[micro, 0].astype(jnp.float32)
        grad_in = cotangent[micro, 0].astype(jnp.float32)
        rows_index = local_rows[micro]
        rows = jnp.take(resid, rows_index, axis=0)
        count = rows.shape[0]
        gate = jax.nn.sigmoid(jnp.dot(rows, w_router, precision=HIGHEST))
        norm1, norm1_back = jax.vjp(rms_norm, rows, gain_attn)
        norm1_low = norm1.astype(jnp.bfloat16)
        qkv = jnp.dot(norm1_low, full_qkv, preferred_element_type=jnp.float32).astype(jnp.bfloat16)
        queries = qkv[:, :width]
        keys_local = qkv[:, width : 2 * width]
        values_local = qkv[:, 2 * width :]
        keys_all, values_all = (
            lax.all_gather(keys_local, "ctx", axis=0, tiled=True),
            lax.all_gather(values_local, "ctx", axis=0, tiled=True),
        )
        total = keys_all.shape[0]
        query_heads = queries.reshape(count, HEADS, HEAD_DIM)
        key_heads = keys_all.reshape(total, HEADS, HEAD_DIM)
        value_heads = values_all.reshape(total, HEADS, HEAD_DIM)
        visible = all_blocks[micro][None, :] <= own_blocks[micro][:, None]
        scores = (
            jnp.einsum("qhd,khd->hqk", query_heads, key_heads, preferred_element_type=jnp.float32)
            * factor
        )
        scores = jnp.where(visible[None], scores, MASKED)
        probs = jax.nn.softmax(scores, axis=-1)
        probs_low = probs.astype(jnp.bfloat16)
        attended = jnp.einsum(
            "hqk,khd->qhd", probs_low, value_heads, preferred_element_type=jnp.float32
        )
        attended_low = attended.reshape(count, width).astype(jnp.bfloat16)
        attn = jnp.dot(attended_low, full_out, preferred_element_type=jnp.float32)
        mid = rows + attn
        norm2, norm2_back = jax.vjp(rms_norm, mid, gain_mlp)
        norm2_low = norm2.astype(jnp.bfloat16)
        hidden = jnp.dot(norm2_low, full_up, preferred_element_type=jnp.float32)
        act, gelu_back = jax.vjp(exact_gelu, hidden)
        act_low = act.astype(jnp.bfloat16)
        mlp = jnp.dot(act_low, full_down, preferred_element_type=jnp.float32)
        branch = attn + mlp
        outputs.append(resid.at[rows_index].set(rows + gate[:, None] * branch).astype(jnp.bfloat16))
        cot_rows = jnp.take(grad_in, rows_index, axis=0)
        d_branch = gate[:, None] * cot_rows
        d_mlp = d_branch.astype(jnp.bfloat16)
        d_logit = jnp.sum(cot_rows * branch, axis=-1) * gate * (1.0 - gate)
        d_act = jnp.dot(d_mlp, full_down.T, preferred_element_type=jnp.float32)
        d_hidden = gelu_back(d_act)[0].astype(jnp.bfloat16)
        d_norm2 = jnp.dot(d_hidden, full_up.T, preferred_element_type=jnp.float32)
        d_mid, d_gain2 = norm2_back(d_norm2)
        d_attn = (d_branch + d_mid).astype(jnp.bfloat16)
        d_attended = jnp.dot(d_attn, full_out.T, preferred_element_type=jnp.float32).astype(
            jnp.bfloat16
        )
        d_heads = d_attended.reshape(count, HEADS, HEAD_DIM)
        d_probs = jnp.einsum(
            "qhd,khd->hqk", d_heads, value_heads, preferred_element_type=jnp.float32
        )
        weighted = jnp.sum(probs * d_probs, axis=-1, keepdims=True)
        d_scores = (probs * (d_probs - weighted)).astype(jnp.bfloat16)
        d_query = (
            jnp.einsum("hqk,khd->qhd", d_scores, key_heads, preferred_element_type=jnp.float32)
            * factor
        )
        d_key_part = (
            jnp.einsum("hqk,qhd->khd", d_scores, query_heads, preferred_element_type=jnp.float32)
            * factor
        )
        d_value_part = jnp.einsum(
            "hqk,qhd->khd", probs_low, d_heads, preferred_element_type=jnp.float32
        )
        d_keys, d_values = (
            lax.psum_scatter(
                d_key_part.reshape(total, width), "ctx", scatter_dimension=0, tiled=True
            ),
            lax.psum_scatter(
                d_value_part.reshape(total, width), "ctx", scatter_dimension=0, tiled=True
            ),
        )
        d_qkv = jnp.concatenate([d_query.reshape(count, width), d_keys, d_values], axis=1).astype(
            jnp.bfloat16
        )
        d_norm1 = jnp.dot(d_qkv, full_qkv.T, preferred_element_type=jnp.float32)
        d_rows_norm, d_gain1 = norm1_back(d_norm1)
        d_rows = cot_rows + d_mid + d_rows_norm + d_logit[:, None] * w_router
        in_grads.append(grad_in.at[rows_index].set(d_rows).astype(jnp.bfloat16))
        sum_router = sum_router + jnp.dot(d_logit, rows, precision=HIGHEST)
        sum_gain_attn = sum_gain_attn + d_gain1
        sum_gain_mlp = sum_gain_mlp + d_gain2
        kept.append((norm1_low, d_qkv, attended_low, d_attn, norm2_low, d_hidden, act_low, d_mlp))
    stacked_rows = tuple((gather_rows(kept, column) for column in range(8)))
    grad_qkv = outer_sum(stacked_rows[0], stacked_rows[1])
    grad_out = outer_sum(stacked_rows[2], stacked_rows[3])
    grad_up = outer_sum(stacked_rows[4], stacked_rows[5])
    grad_down = outer_sum(stacked_rows[6], stacked_rows[7])
    summed = (
        lax.psum_scatter(sum_router, ("ctx", "fsdp"), scatter_dimension=0, tiled=True),
        lax.psum_scatter(sum_gain_attn, ("ctx", "fsdp"), scatter_dimension=0, tiled=True),
        lax.psum_scatter(grad_qkv, ("ctx", "fsdp"), scatter_dimension=0, tiled=True),
        lax.psum_scatter(grad_out, ("ctx", "fsdp"), scatter_dimension=0, tiled=True),
        lax.psum_scatter(sum_gain_mlp, ("ctx", "fsdp"), scatter_dimension=0, tiled=True),
        lax.psum_scatter(grad_up, ("ctx", "fsdp"), scatter_dimension=0, tiled=True),
        lax.psum_scatter(grad_down, ("ctx", "fsdp"), scatter_dimension=0, tiled=True),
    )
    output = jnp.stack(outputs)[:, None]
    input_grad = jnp.stack(in_grads)[:, None]
    return (
        output,
        input_grad,
        summed[0],
        summed[1],
        summed[2],
        summed[3],
        summed[4],
        summed[5],
        summed[6],
    )


ORDER = (0, 2, 1, 3)


def sds(shape, dtype):
    return jax.ShapeDtypeStruct(shape, dtype)


def local(shape, dtype):
    return pltpu.VMEM(shape, dtype)


def near(x):
    return pltpu.with_memory_space_constraint(x, pltpu.VMEM)


class Chain:
    def __init__(self):
        self.last = None

    def __call__(self, kernel, outs, smem, args, scratch=(), name=None, far=(), after=(), weight=WEIGHT):
        count = len(smem) + len(far) + len(args)
        spec = pl.BlockSpec(memory_space=pltpu.VMEM)
        extra = () if self.last is None else (near(self.last),)
        extra = (*extra, *(near(a) for a in after))

        def body(*refs):
            kernel(*refs[:count], *refs[count + len(extra) :])

        results = pl.pallas_call(
            body,
            out_shape=tuple(outs),
            in_specs=[pl.BlockSpec(memory_space=pltpu.SMEM)] * len(smem)
            + [pl.BlockSpec(memory_space=pltpu.HBM)] * len(far)
            + [spec] * (len(args) + len(extra)),
            out_specs=tuple(spec for _ in outs),
            scratch_shapes=list(scratch),
            compiler_params=pltpu.CompilerParams(vmem_limit_bytes=VMEM_LIMIT),
            cost_estimate=pl.CostEstimate(flops=weight, bytes_accessed=weight // 10000, transcendentals=0),
            name=name,
        )(
            *smem, *(pltpu.with_memory_space_constraint(a, pltpu.HBM) for a in far), *(near(a) for a in args), *extra
        )
        if not isinstance(outs[0], jax.ShapeDtypeStruct):
            self.last = results[0]
        return results

    def hold(self, x, *after):
        (x,) = self(hold_kernel, (local(x.shape, x.dtype),), (), (x,), after=after, name="hold", weight=0)
        return x


def hold_kernel(x, out):
    out[...] = x[...]


def mm(left, right):
    return jnp.dot(left, right, preferred_element_type=F32)


def mm_t(left, right):
    return lax.dot_general(left, right, (((1,), (1,)), ((), ())), preferred_element_type=F32)


def t_mm(left, right):
    return lax.dot_general(left, right, (((0,), (0,)), ((), ())), preferred_element_type=F32)


def exchange(x, axis, size, mask):
    return lax.ppermute(x, axis, [(i, i ^ mask) for i in range(size)])


def rms_factor(values):
    return lax.rsqrt(jnp.mean(values * values, axis=-1, keepdims=True) + EPSILON)


def aligned(start, unit):
    return pl.multiple_of(start, unit)


def iota(shape, axis):
    return lax.broadcasted_iota(jnp.int32, shape, axis)


def picks(ids, routed, micro, tok_dev):
    index = routed[micro : micro + 1, :] - ids[0] * tok_dev
    shape = (tok_dev, routed.shape[1])
    return jnp.where(iota(shape, 0) == index, 1.0, 0.0)


def share_peers(ids, bit):
    return ids[1], ids[1] ^ 1, ids[1] ^ (2 + ((ids[0] >> bit) & 1))


def share_rows(c, f, bit):
    side = (c >> bit) & 1
    return f, f ^ 1, f ^ (2 + side), f ^ (3 - side)


def cut_qkv(ids, half, w_qkv, pieces, sem, first, by_y=True):
    width = w_qkv.shape[1] // 3
    copies = []
    peers = share_peers(ids, 0) if by_y else tuple(ids[1] ^ k for k in range(4))
    for k, (peer, piece) in enumerate(zip(peers, pieces)):
        for b in range(3):
            start = b * width + peer * (width // 4) + half * 128
            copies.append(
                pltpu.make_async_copy(
                    w_qkv.at[:, pl.ds(aligned(start, 128), 128)],
                    piece.at[:, pl.ds(b * 128, 128)],
                    sem.at[first + 3 * k + b],
                )
            )
    return copies


def front_kernel(ids, deal, tokens, w_qkv, routed, rowsx, p0, p1, p2, near_tokens, sem):
    micros, tok_dev, width = tokens.shape
    per = routed.shape[1]
    count = micros * per
    span = tok_dev // 2
    first = pltpu.make_async_copy(tokens, near_tokens, sem.at[0])
    first.start()
    copies = cut_qkv(ids, ids[0] >> 2, w_qkv, (p0, p1, p2), sem, 1)
    for copy in copies:
        copy.start()
    stored = routed[...]
    chunk = stored // span
    anchor = jnp.zeros_like(stored)
    for entry in range(deal.shape[0]):
        anchor = jnp.where(chunk == entry, deal[entry], anchor)
    place = ((anchor * span + stored % span) // BLOCK).astype(F32)
    rowsx[count:] = jnp.zeros((8, width), BF16)
    for micro in range(micros):
        rowsx[count + micro : count + micro + 1, :per] = place[micro : micro + 1].astype(BF16)
    first.wait()
    for micro in range(micros):
        pick = picks(ids, routed, micro, tok_dev).astype(BF16)
        rowsx[micro * per : (micro + 1) * per] = t_mm(pick, near_tokens[micro]).astype(BF16)
    for copy in copies:
        copy.wait()


def run(copies):
    for copy in copies:
        copy.start()
    for copy in copies:
        copy.wait()


def cut_up_kernel(ids, w_up, p0, p1, p2, sem):
    share = p0.shape[1]
    run(
        [
            pltpu.make_async_copy(
                w_up.at[:, pl.ds(aligned(peer * share, share), share)], piece, sem.at[k]
            )
            for k, (peer, piece) in enumerate(zip(share_peers(ids, 0), (p0, p1, p2)))
        ]
    )


def cut_rest_kernel(ids, w_qkv, v0, v1, v2, v3, sem):
    run(cut_qkv(ids, 1 - (ids[0] >> 2), w_qkv, (v0, v1, v2, v3), sem, 0, False))


def cot_kernel(ids, routed, cot, rowsx, both):
    micros, tok_dev = cot.shape[:2]
    per = routed.shape[1]
    start = rowsx.shape[0]
    both[:start] = rowsx[...]
    for micro in range(micros):
        pick = picks(ids, routed, micro, tok_dev).astype(BF16)
        both[start + micro * per : start + (micro + 1) * per] = t_mm(pick, cot[micro]).astype(BF16)


def rows_of(both):
    return both[: both.shape[0] // 2 - 4].astype(F32)


def cots_of(both):
    return both[both.shape[0] // 2 + 4 :].astype(F32)


def d_mlp_kernel(b0, b1, b2, b3, w_router, d_mlp, gate_out):
    count = gate_out.shape[1]
    for i, both in enumerate((b0, b1, b2, b3)):
        gate = jax.nn.sigmoid(jnp.sum(rows_of(both) * w_router[...], axis=1, keepdims=True))
        d_mlp[i * count : (i + 1) * count] = (gate * cots_of(both)).astype(BF16)
        gate_out[i] = gate


def head_masks():
    lanes = iota((1, 128), 1)
    low = jnp.where(lanes < 64, 1.0, 0.0)
    return low, 1.0 - low


def attend_kernel(
    ids, near_rows, far_rows, gain, w0, w1, w2, w3,
    far, own, stack, probs, norm1, place_col, result,
):
    c, f = ids[0], ids[1]
    micros, total = stack.shape[0], stack.shape[1]
    count = own.shape[1]
    per = count // micros
    eye = iota((per, 128), 0) == iota((per, 128), 1)
    step = count + 8
    for h, source in enumerate((near_rows, far_rows)):
        for b in range(4):
            rows = source[b * step : b * step + count].astype(F32)
            index = ((c >> 2) ^ h) * 4 + b
            norm1[pl.ds(aligned(index * count, 16), count)] = (
                rows * rms_factor(rows) * gain[...]
            ).astype(BF16)
            places = source[b * step + count : b * step + count + 8, :128].astype(F32)
            for m in range(micros):
                col = jnp.sum(jnp.where(eye, places[m : m + 1], 0.0), axis=1, keepdims=True)
                place_col[m, pl.ds(aligned(index * per, per), per), :] = jnp.broadcast_to(
                    col, (per, 128)
                )
    qkv = jnp.zeros((8 * count, 384), F32)
    for peer, w in zip(share_rows(c, f, 0), (w0, w1, w2, w3)):
        part = w.shape[0]
        qkv = qkv + mm(norm1[:, pl.ds(aligned(peer * part, part), part)], w[...])
    low = qkv.astype(BF16)
    for t in range(8):
        for m in range(micros):
            stack[m, t * per : (t + 1) * per, :] = low[
                t * count + m * per : t * count + (m + 1) * per
            ]
    big_eye = iota((total, total), 0) == iota((total, total), 1)
    masks = head_masks()
    for m in range(micros):
        q, k, v = stack[m, :, :128], stack[m, :, 128:256], stack[m, :, 256:384]
        mine = place_col[m, :, 0:1]
        theirs = jnp.sum(jnp.where(big_eye, mine, 0.0), axis=0, keepdims=True)
        visible = theirs <= mine
        attended = jnp.zeros((total, 128), F32)
        for h in range(2):
            scores = mm_t(q * masks[h].astype(BF16), k) * (HEAD_DIM**-0.5)
            scores = jnp.where(visible, scores, MASKED)
            top = jnp.max(scores, axis=1, keepdims=True)
            grown = jnp.exp(scores - top)
            weight = grown / jnp.sum(grown, axis=1, keepdims=True)
            probs[2 * m + h] = weight
            attended = attended + mm(weight.astype(BF16), v) * masks[h]
        result[m] = attended.astype(BF16)
        for k in range(8):
            out = far if k >= 4 else own
            out[k & 3, m * per : (m + 1) * per, :] = result[
                m, pl.ds(aligned((c ^ k) * per, per), per), :
            ]


def row_slot(f, s, count):
    k = s ^ f
    return aligned(((k & 1) * 2 + (k >> 1)) * count, 16)


def split_rows(full, send, keep):
    count = send.shape[1]
    for i in range(2):
        keep[i] = full[i * count : (i + 1) * count]
        send[i] = full[(2 + i) * count : (3 + i) * count].astype(BF16)


def block_place(ids, k, count, lanes):
    peer = ids[0] ^ k
    columns = aligned((peer >> 2) * lanes, 128)
    return pl.ds(row_slot(ids[1], peer & 3, count), count), pl.ds(columns, lanes)


def out_kernel(ids, b0, b1, b2, b3, w_out, attended, send, keep, full):
    count = b0.shape[1]
    for k, block in enumerate((b0, b1, b2, b3)):
        for far in range(2):
            attended[block_place(ids, k ^ (4 * far), count, 128)] = block[far]
    full[...] = mm(attended[...], w_out[...])
    split_rows(full, send, keep)


def add_both_kernel(keep, received, total):
    total[...] = (keep[...] + received[...].astype(F32)).astype(BF16)


def add_own_kernel(keep, received, send2, keep2):
    send2[...] = (keep[1] + received[1].astype(F32)).astype(BF16)
    keep2[...] = keep[0] + received[0].astype(F32)


def mid_kernel(low, received, both0, both1, gain, attn, norm2):
    for i, both in enumerate((both0, both1)):
        value = low[i].astype(F32) + received[1 - i].astype(F32)
        attn[i] = value
        mid = rows_of(both) + value
        norm2[i] = (mid * rms_factor(mid) * gain[...]).astype(BF16)


def mlp_kernel(
    ids, n0, n1, d_mlp, u0, u1, u2, u3, w_down,
    send, keep, act_send, d_send, act_keep, d_keep, norm2, act, d_hidden, back,
):
    c = ids[0]
    part = u0.shape[0]
    count = n0.shape[1]
    shares = tuple(zip(share_rows(ids[0], ids[1], 0), (u0, u1, u2, u3)))
    for i in range(2):
        norm2[i * count : (i + 1) * count] = n0[i]
        norm2[(2 + i) * count : (3 + i) * count] = n1[i]
    hidden = jnp.zeros(act.shape, F32)
    for peer, u in shares:
        hidden = hidden + mm(norm2[:, pl.ds(aligned(peer * part, part), part)], u[...])
    d_act = mm_t(d_mlp[...], w_down[...])
    phi = 0.5 * (1.0 + lax.erf(hidden * (0.5**0.5)))
    act[...] = (hidden * phi).astype(BF16)
    slope = phi + hidden * jnp.exp(-0.5 * hidden * hidden) * ((2.0 * math.pi) ** -0.5)
    d_hidden[...] = (d_act * slope).astype(BF16)
    for i, (some_act, some_d) in enumerate(((act_keep, d_keep), (act_send, d_send))):
        for high in range(2):
            start = aligned(high * 512 + (((c >> 1) & 1) ^ i) * 256, 128)
            some_act[:, high * 256 : (high + 1) * 256] = act[:, pl.ds(start, 256)]
        some_d[...] = d_hidden[:, pl.ds(aligned(((c & 1) ^ i) * 512, 128), 512)]
    for peer, u in shares:
        back[:, pl.ds(aligned(peer * part, part), part)] = mm_t(d_hidden[...], u[...])
    split_rows(back, send, keep)


def mlp_out_kernel(act, w_down, attn, gate, b0, b1, b2, b3, send, keep, router, full):
    full[...] = mm(act[...], w_down[...])
    split_rows(full, send, keep)
    count = gate.shape[1]
    total = jnp.zeros(router.shape, F32)
    for i, both in enumerate((b0, b1, b2, b3)):
        own = slice(i * count, (i + 1) * count)
        part = jnp.sum(cots_of(both) * (attn[own] + full[own]), axis=1, keepdims=True)
        part = part * gate[i] * (1.0 - gate[i])
        total = total + jnp.sum(rows_of(both) * part, axis=0, keepdims=True)
    router[...] = total


def pick_rows(c, peer, share, out, lanes):
    @pl.when(peer == (c >> 1))
    def _():
        out[:, lanes] = share[pl.ds(aligned((c & 1) * 128, 128), 128), :]


def pick_kernel(ids, *refs):
    shares, (up_rows, qkv_rows) = refs[:12], refs[12:]
    c, f = ids[0], ids[1]
    for peer, u in zip(share_rows(c, f, 0), shares[:4]):
        pick_rows(c, peer, u, up_rows, slice(None))
    for peer, a in zip(share_rows(c, f, 0), shares[4:8]):
        pick_rows(c, peer, a, qkv_rows, slice(0, 384))
    for k, b in enumerate(shares[8:]):
        pick_rows(c, f ^ k, b, qkv_rows, slice(384, 768))


def chunk(f, q):
    return pl.ds(aligned((f ^ q) * 32, 32), 32)


def grad_up_kernel(ids, norm2, near_a, near_b, d_own, d_near, send, keep, rows, columns):
    count = norm2.shape[0]
    half = count // 2
    rows[:count] = norm2[...]
    for i in range(2):
        rows[count + i * (half // 2) : count + (i + 1) * (half // 2)] = near_a[i]
        rows[count + half + i * (half // 2) : count + half + (i + 1) * (half // 2)] = near_b[i]
    columns[:count] = d_own[...]
    columns[count:] = d_near[...]
    for place, (target, index) in enumerate(((keep, 0), (send, 0), (keep, 1), (send, 1))):
        kk = (0, 1, 2, 3)[place]
        start = aligned(((ids[0] >> 1) ^ kk) * 256, 128)
        value = t_mm(rows[:, pl.ds(start, 256)], columns[...])
        for owner in range(2):
            for q in range(4):
                at = pl.ds(aligned(((ids[0] & 1) ^ owner) * 128 + (ids[1] ^ q) * 32, 32), 32)
                piece = value[owner * 128 + q * 32 : owner * 128 + (q + 1) * 32]
                target[index, at] = piece.astype(target.dtype)


def grad_down_kernel(ids, d_mlp, near_a, near_b, a_own, a_near, send, keep, rows, columns):
    count = d_mlp.shape[0]
    half = count // 2
    rows[:count] = d_mlp[...]
    rows[count : count + half] = near_a[...]
    rows[count + half :] = near_b[...]
    columns[:count] = a_own[...]
    columns[count:] = a_near[...]
    c = ids[0]
    for target, index, k in ((keep, 0, 0), (send, 0, 1), (keep, 1, 4), (send, 1, 5)):
        start = aligned(((c >> 2) ^ (k >> 2)) * 256 + ((c & 1) ^ (k & 1)) * 128, 128)
        value = t_mm(columns[:, pl.ds(start, 128)], rows[...])
        target[index] = value.astype(target.dtype)


def grad_attn_kernel(
    ids, norm1, b0, b1, b2, b3, b4, b5, b6, b7, attended, d_attn, router,
    keep, send1, send2, send3, joined, full,
):
    count = b0.shape[0]
    for k, block in enumerate((b0, b1, b2, b3, b4, b5, b6, b7)):
        joined[pl.ds(aligned((ids[0] ^ k) * count, 16), count)] = block[...]
    full[...] = t_mm(attended[...], d_attn[...])
    for k in range(8):
        target, index = (keep, send1, send2, send3)[k & 3], k >> 2
        owner = ids[0] ^ k
        start = aligned(owner * 128, 128)
        value = t_mm(norm1[:, pl.ds(start, 128)], joined[...])
        for q in range(4):
            piece = value[q * 32 : (q + 1) * 32]
            target[index, chunk(ids[1], q), :384] = piece.astype(target.dtype)
            rows = full[pl.ds(aligned(owner * 32, 32), 32), q * 256 : (q + 1) * 256]
            target[index, q * 32 : (q + 1) * 32, 384:640] = rows.astype(target.dtype)
        target[index, 128:136, :] = jnp.zeros((8, 640), target.dtype)
        share = jnp.broadcast_to(router[:, pl.ds(start, 128)], (8, 128))
        target[index, 128:136, 384:512] = share.astype(target.dtype)


def sum_attn_kernel(keep, got1, got2, got3, send, mine):
    for index, target in ((0, mine), (1, send)):
        total = (keep[index] + got1[index].astype(F32)) + (
            got2[index].astype(F32) + got3[index].astype(F32)
        )
        target[0] = total.astype(target.dtype)


def d_attn_kernel(low, received, attn, both0, both1, gate, gain, d_mid_out, d_attn):
    for i, both in enumerate((both0, both1)):
        mid = rows_of(both) + attn[i]
        r2 = rms_factor(mid)
        d_norm2 = low[i].astype(F32) + received[1 - i].astype(F32)
        t2 = d_norm2 * gain[...]
        d_mid = r2 * t2 - mid * (r2 * r2 * r2) * jnp.mean(t2 * mid, axis=1, keepdims=True)
        d_attn[i] = (gate[i] * cots_of(both) + d_mid).astype(BF16)
        if i == 0:
            d_mid_out[...] = d_mid


def d_attended_kernel(ids, d0, d1, w_out, far, own, d_attn, d_att):
    count = d0.shape[1]
    for i in range(2):
        d_attn[i * count : (i + 1) * count] = d0[i]
        d_attn[(2 + i) * count : (3 + i) * count] = d1[i]
    d_att[...] = mm_t(d_attn[...], w_out[...])
    for k in range(8):
        block = far if k >= 4 else own
        block[k & 3] = d_att[block_place(ids, k, count, 128)].astype(BF16)


def attend_back_kernel(ids, *refs):
    blocks, (stack, probs), outs, (d_stack, result) = refs[:4], refs[4:6], refs[6:14], refs[14:]
    micros, total = stack.shape[0], stack.shape[1]
    count = outs[0].shape[0]
    per = count // micros
    masks = head_masks()
    for m in range(micros):
        rows = slice(m * per, (m + 1) * per)
        for k in range(8):
            d_stack[pl.ds(aligned((ids[0] ^ k) * per, per), per), :] = blocks[k & 3][k >> 2, rows]
        q, k, v = stack[m, :, :128], stack[m, :, 128:256], stack[m, :, 256:384]
        d_out = d_stack[...]
        d_q = jnp.zeros((total, 128), F32)
        d_k = jnp.zeros((total, 128), F32)
        d_v = jnp.zeros((total, 128), F32)
        for h in range(2):
            weight = probs[2 * m + h]
            d_probs = mm_t(d_out * masks[h].astype(BF16), v)
            inner = jnp.sum(weight * d_probs, axis=1, keepdims=True)
            d_scores = (weight * (d_probs - inner)).astype(BF16)
            d_q = d_q + mm(d_scores, k) * masks[h]
            d_k = d_k + t_mm(d_scores, q) * masks[h]
            d_v = d_v + t_mm(weight.astype(BF16), d_out) * masks[h]
        result[m, :, :128] = (d_q * (HEAD_DIM**-0.5)).astype(BF16)
        result[m, :, 128:256] = (d_k * (HEAD_DIM**-0.5)).astype(BF16)
        result[m, :, 256:384] = d_v.astype(BF16)
        for k in range(8):
            outs[k][rows] = result[m, pl.ds(aligned((ids[0] ^ k) * per, per), per), :]


def d_norm1_kernel(
    ids, d0, d1, d2, d3, d4, d5, d6, d7, a0, a1, a2, a3, b0, b1, b2, b3,
    send, keep, d_qkv, full,
):
    c, f = ids[0], ids[1]
    count = d0.shape[0]
    part = a0.shape[0]
    for k, block in enumerate((d0, d1, d2, d3, d4, d5, d6, d7)):
        rows = pl.ds(row_slot(f, (c ^ k) & 3, count), count)
        d_qkv[rows, (k >> 2) * 384 : (k >> 2) * 384 + 384] = block[...]
    for peer, a in zip(share_rows(c, f, 0), (a0, a1, a2, a3)):
        full[:, pl.ds(aligned(peer * part, part), part)] = mm_t(d_qkv[:, :384], a[...])
    for k, b in enumerate((b0, b1, b2, b3)):
        columns = pl.ds(aligned((f ^ k) * part, part), part)
        full[:, columns] = full[:, columns] + mm_t(d_qkv[:, 384:], b[...])
    split_rows(full, send, keep)


def place_rows(ids, routed, micro, source, rows, out):
    tok_dev = source.shape[0]
    pick = picks(ids, routed, micro, tok_dev)
    changed = jnp.sum(pick, axis=1, keepdims=True) > 0.5
    placed = mm(pick.astype(BF16), rows)
    out[...] = jnp.where(changed, placed, source[...].astype(F32)).astype(BF16)


def output_kernel(
    ids, routed, keep, received, attn, both, gate, tokens, d_logit_out, output,
):
    count = keep.shape[0]
    micros = tokens.shape[0]
    per = count // micros
    branch = attn[0] + keep[...] + received[...].astype(F32)
    rows = rows_of(both)
    open_gate = gate[0]
    d_logit = (
        jnp.sum(cots_of(both) * branch, axis=1, keepdims=True)
        * open_gate
        * (1.0 - open_gate)
    )
    d_logit_out[...] = d_logit
    result = (rows + open_gate * branch).astype(BF16)
    for micro in range(micros):
        own = result[micro * per : (micro + 1) * per]
        place_rows(ids, routed, micro, tokens.at[micro], own, output.at[micro])


def input_grad_kernel(
    ids, routed, keep, received, d_mid, both, d_logit, w_router, gain, cot, input_grad,
):
    count = keep.shape[0]
    micros = cot.shape[0]
    per = count // micros
    rows = rows_of(both)
    r1 = rms_factor(rows)
    t1 = (keep[...] + received[...].astype(F32)) * gain[...]
    d_rows = (
        cots_of(both)
        + d_mid[...]
        + r1 * t1
        - rows * (r1 * r1 * r1) * jnp.mean(t1 * rows, axis=1, keepdims=True)
        + d_logit[...] * w_router[...]
    ).astype(BF16)
    for micro in range(micros):
        own = d_rows[micro * per : (micro + 1) * per]
        place_rows(ids, routed, micro, cot.at[micro], own, input_grad.at[micro])


def as_row(column):
    count = column.shape[0]
    eye = iota((count, count), 0) == iota((count, count), 1)
    return jnp.sum(jnp.where(eye, column, 0.0), axis=0, keepdims=True)


def owned(ids, vector, count):
    start = (4 * ids[0] + ids[1]) * count
    shape = (count, vector.shape[1])
    hit = iota(shape, 1) == iota(shape, 0) + start
    return jnp.sum(jnp.where(hit, vector[...], 0.0), axis=1, keepdims=True)


def join_up_kernel(ids, p0, p1, p2, p3, gain, out, grad_gain):
    rows, part = out.shape[0], out.shape[1] // 4
    total = jnp.zeros((rows, 1), F32)
    for k, piece in enumerate((p0, p1, p2, p3)):
        out[:, pl.ds(aligned((ids[1] ^ k) * part, part), part)] = piece[:, :part].astype(F32)
        total = total + piece[:, part : part + 128].astype(F32)[:, :1]
    grad_gain[...] = as_row(total / owned(ids, gain, rows))


def join_qkv_kernel(ids, p0, p1, p2, p3, gain, out, grad_gain, grad_router):
    rows, width = out.shape[0], out.shape[1] // 3
    part = width // 4
    total = jnp.zeros((rows, 1), F32)
    router = jnp.zeros((rows, 1), F32)
    for k, piece in enumerate((p0, p1, p2, p3)):
        for half in range(2):
            for b in range(3):
                start = b * width + (ids[1] ^ k) * part + ((ids[0] >> 2) ^ half) * 128
                out[:, pl.ds(aligned(start, 128), 128)] = piece[
                    :, (3 * half + b) * 128 : (3 * half + b + 1) * 128
                ].astype(F32)
        total = total + piece[:, 768:896].astype(F32)[:, :1]
        router = router + piece[:, 896:1024].astype(F32)[:, :1]
    grad_gain[...] = as_row(total / owned(ids, gain, rows))
    grad_router[...] = as_row(router)


def join_down_kernel(block, token, out):
    token[...] = jnp.zeros(token.shape, F32)
    out[...] = block[...].astype(F32)


def hop2_kernel(keep_u, got_u, keep_d, got_d, send, own_u, own_d):
    for i in range(2):
        total = keep_u[i] + got_u[i].astype(F32)
        half, width = total.shape[0] // 2, total.shape[1]
        if i:
            send[0, :, :width] = total[:half].astype(BF16)
            send[0, :, width:] = total[half:].astype(BF16)
        else:
            own_u[...] = total
    own_d[...] = keep_d[0] + got_d[0].astype(F32)
    send[1] = (keep_d[1] + got_d[1].astype(F32)).astype(BF16)


def hop3_kernel(own_u, own_d, got, send, mine, down):
    half, width = own_u.shape[0] // 2, own_u.shape[1]
    mine[...] = own_u[:half] + got[0, :, :width].astype(F32)
    send[...] = (own_u[half:] + got[0, :, width:].astype(F32)).astype(BF16)
    down[...] = (own_d[...] + got[1].astype(F32)).astype(BF16)


def up_pieces_kernel(ids, mine, other, w_rows, c0, c1, c2, c3):
    rows, half = c0.shape[0], mine.shape[1]
    y = ids[0] & 1
    for k, piece in enumerate((c0, c1, c2, c3)):
        own = slice(k * rows, (k + 1) * rows)
        weights = pl.ds(aligned((ids[1] ^ k) * rows, rows), rows)
        total = jnp.zeros((rows, 1), F32)
        for side, value in ((y, mine[own]), (1 - y, other[own].astype(F32))):
            columns = pl.ds(aligned(side * half, 128), half)
            piece[:, columns] = value.astype(BF16)
            total = total + jnp.sum(
                value * w_rows[weights, columns].astype(F32), axis=1, keepdims=True
            )
        piece[:, 2 * half :] = jnp.broadcast_to(total, (rows, 128)).astype(BF16)


def pieces_kernel(ids, mine, got, w_rows, c0, c1, c2, c3, out):
    rows = c0.shape[0]
    router = mine[0, 128:129, 384:512] + got[0, 128:136, 384:512].astype(F32)[0:1]
    for k, piece in enumerate((c0, c1, c2, c3)):
        own = slice(k * rows, (k + 1) * rows)
        first = (ids[1] ^ k) * rows
        weights = pl.ds(aligned(first, rows), rows)
        a, b = mine[0, own, :384], got[0, own, :384].astype(F32)
        piece[:, :384] = a.astype(BF16)
        piece[:, 384:768] = b.astype(BF16)
        total = jnp.sum(a * w_rows[weights, :384].astype(F32), axis=1, keepdims=True)
        total = total + jnp.sum(b * w_rows[weights, 384:].astype(F32), axis=1, keepdims=True)
        piece[:, 768:896] = jnp.broadcast_to(total, (rows, 128)).astype(BF16)
        hit = iota((rows, 128), 1) == iota((rows, 128), 0) + first
        share = jnp.sum(jnp.where(hit, router, 0.0), axis=1, keepdims=True)
        piece[:, 896:] = jnp.broadcast_to(share, (rows, 128)).astype(BF16)
        out[:, k * 256 : (k + 1) * 256] = mine[0, own, 384:640] + got[0, own, 384:640].astype(F32)


def all_rows_sum(call, send, keep, after=()):
    received = exchange(send, "fsdp", 4, 1)
    (low,) = call(
        add_both_kernel, (local(keep.shape, BF16),), (), (keep, received), name="add_both", after=after
    )
    return low, exchange(low, "fsdp", 4, 2)


def own_rows_sum(call, send, keep):
    received = exchange(send, "fsdp", 4, 1)
    shape = keep.shape[1:]
    send2, keep2 = call(
        add_own_kernel, (local(shape, BF16), local(shape, F32)), (), (keep, received), name="add_own"
    )
    return keep2, exchange(send2, "fsdp", 4, 2)


def swap_blocks(blocks):
    got = {k: exchange(blocks[k], "ctx", 8, k) for k in (7, 6, 5, 4, 3, 2, 1)}
    return (blocks[0], *(got[k] for k in range(1, 8)))


def swap_across(across, bit):
    return lax.ppermute(
        across, ("ctx", "fsdp"),
        [(4 * a + b, 4 * a + (b ^ (2 + ((a >> bit) & 1)))) for a in range(8) for b in range(4)],
    )


def pair_kernel(own, far, *outs):
    for k, out in enumerate(outs):
        out[0] = own[k]
        out[1] = far[k]


def swap_in_two(call, own, far, *after):
    came = exchange(far, "ctx", 8, 4)
    shape = (2, *own.shape[1:])
    pairs = call(pair_kernel, (local(shape, own.dtype),) * 4, (), (own, came), name="pair", after=after)
    return (pairs[0], *(exchange(pairs[k], "ctx", 8, k) for k in (1, 2, 3)))


def swap_pieces(pieces):
    return (pieces[0], *(exchange(pieces[k], "fsdp", 4, k) for k in (1, 2, 3)))


def shards_8x4(
    tokens, w_router, gain_attn, w_qkv, w_out, gain_mlp, w_up, w_down, routed, deal, cotangent
):
    micros, tok_dev, width = tokens.shape[0], tokens.shape[2], tokens.shape[3]
    per = routed.shape[2]
    count = micros * per
    total = 8 * per
    part = width // 4
    hidden = w_down.shape[0]
    c, f = lax.axis_index("ctx"), lax.axis_index("fsdp")
    ids = jnp.stack([c, f]).astype(jnp.int32)
    tok, cot, routed = tokens[:, 0], cotangent[:, 0], routed[:, 0]
    w_router, gain_attn, gain_mlp = (
        w_router.reshape(1, width), gain_attn.reshape(1, width), gain_mlp.reshape(1, width),
    )
    rows_bf, rows_f = local((count, width), BF16), local((count, width), F32)
    pair_bf, pair_f = local((2, count, width), BF16), local((2, count, width), F32)
    all_bf, all_quarter = local((4 * count, width), BF16), local((4 * count, part), BF16)
    hidden_bf = local((4 * count, hidden), BF16)
    vector = local((1, width), F32)
    dma = pltpu.SemaphoreType.DMA
    call = Chain()

    rowsx, *w_parts = call(
        front_kernel,
        (local((count + 8, width), BF16), *(local((part, 384), BF16),) * 3),
        (ids, deal), (routed,), far=(tok, w_qkv),
        scratch=[pltpu.VMEM(tok.shape, BF16), dma((10,))], name="front",
    )
    turn = [(4 * a + b, 4 * ((a & 4) | b) + (a & 3)) for a in range(8) for b in range(4)]
    turned = lax.ppermute(rowsx, ("ctx", "fsdp"), turn)
    turned_far = exchange(turned, "ctx", 8, 4)
    w_mine, w_beside, w_across = w_parts
    w_across = swap_across(w_across, 0)
    up_mine, up_beside, up_across = call(
        cut_up_kernel, (local((part, hidden), BF16),) * 3, (ids,), (), far=(w_up,),
        scratch=[dma((3,))], name="cut_up", weight=0,
    )
    near_rows = lax.all_gather(turned, "fsdp", axis=0, tiled=True)
    far_rows = lax.all_gather(turned_far, "fsdp", axis=0, tiled=True)
    w_across = call.hold(w_across, near_rows)
    up_across = call.hold(up_across, far_rows)
    w_parts = (w_mine, exchange(w_beside, "fsdp", 4, 1), w_across, exchange(w_across, "ctx", 8, 1))
    up_beside, up_across = exchange(up_beside, "fsdp", 4, 1), swap_across(up_across, 0)
    far_heads, heads, stack, probs, norm1 = call(
        attend_kernel,
        (
            *(local((4, count, 128), BF16),) * 2, local((micros, total, 384), BF16),
            local((2 * micros, total, total), F32), local((8 * count, width), BF16),
        ),
        (ids,), (near_rows, far_rows, gain_attn, *w_parts),
        scratch=[pltpu.VMEM((micros, total, 128), F32), pltpu.VMEM((micros, total, 128), BF16)],
        name="attend",
    )
    (both,) = call(
        cot_kernel, (local((2 * count + 8, width), BF16),), (ids,), (routed, cot, rowsx), name="cot_rows",
        weight=0,
    )
    both_x, both_c = exchange(both, "fsdp", 4, 2), exchange(both, "fsdp", 4, 1)
    both_xc = exchange(both_x, "fsdp", 4, 1)
    rest = call(
        cut_rest_kernel, (local((part, 384), BF16),) * 4, (ids,), (), far=(w_qkv,),
        scratch=[dma((12,))], name="cut_rest", weight=0,
    )
    heads = swap_in_two(call, heads, far_heads, up_across)
    attended, send, keep, attn_part = call(
        out_kernel, (all_quarter, pair_bf, pair_f, local((4 * count, width), F32)),
        (ids,), (*heads, w_out), name="attn_out", after=(up_across, both_x),
    )
    up_parts = (up_mine, up_beside, up_across, exchange(up_across, "ctx", 8, 1))
    rest = swap_pieces(rest)
    low, received = all_rows_sum(call, send, keep)
    d_mlp, gate = call(
        d_mlp_kernel, (all_bf, local((4, count, 1), F32)), (),
        (both, both_x, both_c, both_xc, w_router), name="d_mlp", weight=0,
    )
    d_mlp_a = exchange(d_mlp[: 2 * count], "ctx", 8, 2)
    d_mlp_b = exchange(d_mlp_a, "fsdp", 4, 1)
    attn, norm2 = call(
        mid_kernel, (pair_f, pair_bf), (), (low, received, both, both_x, gain_mlp), name="mid",
    )
    norm2_a = exchange(norm2, "ctx", 8, 1)
    norm2_b = exchange(norm2_a, "fsdp", 4, 1)
    half_bf = local((4 * count, hidden // 2), BF16)
    send, keep, act_send, d_send, act_keep, d_keep, norm2, act = call(
        mlp_kernel, (pair_bf, pair_f, half_bf, half_bf, half_bf, half_bf, all_bf, hidden_bf), (ids,),
        (norm2, exchange(norm2, "fsdp", 4, 1), d_mlp, *up_parts, w_down),
        scratch=[pltpu.VMEM((4 * count, hidden), BF16), pltpu.VMEM((4 * count, width), F32)],
        name="mlp",
    )
    d_near, act_near = exchange(d_send, "ctx", 8, 1), exchange(act_send, "ctx", 8, 2)
    low, received = all_rows_sum(call, send, keep, (norm2_a, d_mlp_a))
    d_mid, d_attn = call(
        d_attn_kernel, (rows_f, pair_bf), (),
        (low, received, attn, both, both_x, gate, gain_mlp), name="d_attn",
        after=(d_near, act_near),
    )
    far_heads, d_heads, d_attn = call(
        d_attended_kernel, (*(local((4, count, 128), BF16),) * 2, all_bf), (ids,),
        (d_attn, exchange(d_attn, "fsdp", 4, 1), w_out),
        scratch=[pltpu.VMEM((4 * count, part), F32)], name="d_attended",
    )
    send_u, keep_u = call(
        grad_up_kernel, (local((2, 256, hidden // 2), BF16), local((2, 256, hidden // 2), F32)), (ids,),
        (norm2, norm2_a, norm2_b, d_keep, d_near), name="grad_up", weight=0,
        scratch=[pltpu.VMEM((8 * count, width), BF16), pltpu.VMEM((8 * count, hidden // 2), BF16)],
    )
    send_d, keep_d = call(
        grad_down_kernel, (local((2, 128, width), BF16), local((2, 128, width), F32)), (ids,),
        (d_mlp, d_mlp_a, d_mlp_b, act_keep, act_near), name="grad_down", weight=0,
        scratch=[pltpu.VMEM((8 * count, width), BF16), pltpu.VMEM((8 * count, hidden // 2), BF16)],
    )
    got_u, got_d = exchange(send_u, "ctx", 8, 2), exchange(send_d, "ctx", 8, 1)
    d_heads = swap_in_two(call, d_heads, far_heads)
    d_blocks = call(
        attend_back_kernel, (local((count, 384), BF16),) * 8, (ids,), (*d_heads, stack, probs),
        scratch=[pltpu.VMEM((total, 128), BF16), pltpu.VMEM((micros, total, 384), BF16)],
        name="attend_back", after=(*rest[1:], got_u, got_d),
    )
    d_own = swap_blocks(d_blocks)
    send_z, own_u, own_d = call(
        hop2_kernel,
        (local((2, 128, width), BF16), local((256, hidden // 2), F32), local((128, width), F32)),
        (), (keep_u, got_u, keep_d, got_d), name="hop2", weight=0,
    )
    got_z = exchange(send_z, "ctx", 8, 4)
    owners = [(4 * a + b, 4 * (2 * b + a // 4) + a % 4) for a in range(8) for b in range(4)]
    send_m, keep_m, router = call(
        mlp_out_kernel, (pair_bf, pair_f, vector), (),
        (act, w_down, attn_part, gate, both, both_x, both_c, both_xc), name="mlp_out", weight=0,
        scratch=[pltpu.VMEM((4 * count, width), F32)],
    )
    part_bf = local((2, 136, 640), BF16)
    keep_q, *send_q = call(
        grad_attn_kernel, (local((2, 136, 640), F32), part_bf, part_bf, part_bf), (ids,),
        (norm1, *d_blocks, attended, d_attn, router), name="grad_attn", weight=0,
        scratch=[pltpu.VMEM((8 * count, 384), BF16), pltpu.VMEM((part, width), F32)],
    )
    got_q = [exchange(x, "ctx", 8, k + 1) for k, x in enumerate(send_q)]
    send, keep = call(
        d_norm1_kernel, (pair_bf, pair_f), (ids,),
        (*d_own, *w_parts, *rest), name="d_norm1",
        scratch=[pltpu.VMEM((4 * count, 768), BF16), pltpu.VMEM((4 * count, width), F32)],
    )
    keep, received = own_rows_sum(call, send, keep)
    keep_m, received_m = own_rows_sum(call, send_m, keep_m)
    send_u, mine_u, down = call(
        hop3_kernel,
        (local((128, hidden // 2), BF16), local((128, hidden // 2), F32), local((128, width), BF16)),
        (), (own_u, own_d, got_z), name="hop3", weight=0,
    )
    down = lax.ppermute(down, ("ctx", "fsdp"), owners)
    other_u = exchange(send_u, "ctx", 8, 1)
    send_q, keep_q = call(
        sum_attn_kernel, (local((1, 136, 640), BF16), local((1, 136, 640), F32)), (),
        (keep_q, *got_q), name="sum_attn", weight=0,
    )
    got_q = exchange(send_q, "ctx", 8, 4)
    d_logit, output = call(
        output_kernel, (local((count, 1), F32), sds(tok.shape, BF16)), (ids,),
        (routed, keep_m, received_m, attn, both, gate, tok), name="output", weight=0,
    )
    (input_grad,) = call(
        input_grad_kernel, (sds(cot.shape, BF16),), (ids,),
        (routed, keep, received, d_mid, both, d_logit, w_router, gain_attn, cot), name="input_grad",
        weight=0,
    )
    w_up_rows, w_qkv_rows = call(
        pick_kernel, (local((128, hidden), BF16), local((128, 768), BF16)), (ids,),
        (*up_parts, *w_parts, *rest), name="pick", weight=0,
    )
    chunks = call(
        up_pieces_kernel, (local((32, hidden + 128), BF16),) * 4, (ids,), (mine_u, other_u, w_up_rows),
        name="up_pieces",
    )
    chunks = swap_pieces(chunks)
    *qkv_chunks, grad_out = call(
        pieces_kernel, (local((32, 1024), BF16),) * 4 + (local((32, width), F32),), (ids,),
        (keep_q, got_q, w_qkv_rows), name="qkv_pieces",
    )
    qkv_chunks = swap_pieces(qkv_chunks)
    grad_out = lax.ppermute(grad_out, ("ctx", "fsdp"), owners)
    row = sds((1, 32), F32)
    _, grad_down = call(
        join_down_kernel, (local((8, 128), F32), sds((128, width), F32)), (), (down,), name="join_down"
    )
    grad_up, grad_gain_mlp = call(
        join_up_kernel, (sds((32, 4 * hidden), F32), row), (ids,), (*chunks, gain_mlp), name="join_up"
    )
    grad_qkv, grad_gain_attn, grad_router = call(
        join_qkv_kernel, (sds((32, 3 * width), F32), row, row), (ids,), (*qkv_chunks, gain_attn),
        name="join_qkv",
    )
    return (
        output[:, None], input_grad[:, None], grad_router[0], grad_gain_attn[0], grad_qkv, grad_out,
        grad_gain_mlp[0], grad_up, grad_down,
    )


def solution(mesh):
    placed = (
        P(None, "fsdp", "ctx", None),
        P(),
        P(),
        P("fsdp", None),
        P("fsdp", None),
        P(),
        P("fsdp", None),
        P("fsdp", None),
        P(None, "fsdp", "ctx"),
        P(),
        P(None, "fsdp", "ctx", None),
    )
    fits = mesh.shape["ctx"] == 8 and mesh.shape["fsdp"] == 4
    return jax.shard_map(
        shards_8x4 if fits else shards,
        mesh=mesh,
        in_specs=placed,
        out_specs=(
            P(None, "fsdp", "ctx", None),
            P(None, "fsdp", "ctx", None),
            P(("ctx", "fsdp")),
            P(("ctx", "fsdp")),
            P(("ctx", "fsdp"), None),
            P(("ctx", "fsdp"), None),
            P(("ctx", "fsdp")),
            P(("ctx", "fsdp"), None),
            P(("ctx", "fsdp"), None),
        ),
        check_vma=False,
    )
```
